32 devices in a mesh: stream: 8 (over z, y), span: 4 (over x, core).
Axes of the slice: x: 2, y: 2, z: 4, core: 2. Of those that a mesh axis runs over, the one named last changes fastest.
Arguments:
- flow_vector: float32 [3, 64, 32, 256], P(None, 'stream', 'span'), may hold values from -4.8 to 4.8
- mass_per_volume: float32 [64, 32, 256], P('stream', 'span'), may hold values from 0.5 to 2
- thermal_state: float32 [64, 32, 256], P('stream', 'span'), may hold values from 0.8 to 2.5
- mass_fractions: float32 [9, 64, 32, 256], P(None, 'stream', 'span'), may hold values from 0.01 to 0.3
- solid_boundary_indicator: int32 [64, 32, 256], P('stream', 'span'), may hold values 0 or 1
- fuel_inlet_indicator: int32 [64, 32, 256], P('stream', 'span'), may hold values 0 or 1
Outputs:
- flow_vector_next: float32 [3, 64, 32, 256], P(None, 'stream', 'span')
- mass_per_volume_next: float32 [64, 32, 256], P('stream', 'span')
- thermal_state_next: float32 [64, 32, 256], P('stream', 'span')
- mass_fractions_next: float32 [9, 64, 32, 256], P(None, 'stream', 'span')
- smag_coef: float32 [64, 256], P('stream')
The draws below stay inside these ranges and needn't reach their ends.
All inputs are finite; a program needn't handle non-finite values. Where the reference program divides by a largest or mean magnitude, that divisor is 1e-20 or more. No bound on the sum of `solid_boundary_indicator` or of `fuel_inlet_indicator` on one device may be relied on, other than what follows from the above.
Results may differ from the reference program's by a relative error of at most 0.00029.
Values sent between devices are 32-bit elements; how exact they have to be, the bound alone decides.
No kernel may reach another device: no remote copies, remote signals or barrier semaphores. Data moves between devices by JAX's collectives and lax.ppermute only.
A program may use at most 64 MiB of HBM per device.

```python
import math
import jax
import jax.numpy as jnp
import numpy as np
from jax import lax

CROSS_POINTS = 256
SPECIES = 9
AXIAL_POINTS = 64
LATERAL_POINTS = 32


def draw_flow_vector(key, part):
    keys = jax.random.split(jax.random.fold_in(key, 11), 1)
    place = jnp.arange(LATERAL_POINTS, dtype=jnp.float32) / LATERAL_POINTS
    ramp = (0.6 * 2.0 ** place)[None, None, :, None]
    values = jax.random.normal(keys[0], (3, AXIAL_POINTS, LATERAL_POINTS, CROSS_POINTS), jnp.float32) * ramp
    return jnp.clip(values, -4.8, 4.8)


def place_ends(values, own_key, least, high):
    spot = [jax.random.randint(jax.random.fold_in(own_key, axis), (), 0, length) for axis, length in enumerate(values.shape)]
    main_axis = values.shape.index(max(values.shape))
    beside = spot[:main_axis] + [(spot[main_axis] + 1) % values.shape[main_axis]] + spot[main_axis + 1:]
    return values.at[tuple(spot)].set(least).at[tuple(beside)].set(high)


def block_levels(rng, shape, cuts, least, largest):
    loudness, own = 1.0, jax.random.fold_in(rng, 6)
    for axis_at, parts in cuts:
        draws = jnp.exp(jax.random.uniform(jax.random.fold_in(own, axis_at), (parts,), jnp.float32, least / len(cuts), largest / len(cuts)))
        loudness = loudness * jnp.repeat(draws, shape[axis_at] // parts).reshape([-1 if axis == axis_at else 1 for axis in range(len(shape))])
    return loudness


def setup_inputs(seed: int = 0) -> dict:
    seeds = jax.random.split(jax.random.key(seed), 7)
    return {
        "flow_vector": draw_flow_vector(jax.random.fold_in(seeds[6], 71), 0),
        "mass_per_volume": jnp.clip(jnp.exp(math.log(2.0) - 1.3862944 * jax.random.uniform(seeds[1], (AXIAL_POINTS, LATERAL_POINTS, CROSS_POINTS), jnp.float32) ** block_levels(seeds[1], (AXIAL_POINTS, LATERAL_POINTS, CROSS_POINTS), ((0, 8), (1, 4)), -0.2, 0.2)), 0.5, 2.0),
        "thermal_state": jnp.clip(jnp.exp(math.log(2.5) - 1.13943427 * jax.random.uniform(seeds[2], (AXIAL_POINTS, LATERAL_POINTS, CROSS_POINTS), jnp.float32) ** block_levels(seeds[2], (AXIAL_POINTS, LATERAL_POINTS, CROSS_POINTS), ((0, 8), (1, 4)), -0.2, 0.2)), 0.8, 2.5),
        "mass_fractions": jnp.clip(jnp.exp(math.log(0.3) - 3.4011974 * jax.random.uniform(seeds[3], (SPECIES, AXIAL_POINTS, LATERAL_POINTS, CROSS_POINTS), jnp.float32) ** block_levels(seeds[3], (SPECIES, AXIAL_POINTS, LATERAL_POINTS, CROSS_POINTS), ((1, 8), (2, 4)), -0.2, 0.2)), 0.01, 0.3),
        "solid_boundary_indicator": place_ends((jax.random.randint(seeds[4], (AXIAL_POINTS, LATERAL_POINTS, CROSS_POINTS), 0, 10) < 1).astype(jnp.int32), jax.random.fold_in(seeds[4], 1), 0, 1),
        "fuel_inlet_indicator": place_ends((jax.random.randint(seeds[5], (AXIAL_POINTS, LATERAL_POINTS, CROSS_POINTS), 0, 20) < 1).astype(jnp.int32), jax.random.fold_in(seeds[5], 1), 0, 1),
    }


adiabatic_gamma = 1.4
courant = 0.5
laminar_diffusivity = 0.05
momentum_thermal_quotient = 0.7
schmidt = 0.7
subgrid_thermal_quotient = 0.9
inject_rate = 5.0
inject_speed = 2.0
heat_capacity = 3.5
tiny_value = 1e-06
reaction_list = (((4, 1), (5, 3)), ((5, 0), (4, 3)), ((0, 3), (2, 4)), ((5, 2), (3, 3)), ((0, 9), (4, 4)), ((5, 5, 9), (1,)), ((5, 4, 9), (3,)), ((4, 3, 9), (2,)), ((4, 1, 9), (6,)), ((6, 4), (0, 1)), ((6, 4), (3, 3)), ((6, 5), (1, 3)), ((6, 3), (2, 1)), ((6, 6), (7, 1)), ((7, 9), (3, 3)), ((7, 4), (2, 3)), ((7, 4), (6, 0)), ((7, 5), (3, 6)), ((7, 3), (6, 2)))
log_prefactor = np.array([3.9, 3.2, 3.4, 3.0, 2.0, 6.0, 6.2, 6.5, 5.8, 3.8, 3.6, 3.5, 3.7, 3.1, 2.2, 3.3, 3.4, 3.0, 3.2], np.float32)
thermal_power_index = np.array([0.0, 0.5, 0.5, 1.0, -1.0, -0.5, -1.0, -2.0, -1.0, 0.0, 0.0, 0.0, 0.0, 0.0, 0.0, 0.0, 0.0, 1.0, 0.0], np.float32)
arrhenius_barrier = np.array([1.6, 0.7, 0.4, 1.5, 2.0, 0.0, 0.0, 0.0, 0.0, 0.1, 0.05, 0.0, 0.0, 0.2, 1.8, 0.4, 0.8, 0.3, 0.1], np.float32)
molar_weight = np.array([0.125, 2.0, 1.125, 1.0625, 0.0625, 1.0, 2.0625, 2.125, 1.75], np.float32)
formation = np.array([0.0, 0.0, -2.42, 0.39, 2.18, 2.49, 0.12, -1.36, 0.0], np.float32)
pair_list = ((0, 0), (1, 1), (2, 2), (0, 1), (0, 2), (1, 2))

def reaction_tables():
    orders = np.zeros((19, 10), np.float32)
    net_change = np.zeros((9, 19), np.float32)
    for number, (reactants, products_list) in enumerate(reaction_list):
        for species_id in reactants:
            orders[number, species_id] += 1.0
            if species_id < 9:
                net_change[species_id, number] -= 1.0
        for species_id in products_list:
            net_change[species_id, number] += 1.0
    return (orders, net_change)

def kinetics_advance(mass_per_volume, thermal_state, mass_fractions):
    orders, net_change = reaction_tables()
    final_dimensions = (1,) * mass_per_volume.ndim
    weights = jnp.asarray(molar_weight).reshape((9,) + final_dimensions)
    concentration = mass_per_volume[None] * mass_fractions / weights
    log_terms = jnp.concatenate([jnp.log(concentration), jnp.log(lax.optimization_barrier(jnp.sum(concentration, axis=0)))[None]], axis=0)
    logarithm_progress_pace = jnp.einsum('rk,k...->r...', jnp.asarray(orders), log_terms, precision=lax.Precision.HIGHEST)
    logarithm_progress_pace = logarithm_progress_pace + jnp.asarray(log_prefactor).reshape((19,) + final_dimensions)
    logarithm_progress_pace = logarithm_progress_pace + jnp.asarray(thermal_power_index).reshape((19,) + final_dimensions) * jnp.log(thermal_state)[None]
    logarithm_progress_pace = logarithm_progress_pace - jnp.asarray(arrhenius_barrier).reshape((19,) + final_dimensions) / thermal_state[None]
    produced = jnp.einsum('kr,r...->k...', jnp.asarray(net_change), jnp.exp(logarithm_progress_pace), precision=lax.Precision.HIGHEST)
    fraction_creation = weights * produced / mass_per_volume[None]
    exothermic_output = -jnp.einsum('k,k...->...', jnp.asarray(formation), produced, precision=lax.Precision.HIGHEST) / (heat_capacity * mass_per_volume)
    return (fraction_creation, exothermic_output)

def neighbour(values, direction, offset):
    if direction == 2:
        return jnp.roll(values, -offset, axis=values.ndim - 2)
    axis_num = values.ndim - 3 if direction == 0 else values.ndim - 1
    extent = values.shape[axis_num]
    widths = [(0, 0)] * values.ndim
    widths[axis_num] = (1, 1)
    return lax.slice_in_dim(jnp.pad(values, widths), 1 + offset, 1 + offset + extent, axis=axis_num)

def derivative(values, direction):
    return 0.5 * (neighbour(values, direction, 1) - neighbour(values, direction, -1))

def second_difference_sum(values):
    summed = neighbour(values, 0, 1) + neighbour(values, 0, -1)
    summed = summed + neighbour(values, 2, 1) + neighbour(values, 2, -1)
    summed = summed + neighbour(values, 1, 1) + neighbour(values, 1, -1)
    return summed - 6.0 * values

def test_filter(values):
    row_filter = 0.25 * neighbour(values, 0, -1) + 0.5 * values + 0.25 * neighbour(values, 0, 1)
    return 0.25 * neighbour(row_filter, 2, -1) + 0.5 * row_filter + 0.25 * neighbour(row_filter, 2, 1)

def strain(flow_vector):
    gradients = [[derivative(flow_vector[first_comp], second_comp) for second_comp in range(3)] for first_comp in range(3)]
    strain_parts = [0.5 * (gradients[first_comp][second_comp] + gradients[second_comp][first_comp]) for first_comp, second_comp in pair_list]
    diagonal_sum = strain_parts[0] * strain_parts[0] + strain_parts[1] * strain_parts[1] + strain_parts[2] * strain_parts[2]
    off_sum = strain_parts[3] * strain_parts[3] + strain_parts[4] * strain_parts[4] + strain_parts[5] * strain_parts[5]
    magnitude = jnp.sqrt(2.0 * (diagonal_sum + 2.0 * off_sum))
    return (strain_parts, magnitude)

def reference(flow_vector, mass_per_volume, thermal_state, mass_fractions, solid_boundary_indicator, fuel_inlet_indicator):
    peak_signal_celerity = jnp.max(jnp.abs(flow_vector[0]) + jnp.abs(flow_vector[1]) + jnp.abs(flow_vector[2]) + jnp.sqrt(adiabatic_gamma * thermal_state))
    interval_duration = courant / peak_signal_celerity
    strain_parts, magnitude = strain(flow_vector)
    filtered = test_filter(flow_vector)
    hat_parts, hat_magnitude = strain(filtered)
    contract_lm = jnp.zeros(magnitude.shape, jnp.float32)
    contract_mm = jnp.zeros(magnitude.shape, jnp.float32)
    for number, (first_comp, second_comp) in enumerate(pair_list):
        weight = 1.0 if first_comp == second_comp else 2.0
        resolved = test_filter(flow_vector[first_comp] * flow_vector[second_comp]) - filtered[first_comp] * filtered[second_comp]
        model_term = test_filter(magnitude * strain_parts[number]) - 4.0 * hat_magnitude * hat_parts[number]
        contract_lm = contract_lm + weight * resolved * model_term
        contract_mm = contract_mm + weight * model_term * model_term
    plane_lm = lax.optimization_barrier(jnp.sum(contract_lm, axis=1)) / LATERAL_POINTS
    plane_mm = lax.optimization_barrier(jnp.sum(contract_mm, axis=1)) / LATERAL_POINTS
    closure_constant = jnp.maximum(0.5 * plane_lm / (plane_mm + tiny_value), 0.0)
    subgrid_diffusivity = closure_constant[:, None, :] * magnitude
    carried_fractions = jnp.moveaxis(mass_fractions, 1, 0)
    forcing_group_sequence, exothermic_output = lax.map(lambda grouped_arrays: kinetics_advance(grouped_arrays[0], grouped_arrays[1], grouped_arrays[2]), (mass_per_volume, thermal_state, carried_fractions))
    fraction_creation = jnp.moveaxis(forcing_group_sequence, 0, 1)
    injector = fuel_inlet_indicator.astype(jnp.float32)
    wall = solid_boundary_indicator.astype(jnp.float32)

    def transport_quantity(values):
        return flow_vector[0] * derivative(values, 0) + flow_vector[1] * derivative(values, 1) + flow_vector[2] * derivative(values, 2)
    thermodynamic_push = mass_per_volume * thermal_state
    tendencies = []
    for first_comp in range(3):
        tendency = -transport_quantity(flow_vector[first_comp]) - derivative(thermodynamic_push, first_comp) / mass_per_volume + (laminar_diffusivity + subgrid_diffusivity) * second_difference_sum(flow_vector[first_comp])
        if first_comp == 1:
            tendency = tendency + inject_rate * injector * (inject_speed - flow_vector[1])
        tendencies.append(tendency)
    flow_vector_next = (1.0 - wall)[None] * (flow_vector + interval_duration * jnp.stack(tendencies))
    flux_sum = derivative(mass_per_volume * flow_vector[0], 0) + derivative(mass_per_volume * flow_vector[1], 1) + derivative(mass_per_volume * flow_vector[2], 2)
    mass_per_volume_next = mass_per_volume - interval_duration * flux_sum
    thermal_change_pace = -transport_quantity(thermal_state) + (laminar_diffusivity / momentum_thermal_quotient + subgrid_diffusivity / subgrid_thermal_quotient) * second_difference_sum(thermal_state) + exothermic_output
    thermal_state_next = thermal_state + interval_duration * thermal_change_pace
    spec_tend = -transport_quantity(mass_fractions) + (laminar_diffusivity / schmidt + subgrid_diffusivity / subgrid_thermal_quotient)[None] * second_difference_sum(mass_fractions) + fraction_creation
    spec_tend = spec_tend.at[0].add(inject_rate * injector * (1.0 - mass_fractions[0]))
    mass_fractions_next = mass_fractions + interval_duration * spec_tend
    return (flow_vector_next, mass_per_volume_next, thermal_state_next, mass_fractions_next, closure_constant)
```

```python
import functools

import jax
import jax.numpy as jnp
import numpy as np
from jax import lax
from jax.experimental import pallas as pl
from jax.experimental.pallas import tpu as pltpu
from jax.sharding import PartitionSpec as P

SPECIES = 9
adiabatic_gamma = 1.4
courant = 0.5
laminar_diffusivity = 0.05
momentum_thermal_quotient = 0.7
schmidt = 0.7
subgrid_thermal_quotient = 0.9
inject_rate = 5.0
inject_speed = 2.0
heat_capacity = 3.5
tiny_value = 1e-06
reaction_list = (
    ((4, 1), (5, 3)),
    ((5, 0), (4, 3)),
    ((0, 3), (2, 4)),
    ((5, 2), (3, 3)),
    ((0, 9), (4, 4)),
    ((5, 5, 9), (1,)),
    ((5, 4, 9), (3,)),
    ((4, 3, 9), (2,)),
    ((4, 1, 9), (6,)),
    ((6, 4), (0, 1)),
    ((6, 4), (3, 3)),
    ((6, 5), (1, 3)),
    ((6, 3), (2, 1)),
    ((6, 6), (7, 1)),
    ((7, 9), (3, 3)),
    ((7, 4), (2, 3)),
    ((7, 4), (6, 0)),
    ((7, 5), (3, 6)),
    ((7, 3), (6, 2)),
)
log_prefactor = np.array(
    [3.9, 3.2, 3.4, 3.0, 2.0, 6.0, 6.2, 6.5, 5.8, 3.8, 3.6, 3.5, 3.7, 3.1, 2.2, 3.3, 3.4, 3.0, 3.2],
    np.float32,
)
thermal_power_index = np.array(
    [
        0.0,
        0.5,
        0.5,
        1.0,
        -1.0,
        -0.5,
        -1.0,
        -2.0,
        -1.0,
        0.0,
        0.0,
        0.0,
        0.0,
        0.0,
        0.0,
        0.0,
        0.0,
        1.0,
        0.0,
    ],
    np.float32,
)
arrhenius_barrier = np.array(
    [
        1.6,
        0.7,
        0.4,
        1.5,
        2.0,
        0.0,
        0.0,
        0.0,
        0.0,
        0.1,
        0.05,
        0.0,
        0.0,
        0.2,
        1.8,
        0.4,
        0.8,
        0.3,
        0.1,
    ],
    np.float32,
)
molar_weight = np.array([0.125, 2.0, 1.125, 1.0625, 0.0625, 1.0, 2.0625, 2.125, 1.75], np.float32)
formation = np.array([0.0, 0.0, -2.42, 0.39, 2.18, 2.49, 0.12, -1.36, 0.0], np.float32)
pair_list = ((0, 0), (1, 1), (2, 2), (0, 1), (0, 2), (1, 2))


VMEM = pltpu.VMEM


def pair_up(count, start, wrap):
    pairs = []
    for low in range(start, count - 1, 2):
        pairs += [(low, low + 1), (low + 1, low)]
    if wrap and start == 1:
        pairs += [(count - 1, 0), (0, count - 1)]
    return pairs


def flip(count, bit):
    return [(index, index ^ bit) for index in range(count)]


def even_index(axis):
    return lax.rem(lax.axis_index(axis), 2) == 0


def call(body, outs, args, scratch=(), flops=0, name=None):
    nbytes = sum(int(np.prod(a.shape)) * 4 for a in args) + sum(
        int(np.prod(s)) * 4 for s in outs
    )
    return pl.pallas_call(
        body,
        out_shape=[jax.ShapeDtypeStruct(s, jnp.float32) for s in outs],
        in_specs=[pl.BlockSpec(memory_space=VMEM)] * len(args),
        out_specs=[pl.BlockSpec(memory_space=VMEM)] * len(outs),
        scratch_shapes=list(scratch),
        cost_estimate=pl.CostEstimate(flops=flops, bytes_accessed=nbytes, transcendentals=0),
        name=name,
    )(*args)


def pack_stream(vel, temp, send_a, send_b):
    even = even_index("stream")
    nx = vel.shape[1]
    for comp in range(3):
        for layer in range(2):
            low = vel[comp, layer]
            high = vel[comp, nx - 2 + layer]
            send_a[2 * comp + layer] = jnp.where(even, high, low)
            send_b[2 * comp + layer] = jnp.where(even, low, high)
    fastest = None
    for x in range(nx):
        speed = (
            jnp.abs(vel[0, x])
            + jnp.abs(vel[1, x])
            + jnp.abs(vel[2, x])
            + jnp.sqrt(adiabatic_gamma * temp[x])
        )
        fastest = speed if fastest is None else jnp.maximum(fastest, speed)
    send_a[6] = fastest


def pack_span(vel, got_a, got_b, send_c, send_d):
    even_s = even_index("stream")
    even_p = even_index("span")
    nx, nz = vel.shape[1], vel.shape[2]
    for comp in range(3):
        for x in range(nx + 4):
            if x < 2:
                tile = jnp.where(even_s, got_b[2 * comp + x], got_a[2 * comp + x])
            elif x < nx + 2:
                tile = vel[comp, x - 2]
            else:
                at = 2 * comp + x - nx - 2
                tile = jnp.where(even_s, got_a[at], got_b[at])
            first, last = tile[0:2], tile[nz - 2 : nz]
            row = 2 * (comp * (nx + 4) + x)
            send_c[row : row + 2] = jnp.where(even_p, last, first)
            send_d[row : row + 2] = jnp.where(even_p, first, last)


def pack_scalars(dens, temp, spec, send_a, send_b, send_c, send_d):
    even_s = even_index("stream")
    even_p = even_index("span")
    nx, nz = dens.shape[0], dens.shape[1]
    for field in range(2 + SPECIES):
        ref = dens if field == 0 else temp if field == 1 else spec.at[field - 2]
        low, high = ref[0], ref[nx - 1]
        send_a[field] = jnp.where(even_s, high, low)
        send_b[field] = jnp.where(even_s, low, high)
        first, last = ref[:, 0, :], ref[:, nz - 1, :]
        send_c[field * nx : (field + 1) * nx] = jnp.where(even_p, last, first)
        send_d[field * nx : (field + 1) * nx] = jnp.where(even_p, first, last)


def along_y(tile, lane):
    width = tile.shape[-1]
    after = jnp.where(lane == width - 1, 0.0, pltpu.roll(tile, width - 1, 1))
    before = jnp.where(lane == 0, 0.0, pltpu.roll(tile, 1, 1))
    return after, before


def strain_of(grads):
    parts = [
        grads[i][i] if i == j else 0.5 * (grads[i][j] + grads[j][i]) for i, j in pair_list
    ]
    diagonal = parts[0] * parts[0] + parts[1] * parts[1] + parts[2] * parts[2]
    off = parts[3] * parts[3] + parts[4] * parts[4] + parts[5] * parts[5]
    return parts, jnp.sqrt(2.0 * (diagonal + 2.0 * off))


def germano(vel, got_a, got_b, got_c, got_d, top, red, mag, wide, shear, smooth):
    even_s = even_index("stream")
    even_p = even_index("span")
    nx, nz, ny = vel.shape[1], vel.shape[2], vel.shape[3]
    rows = 2 * nz
    zero = jnp.zeros((nz - 4, ny), jnp.float32)
    for comp in range(3):
        for x in range(nx + 4):
            if x < 2:
                tile = jnp.where(even_s, got_b[2 * comp + x], got_a[2 * comp + x])
            elif x < nx + 2:
                tile = vel[comp, x - 2]
            else:
                at = 2 * comp + x - nx - 2
                tile = jnp.where(even_s, got_a[at], got_b[at])
            row = 2 * (comp * (nx + 4) + x)
            one, two = got_c[row : row + 2], got_d[row : row + 2]
            wide[comp, x, 0:nz] = tile
            wide[comp, x, nz : nz + 2] = jnp.where(even_p, one, two)
            wide[comp, x, nz + 2 : rows - 2] = zero
            wide[comp, x, rows - 2 : rows] = jnp.where(even_p, two, one)
    lane = lax.broadcasted_iota(jnp.int32, (rows, ny), 1)

    def z_after(tile):
        return pltpu.roll(tile, rows - 1, 0)

    def z_before(tile):
        return pltpu.roll(tile, 1, 0)

    def gradients(ref, x, i):
        center = ref[i, x]
        after, before = along_y(center, lane)
        return [
            0.5 * (ref[i, x + 1] - ref[i, x - 1]),
            0.5 * (after - before),
            0.5 * (z_after(center) - z_before(center)),
        ]

    def z_filter(tile):
        return 0.25 * (z_after(tile) + z_before(tile)) + 0.5 * tile

    def x_filter(take):
        return 0.25 * (take(-1) + take(1)) + 0.5 * take(0)

    position = lax.axis_index("stream") * nx
    total = lax.axis_size("stream") * nx

    for x in range(nx + 2):
        keep = None
        if x == 0:
            keep = jnp.where(position > 0, 1.0, 0.0)
        elif x == nx + 1:
            keep = jnp.where(position + nx < total, 1.0, 0.0)
        parts, size = strain_of([gradients(wide, x + 1, i) for i in range(3)])
        if 1 <= x <= nx:
            mag[x - 1] = size[0:nz]
        if keep is not None:
            size = size * keep
        for k in range(6):
            shear[k, x] = size * parts[k]
        for i in range(3):
            value = z_filter(x_filter(lambda d: wide[i, x + 1 + d]))
            smooth[i, x] = value if keep is None else value * keep
    for x in range(nx):
        hat_parts, hat_size = strain_of([gradients(smooth, x + 1, i) for i in range(3)])
        lm = jnp.zeros((rows, ny), jnp.float32)
        mm = jnp.zeros((rows, ny), jnp.float32)
        for k, (i, j) in enumerate(pair_list):
            weight = 1.0 if i == j else 2.0
            product = z_filter(x_filter(lambda d: wide[i, x + 2 + d] * wide[j, x + 2 + d]))
            resolved = product - smooth[i, x + 1] * smooth[j, x + 1]
            model = z_filter(x_filter(lambda d: shear[k, x + 1 + d])) - 4.0 * hat_size * hat_parts[k]
            lm = lm + weight * resolved * model
            mm = mm + weight * model * model
        red[x : x + 1] = jnp.sum(lm[0:nz], axis=0, keepdims=True)
        red[nx + x : nx + x + 1] = jnp.sum(mm[0:nz], axis=0, keepdims=True)
    red[2 * nx : 2 * nx + nz] = top[...]


def chemistry(dens, inverse, temp, species):
    over = 1.0 / temp
    root = jnp.sqrt(temp)
    powers = {0.0: None, 0.5: root, 1.0: temp, -1.0: over, -0.5: root * over, -2.0: over * over}
    e05 = jnp.exp(-0.05 * over)
    e15 = jnp.exp(-1.5 * over)
    decay = {0: None, 5: e05, 150: e15}
    decay[10] = e05 * e05
    decay[20] = decay[10] * decay[10]
    decay[30] = decay[20] * decay[10]
    decay[40] = decay[20] * decay[20]
    decay[70] = decay[40] * decay[30]
    decay[80] = decay[40] * decay[40]
    decay[160] = e15 * decay[10]
    decay[180] = e15 * decay[30]
    decay[200] = decay[180] * decay[20]
    conc = [dens * (species[k] * float(1.0 / molar_weight[k])) for k in range(SPECIES)]
    total = conc[0]
    for k in range(1, SPECIES):
        total = total + conc[k]
    conc.append(total)
    products = {}

    def product(ids):
        if len(ids) == 1:
            return conc[ids[0]]
        if ids not in products:
            products[ids] = product(ids[:-1]) * conc[ids[-1]]
        return products[ids]

    produced = [None] * SPECIES
    for number, (reactants, results) in enumerate(reaction_list):
        ordered = tuple(sorted(reactants))
        pace = product(ordered) * float(np.exp(np.float64(log_prefactor[number])))
        power = powers[float(thermal_power_index[number])]
        if power is not None:
            pace = pace * power
        fall = decay[int(round(float(arrhenius_barrier[number]) * 100))]
        if fall is not None:
            pace = pace * fall
        change = {}
        for k in reactants:
            if k < SPECIES:
                change[k] = change.get(k, 0) - 1
        for k in results:
            change[k] = change.get(k, 0) + 1
        for k, times in change.items():
            if times == 0:
                continue
            term = pace if abs(times) == 1 else pace * float(abs(times))
            if produced[k] is None:
                produced[k] = term if times > 0 else -term
            else:
                produced[k] = produced[k] + term if times > 0 else produced[k] - term
    heat = None
    for k in range(SPECIES):
        if formation[k] != 0.0 and produced[k] is not None:
            term = produced[k] * float(-formation[k] / heat_capacity)
            heat = term if heat is None else heat + term
    source = [
        None if produced[k] is None else produced[k] * inverse * float(molar_weight[k])
        for k in range(SPECIES)
    ]
    return source, heat * inverse


def tendencies(
    vel, dens, temp, spec, fuel, vel_a, vel_b, vel_c, vel_d, got_a, got_b, got_c, got_d, mag, base, slope
):
    even_s = even_index("stream")
    even_p = even_index("span")
    nx, nz, ny = dens.shape
    lane = lax.broadcasted_iota(jnp.int32, (nz, ny), 1)
    line = lax.broadcasted_iota(jnp.int32, (nz, ny), 0)

    def own(field, x):
        if field < 3:
            return vel[field, x]
        if field == 3:
            return dens[x]
        if field == 4:
            return temp[x]
        return spec[field - 5, x]

    def cell(field, x):
        if 0 <= x < nx:
            return own(field, x)
        if field < 3:
            at = 2 * field + (1 if x < 0 else 0)
            one, two = vel_a[at], vel_b[at]
        else:
            one, two = got_a[field - 3], got_b[field - 3]
        return jnp.where(even_s, two, one) if x < 0 else jnp.where(even_s, one, two)

    def edges(field, x):
        if field < 3:
            row = 2 * (field * (nx + 4) + x + 2)
            c0, c1 = vel_c[row : row + 1], vel_c[row + 1 : row + 2]
            d0, d1 = vel_d[row : row + 1], vel_d[row + 1 : row + 2]
            return jnp.where(even_p, c0, d0), jnp.where(even_p, d1, c1)
        row = (field - 3) * nx + x
        c0, d0 = got_c[row : row + 1], got_d[row : row + 1]
        return jnp.where(even_p, c0, d0), jnp.where(even_p, d0, c0)

    def neighbours(field, x):
        center = own(field, x)
        after, before = along_y(center, lane)
        high, low = edges(field, x)
        up = jnp.where(line == nz - 1, high, pltpu.roll(center, nz - 1, 0))
        down = jnp.where(line == 0, low, pltpu.roll(center, 1, 0))
        return center, cell(field, x + 1), cell(field, x - 1), after, before, up, down

    for x in range(nx):
        v = [neighbours(i, x) for i in range(3)]
        r = neighbours(3, x)
        t = neighbours(4, x)
        half = [0.5 * v[i][0] for i in range(3)]
        inverse = 1.0 / r[0]
        size = mag[x]
        inject = fuel[x].astype(jnp.float32) * inject_rate
        species = [own(5 + k, x) for k in range(SPECIES)]
        source, release = chemistry(r[0], inverse, t[0], species)

        def advect(n):
            return half[0] * (n[1] - n[2]) + half[1] * (n[3] - n[4]) + half[2] * (n[5] - n[6])

        def laplace(n):
            return ((n[1] + n[2]) + (n[3] + n[4])) + ((n[5] + n[6]) - 6.0 * n[0])

        push = [r[m] * t[m] for m in range(1, 7)]
        scale = 0.5 * inverse
        for i in range(3):
            lap = laplace(v[i])
            value = laminar_diffusivity * lap - advect(v[i]) - (push[2 * i] - push[2 * i + 1]) * scale
            if i == 1:
                value = value + inject * (inject_speed - v[1][0])
            base[i, x] = value
            slope[i, x] = size * lap
        flux = (
            (r[1] * v[0][1] - r[2] * v[0][2])
            + (r[3] * v[1][3] - r[4] * v[1][4])
            + (r[5] * v[2][5] - r[6] * v[2][6])
        )
        base[3, x] = -0.5 * flux
        thin = size * (1.0 / subgrid_thermal_quotient)
        lap = laplace(t)
        base[4, x] = (laminar_diffusivity / momentum_thermal_quotient) * lap - advect(t) + release
        slope[3, x] = thin * lap
        for k in range(SPECIES):
            n = neighbours(5 + k, x)
            lap = laplace(n)
            value = (laminar_diffusivity / schmidt) * lap - advect(n)
            if source[k] is not None:
                value = value + source[k]
            if k == 0:
                value = value + inject * (1.0 - n[0])
            base[5 + k, x] = value
            slope[4 + k, x] = thin * lap


def finish(
    total_z, vel, dens, temp, spec, wall, base, slope, r0, r1, r2, r3, out_v, out_r, out_t, out_y, out_c
):
    nx = dens.shape[0]
    lm = (r0[0:nx] + r1[0:nx]) + (r2[0:nx] + r3[0:nx])
    mm = (r0[nx : 2 * nx] + r1[nx : 2 * nx]) + (r2[nx : 2 * nx] + r3[nx : 2 * nx])
    coef = jnp.maximum(0.5 * (lm / total_z) / (mm / total_z + tiny_value), 0.0)
    out_c[...] = coef
    top = jnp.maximum(
        jnp.maximum(r0[2 * nx :], r1[2 * nx :]), jnp.maximum(r2[2 * nx :], r3[2 * nx :])
    )
    step = courant / jnp.max(jnp.max(top, axis=0, keepdims=True), axis=1, keepdims=True)
    gain = coef * step
    for x in range(nx):
        g = gain[x : x + 1]
        open_cell = 1.0 - wall[x].astype(jnp.float32)
        for i in range(3):
            out_v[i, x] = open_cell * (vel[i, x] + step * base[i, x] + g * slope[i, x])
        out_r[x] = dens[x] + step * base[3, x]
        out_t[x] = temp[x] + step * base[4, x] + g * slope[3, x]
        for k in range(SPECIES):
            out_y[k, x] = spec[k, x] + step * base[5 + k, x] + g * slope[4 + k, x]


def per_device(vel, dens, temp, spec, wall, fuel):
    nx, nz, ny = dens.shape
    n_stream = lax.axis_size("stream")
    n_span = lax.axis_size("span")
    send_a, send_b = call(
        pack_stream, [(7, nz, ny), (6, nz, ny)], (vel, temp), name="pack_stream"
    )
    got_b = lax.ppermute(send_b, "stream", pair_up(n_stream, 1, False))
    got_a = lax.ppermute(send_a, "stream", pair_up(n_stream, 0, False))
    faces = call(
        pack_scalars,
        [(2 + SPECIES, nz, ny)] * 2 + [((2 + SPECIES) * nx, ny)] * 2,
        (dens, temp, spec),
        name="pack_scalars",
    )
    rows = 6 * (nx + 4)
    send_c, send_d = call(
        pack_span, [(rows, ny)] * 2, (vel, got_a, got_b), name="pack_span"
    )
    got_c = lax.ppermute(send_c, "span", pair_up(n_span, 0, True))
    got_d = lax.ppermute(send_d, "span", pair_up(n_span, 1, True))
    far_b = lax.ppermute(faces[1], "stream", pair_up(n_stream, 1, False))
    far_a = lax.ppermute(faces[0], "stream", pair_up(n_stream, 0, False))
    far_c = lax.ppermute(faces[2], "span", pair_up(n_span, 0, True))
    far_d = lax.ppermute(faces[3], "span", pair_up(n_span, 1, True))
    top = jnp.maximum(send_a[6], got_a[6])
    bit = 2
    while bit < n_stream:
        top = jnp.maximum(top, lax.ppermute(top, "stream", flip(n_stream, bit)))
        bit *= 2
    red, mag = call(
        germano,
        [(2 * nx + nz, ny), (nx, nz, ny)],
        (vel, got_a, got_b, got_c, got_d, top),
        scratch=[
            VMEM((3, nx + 4, 2 * nz, ny), jnp.float32),
            VMEM((6, nx + 2, 2 * nz, ny), jnp.float32),
            VMEM((3, nx + 2, 2 * nz, ny), jnp.float32),
        ],
        name="germano",
    )
    base, slope = call(
        tendencies,
        [(5 + SPECIES, nx, nz, ny), (4 + SPECIES, nx, nz, ny)],
        (vel, dens, temp, spec, fuel, got_a, got_b, got_c, got_d, far_a, far_b, far_c, far_d, mag),
        name="tendencies",
    )
    bit = 1
    while bit * 4 < n_span:
        others = [lax.ppermute(red, "span", flip(n_span, bit * m)) for m in (1, 2, 3)]
        low = (red[: 2 * nx] + others[0][: 2 * nx]) + (others[1][: 2 * nx] + others[2][: 2 * nx])
        high = jnp.maximum(
            jnp.maximum(red[2 * nx :], others[0][2 * nx :]),
            jnp.maximum(others[1][2 * nx :], others[2][2 * nx :]),
        )
        red = jnp.concatenate([low, high], axis=0)
        bit *= 4
    others = [lax.ppermute(red, "span", flip(n_span, bit * m)) for m in (3, 2, 1)]
    return tuple(
        call(
            functools.partial(finish, float(nz * n_span)),
            [vel.shape, dens.shape, dens.shape, spec.shape, (nx, ny)],
            (vel, dens, temp, spec, wall, base, slope, red, *others),
            name="finish",
        )
    )


def solution(mesh):
    return jax.shard_map(
        per_device,
        mesh=mesh,
        in_specs=(
            P(None, "stream", "span", None),
            P("stream", "span", None),
            P("stream", "span", None),
            P(None, "stream", "span", None),
            P("stream", "span", None),
            P("stream", "span", None),
        ),
        out_specs=(
            P(None, "stream", "span", None),
            P("stream", "span", None),
            P("stream", "span", None),
            P(None, "stream", "span", None),
            P("stream", None),
        ),
        check_vma=False,
    )
```

```python
import functools

import jax
import jax.numpy as jnp
import numpy as np
from jax import lax
from jax.experimental import pallas as pl
from jax.experimental.pallas import tpu as pltpu
from jax.sharding import PartitionSpec as P

SPECIES = 9
adiabatic_gamma = 1.4
courant = 0.5
laminar_diffusivity = 0.05
momentum_thermal_quotient = 0.7
schmidt = 0.7
subgrid_thermal_quotient = 0.9
inject_rate = 5.0
inject_speed = 2.0
heat_capacity = 3.5
tiny_value = 1e-06
reaction_list = (
    ((4, 1), (5, 3)),
    ((5, 0), (4, 3)),
    ((0, 3), (2, 4)),
    ((5, 2), (3, 3)),
    ((0, 9), (4, 4)),
    ((5, 5, 9), (1,)),
    ((5, 4, 9), (3,)),
    ((4, 3, 9), (2,)),
    ((4, 1, 9), (6,)),
    ((6, 4), (0, 1)),
    ((6, 4), (3, 3)),
    ((6, 5), (1, 3)),
    ((6, 3), (2, 1)),
    ((6, 6), (7, 1)),
    ((7, 9), (3, 3)),
    ((7, 4), (2, 3)),
    ((7, 4), (6, 0)),
    ((7, 5), (3, 6)),
    ((7, 3), (6, 2)),
)
log_prefactor = np.array(
    [3.9, 3.2, 3.4, 3.0, 2.0, 6.0, 6.2, 6.5, 5.8, 3.8, 3.6, 3.5, 3.7, 3.1, 2.2, 3.3, 3.4, 3.0, 3.2],
    np.float32,
)
thermal_power_index = np.array(
    [
        0.0,
        0.5,
        0.5,
        1.0,
        -1.0,
        -0.5,
        -1.0,
        -2.0,
        -1.0,
        0.0,
        0.0,
        0.0,
        0.0,
        0.0,
        0.0,
        0.0,
        0.0,
        1.0,
        0.0,
    ],
    np.float32,
)
arrhenius_barrier = np.array(
    [
        1.6,
        0.7,
        0.4,
        1.5,
        2.0,
        0.0,
        0.0,
        0.0,
        0.0,
        0.1,
        0.05,
        0.0,
        0.0,
        0.2,
        1.8,
        0.4,
        0.8,
        0.3,
        0.1,
    ],
    np.float32,
)
molar_weight = np.array([0.125, 2.0, 1.125, 1.0625, 0.0625, 1.0, 2.0625, 2.125, 1.75], np.float32)
formation = np.array([0.0, 0.0, -2.42, 0.39, 2.18, 2.49, 0.12, -1.36, 0.0], np.float32)
pair_list = ((0, 0), (1, 1), (2, 2), (0, 1), (0, 2), (1, 2))


VMEM = pltpu.VMEM


def pair_up(count, start, wrap):
    pairs = []
    for low in range(start, count - 1, 2):
        pairs += [(low, low + 1), (low + 1, low)]
    if wrap and start == 1:
        pairs += [(count - 1, 0), (0, count - 1)]
    return pairs


def flip(count, bit):
    return [(index, index ^ bit) for index in range(count)]


def even_index(axis):
    return lax.rem(lax.axis_index(axis), 2) == 0


def call(body, outs, args, scratch=(), flops=0, name=None, to_hbm=False):
    nbytes = sum(int(np.prod(a.shape)) * 4 for a in args) + sum(
        int(np.prod(s)) * 4 for s in outs
    )
    return pl.pallas_call(
        body,
        out_shape=[
            jax.ShapeDtypeStruct(s, jnp.float32) if to_hbm else VMEM(s, jnp.float32) for s in outs
        ],
        in_specs=[pl.BlockSpec(memory_space=VMEM)] * len(args),
        out_specs=[pl.BlockSpec(memory_space=VMEM)] * len(outs),
        scratch_shapes=list(scratch),
        compiler_params=pltpu.CompilerParams(vmem_limit_bytes=8 << 20),
        cost_estimate=pl.CostEstimate(flops=flops, bytes_accessed=nbytes, transcendentals=0),
        name=name,
    )(*[pltpu.with_memory_space_constraint(a, VMEM) for a in args])


def pack_stream(vel, temp, send_a, send_b):
    even = even_index("stream")
    nx = vel.shape[1]
    for comp in range(3):
        for layer in range(2):
            low = vel[comp, layer]
            high = vel[comp, nx - 2 + layer]
            send_a[2 * comp + layer] = jnp.where(even, high, low)
            send_b[2 * comp + layer] = jnp.where(even, low, high)
    fastest = None
    for x in range(nx):
        speed = (
            jnp.abs(vel[0, x])
            + jnp.abs(vel[1, x])
            + jnp.abs(vel[2, x])
            + jnp.sqrt(adiabatic_gamma * temp[x])
        )
        fastest = speed if fastest is None else jnp.maximum(fastest, speed)
    send_a[6] = fastest


def pack_span(vel, got_a, got_b, send_c, send_d):
    even_s = even_index("stream")
    even_p = even_index("span")
    nx, nz = vel.shape[1], vel.shape[2]
    for comp in range(3):
        for x in range(nx + 4):
            if x < 2:
                tile = jnp.where(even_s, got_b[2 * comp + x], got_a[2 * comp + x])
            elif x < nx + 2:
                tile = vel[comp, x - 2]
            else:
                at = 2 * comp + x - nx - 2
                tile = jnp.where(even_s, got_a[at], got_b[at])
            first, last = tile[0:2], tile[nz - 2 : nz]
            row = 2 * (comp * (nx + 4) + x)
            send_c[row : row + 2] = jnp.where(even_p, last, first)
            send_d[row : row + 2] = jnp.where(even_p, first, last)


def pack_scalars(dens, temp, spec, send_a, send_b, send_c, send_d):
    even_s = even_index("stream")
    even_p = even_index("span")
    nx, nz = dens.shape[0], dens.shape[1]
    for field in range(2 + SPECIES):
        ref = dens if field == 0 else temp if field == 1 else spec.at[field - 2]
        low, high = ref[0], ref[nx - 1]
        send_a[field] = jnp.where(even_s, high, low)
        send_b[field] = jnp.where(even_s, low, high)
        first, last = ref[:, 0, :], ref[:, nz - 1, :]
        send_c[field * nx : (field + 1) * nx] = jnp.where(even_p, last, first)
        send_d[field * nx : (field + 1) * nx] = jnp.where(even_p, first, last)


def along_y(tile, lane):
    width = tile.shape[-1]
    after = jnp.where(lane == width - 1, 0.0, pltpu.roll(tile, width - 1, 1))
    before = jnp.where(lane == 0, 0.0, pltpu.roll(tile, 1, 1))
    return after, before


def strain_of(grads):
    parts = [
        grads[i][i] if i == j else 0.5 * (grads[i][j] + grads[j][i]) for i, j in pair_list
    ]
    diagonal = parts[0] * parts[0] + parts[1] * parts[1] + parts[2] * parts[2]
    off = parts[3] * parts[3] + parts[4] * parts[4] + parts[5] * parts[5]
    return parts, jnp.sqrt(2.0 * (diagonal + 2.0 * off))


def germano(vel, got_a, got_b, got_c, got_d, top, red, mag, wide, shear, smooth):
    even_s = even_index("stream")
    even_p = even_index("span")
    nx, nz, ny = vel.shape[1], vel.shape[2], vel.shape[3]
    rows = 2 * nz
    zero = jnp.zeros((nz - 4, ny), jnp.float32)
    for comp in range(3):
        for x in range(nx + 4):
            if x < 2:
                tile = jnp.where(even_s, got_b[2 * comp + x], got_a[2 * comp + x])
            elif x < nx + 2:
                tile = vel[comp, x - 2]
            else:
                at = 2 * comp + x - nx - 2
                tile = jnp.where(even_s, got_a[at], got_b[at])
            row = 2 * (comp * (nx + 4) + x)
            one, two = got_c[row : row + 2], got_d[row : row + 2]
            wide[comp, x, 0:nz] = tile
            wide[comp, x, nz : nz + 2] = jnp.where(even_p, one, two)
            wide[comp, x, nz + 2 : rows - 2] = zero
            wide[comp, x, rows - 2 : rows] = jnp.where(even_p, two, one)
    lane = lax.broadcasted_iota(jnp.int32, (rows, ny), 1)

    def z_after(tile):
        return pltpu.roll(tile, rows - 1, 0)

    def z_before(tile):
        return pltpu.roll(tile, 1, 0)

    def gradients(ref, x, i):
        center = ref[i, x]
        after, before = along_y(center, lane)
        return [
            0.5 * (ref[i, x + 1] - ref[i, x - 1]),
            0.5 * (after - before),
            0.5 * (z_after(center) - z_before(center)),
        ]

    def z_filter(tile):
        return 0.25 * (z_after(tile) + z_before(tile)) + 0.5 * tile

    def x_filter(take):
        return 0.25 * (take(-1) + take(1)) + 0.5 * take(0)

    position = lax.axis_index("stream") * nx
    total = lax.axis_size("stream") * nx

    for x in range(nx + 2):
        keep = None
        if x == 0:
            keep = jnp.where(position > 0, 1.0, 0.0)
        elif x == nx + 1:
            keep = jnp.where(position + nx < total, 1.0, 0.0)
        parts, size = strain_of([gradients(wide, x + 1, i) for i in range(3)])
        if 1 <= x <= nx:
            mag[x - 1] = size[0:nz]
        if keep is not None:
            size = size * keep
        for k in range(6):
            shear[k, x] = size * parts[k]
        for i in range(3):
            value = z_filter(x_filter(lambda d: wide[i, x + 1 + d]))
            smooth[i, x] = value if keep is None else value * keep
    for x in range(nx):
        hat_parts, hat_size = strain_of([gradients(smooth, x + 1, i) for i in range(3)])
        lm = jnp.zeros((rows, ny), jnp.float32)
        mm = jnp.zeros((rows, ny), jnp.float32)
        for k, (i, j) in enumerate(pair_list):
            weight = 1.0 if i == j else 2.0
            product = z_filter(x_filter(lambda d: wide[i, x + 2 + d] * wide[j, x + 2 + d]))
            resolved = product - smooth[i, x + 1] * smooth[j, x + 1]
            model = z_filter(x_filter(lambda d: shear[k, x + 1 + d])) - 4.0 * hat_size * hat_parts[k]
            lm = lm + weight * resolved * model
            mm = mm + weight * model * model
        red[x : x + 1] = jnp.sum(lm[0:nz], axis=0, keepdims=True)
        red[nx + x : nx + x + 1] = jnp.sum(mm[0:nz], axis=0, keepdims=True)
    red[2 * nx : 2 * nx + nz] = top[...]


def chemistry(dens, inverse, temp, species):
    over = 1.0 / temp
    root = jnp.sqrt(temp)
    powers = {0.0: None, 0.5: root, 1.0: temp, -1.0: over, -0.5: root * over, -2.0: over * over}
    e05 = jnp.exp(-0.05 * over)
    e15 = jnp.exp(-1.5 * over)
    decay = {0: None, 5: e05, 150: e15}
    decay[10] = e05 * e05
    decay[20] = decay[10] * decay[10]
    decay[30] = decay[20] * decay[10]
    decay[40] = decay[20] * decay[20]
    decay[70] = decay[40] * decay[30]
    decay[80] = decay[40] * decay[40]
    decay[160] = e15 * decay[10]
    decay[180] = e15 * decay[30]
    decay[200] = decay[180] * decay[20]
    conc = [dens * (species[k] * float(1.0 / molar_weight[k])) for k in range(SPECIES)]
    total = conc[0]
    for k in range(1, SPECIES):
        total = total + conc[k]
    conc.append(total)
    products = {}

    def product(ids):
        if len(ids) == 1:
            return conc[ids[0]]
        if ids not in products:
            products[ids] = product(ids[:-1]) * conc[ids[-1]]
        return products[ids]

    produced = [None] * SPECIES
    for number, (reactants, results) in enumerate(reaction_list):
        ordered = tuple(sorted(reactants))
        pace = product(ordered) * float(np.exp(np.float64(log_prefactor[number])))
        power = powers[float(thermal_power_index[number])]
        if power is not None:
            pace = pace * power
        fall = decay[int(round(float(arrhenius_barrier[number]) * 100))]
        if fall is not None:
            pace = pace * fall
        change = {}
        for k in reactants:
            if k < SPECIES:
                change[k] = change.get(k, 0) - 1
        for k in results:
            change[k] = change.get(k, 0) + 1
        for k, times in change.items():
            if times == 0:
                continue
            term = pace if abs(times) == 1 else pace * float(abs(times))
            if produced[k] is None:
                produced[k] = term if times > 0 else -term
            else:
                produced[k] = produced[k] + term if times > 0 else produced[k] - term
    heat = None
    for k in range(SPECIES):
        if formation[k] != 0.0 and produced[k] is not None:
            term = produced[k] * float(-formation[k] / heat_capacity)
            heat = term if heat is None else heat + term
    source = [
        None if produced[k] is None else produced[k] * inverse * float(molar_weight[k])
        for k in range(SPECIES)
    ]
    return source, heat * inverse


def tendencies(
    vel, dens, temp, spec, fuel, vel_a, vel_b, vel_c, vel_d, got_a, got_b, got_c, got_d, mag, base, slope
):
    even_s = even_index("stream")
    even_p = even_index("span")
    nx, nz, ny = dens.shape
    lane = lax.broadcasted_iota(jnp.int32, (nz, ny), 1)
    line = lax.broadcasted_iota(jnp.int32, (nz, ny), 0)

    def own(field, x):
        if field < 3:
            return vel[field, x]
        if field == 3:
            return dens[x]
        if field == 4:
            return temp[x]
        return spec[field - 5, x]

    def cell(field, x):
        if 0 <= x < nx:
            return own(field, x)
        if field < 3:
            at = 2 * field + (1 if x < 0 else 0)
            one, two = vel_a[at], vel_b[at]
        else:
            one, two = got_a[field - 3], got_b[field - 3]
        return jnp.where(even_s, two, one) if x < 0 else jnp.where(even_s, one, two)

    def edges(field, x):
        if field < 3:
            row = 2 * (field * (nx + 4) + x + 2)
            c0, c1 = vel_c[row : row + 1], vel_c[row + 1 : row + 2]
            d0, d1 = vel_d[row : row + 1], vel_d[row + 1 : row + 2]
            return jnp.where(even_p, c0, d0), jnp.where(even_p, d1, c1)
        row = (field - 3) * nx + x
        c0, d0 = got_c[row : row + 1], got_d[row : row + 1]
        return jnp.where(even_p, c0, d0), jnp.where(even_p, d0, c0)

    def neighbours(field, x):
        center = own(field, x)
        after, before = along_y(center, lane)
        high, low = edges(field, x)
        up = jnp.where(line == nz - 1, high, pltpu.roll(center, nz - 1, 0))
        down = jnp.where(line == 0, low, pltpu.roll(center, 1, 0))
        return center, cell(field, x + 1), cell(field, x - 1), after, before, up, down

    for x in range(nx):
        v = [neighbours(i, x) for i in range(3)]
        r = neighbours(3, x)
        t = neighbours(4, x)
        half = [0.5 * v[i][0] for i in range(3)]
        inverse = 1.0 / r[0]
        size = mag[x]
        inject = fuel[x].astype(jnp.float32) * inject_rate
        species = [own(5 + k, x) for k in range(SPECIES)]
        source, release = chemistry(r[0], inverse, t[0], species)

        def advect(n):
            return half[0] * (n[1] - n[2]) + half[1] * (n[3] - n[4]) + half[2] * (n[5] - n[6])

        def laplace(n):
            return ((n[1] + n[2]) + (n[3] + n[4])) + ((n[5] + n[6]) - 6.0 * n[0])

        push = [r[m] * t[m] for m in range(1, 7)]
        scale = 0.5 * inverse
        for i in range(3):
            lap = laplace(v[i])
            value = laminar_diffusivity * lap - advect(v[i]) - (push[2 * i] - push[2 * i + 1]) * scale
            if i == 1:
                value = value + inject * (inject_speed - v[1][0])
            base[i, x] = value
            slope[i, x] = size * lap
        flux = (
            (r[1] * v[0][1] - r[2] * v[0][2])
            + (r[3] * v[1][3] - r[4] * v[1][4])
            + (r[5] * v[2][5] - r[6] * v[2][6])
        )
        base[3, x] = -0.5 * flux
        thin = size * (1.0 / subgrid_thermal_quotient)
        lap = laplace(t)
        base[4, x] = (laminar_diffusivity / momentum_thermal_quotient) * lap - advect(t) + release
        slope[3, x] = thin * lap
        for k in range(SPECIES):
            n = neighbours(5 + k, x)
            lap = laplace(n)
            value = (laminar_diffusivity / schmidt) * lap - advect(n)
            if source[k] is not None:
                value = value + source[k]
            if k == 0:
                value = value + inject * (1.0 - n[0])
            base[5 + k, x] = value
            slope[4 + k, x] = thin * lap


def finish(
    total_z, vel, dens, temp, spec, wall, base, slope, r0, r1, r2, r3, out_v, out_r, out_t, out_y, out_c
):
    nx = dens.shape[0]
    lm = (r0[0:nx] + r1[0:nx]) + (r2[0:nx] + r3[0:nx])
    mm = (r0[nx : 2 * nx] + r1[nx : 2 * nx]) + (r2[nx : 2 * nx] + r3[nx : 2 * nx])
    coef = jnp.maximum(0.5 * (lm / total_z) / (mm / total_z + tiny_value), 0.0)
    out_c[...] = coef
    top = jnp.maximum(
        jnp.maximum(r0[2 * nx :], r1[2 * nx :]), jnp.maximum(r2[2 * nx :], r3[2 * nx :])
    )
    step = courant / jnp.max(jnp.max(top, axis=0, keepdims=True), axis=1, keepdims=True)
    gain = coef * step
    for x in range(nx):
        g = gain[x : x + 1]
        open_cell = 1.0 - wall[x].astype(jnp.float32)
        for i in range(3):
            out_v[i, x] = open_cell * (vel[i, x] + step * base[i, x] + g * slope[i, x])
        out_r[x] = dens[x] + step * base[3, x]
        out_t[x] = temp[x] + step * base[4, x] + g * slope[3, x]
        for k in range(SPECIES):
            out_y[k, x] = spec[k, x] + step * base[5 + k, x] + g * slope[4 + k, x]


def per_device(vel, dens, temp, spec, wall, fuel):
    nx, nz, ny = dens.shape
    n_stream = lax.axis_size("stream")
    n_span = lax.axis_size("span")
    send_a, send_b = call(
        pack_stream, [(7, nz, ny), (6, nz, ny)], (vel, temp), name="pack_stream"
    )
    got_b = lax.ppermute(send_b, "stream", pair_up(n_stream, 1, False))
    got_a = lax.ppermute(send_a, "stream", pair_up(n_stream, 0, False))
    faces = call(
        pack_scalars,
        [(2 + SPECIES, nz, ny)] * 2 + [((2 + SPECIES) * nx, ny)] * 2,
        (dens, temp, spec),
        name="pack_scalars",
    )
    rows = 6 * (nx + 4)
    send_c, send_d = call(
        pack_span, [(rows, ny)] * 2, (vel, got_a, got_b), name="pack_span"
    )
    got_c = lax.ppermute(send_c, "span", pair_up(n_span, 0, True))
    got_d = lax.ppermute(send_d, "span", pair_up(n_span, 1, True))
    far_b = lax.ppermute(faces[1], "stream", pair_up(n_stream, 1, False))
    far_a = lax.ppermute(faces[0], "stream", pair_up(n_stream, 0, False))
    far_c = lax.ppermute(faces[2], "span", pair_up(n_span, 0, True))
    far_d = lax.ppermute(faces[3], "span", pair_up(n_span, 1, True))
    top = jnp.maximum(send_a[6], got_a[6])
    bit = 2
    while bit < n_stream:
        top = jnp.maximum(top, lax.ppermute(top, "stream", flip(n_stream, bit)))
        bit *= 2
    red, mag = call(
        germano,
        [(2 * nx + nz, ny), (nx, nz, ny)],
        (vel, got_a, got_b, got_c, got_d, top),
        scratch=[
            VMEM((3, nx + 4, 2 * nz, ny), jnp.float32),
            VMEM((6, nx + 2, 2 * nz, ny), jnp.float32),
            VMEM((3, nx + 2, 2 * nz, ny), jnp.float32),
        ],
        name="germano",
    )
    base, slope = call(
        tendencies,
        [(5 + SPECIES, nx, nz, ny), (4 + SPECIES, nx, nz, ny)],
        (vel, dens, temp, spec, fuel, got_a, got_b, got_c, got_d, far_a, far_b, far_c, far_d, mag),
        name="tendencies",
    )
    bit = 1
    while bit * 4 < n_span:
        others = [lax.ppermute(red, "span", flip(n_span, bit * m)) for m in (1, 2, 3)]
        low = (red[: 2 * nx] + others[0][: 2 * nx]) + (others[1][: 2 * nx] + others[2][: 2 * nx])
        high = jnp.maximum(
            jnp.maximum(red[2 * nx :], others[0][2 * nx :]),
            jnp.maximum(others[1][2 * nx :], others[2][2 * nx :]),
        )
        red = jnp.concatenate([low, high], axis=0)
        bit *= 4
    others = [lax.ppermute(red, "span", flip(n_span, bit * m)) for m in (3, 2, 1)]
    return tuple(
        call(
            functools.partial(finish, float(nz * n_span)),
            [vel.shape, dens.shape, dens.shape, spec.shape, (nx, ny)],
            (vel, dens, temp, spec, wall, base, slope, red, *others),
            name="finish",
            to_hbm=True,
        )
    )


def solution(mesh):
    return jax.shard_map(
        per_device,
        mesh=mesh,
        in_specs=(
            P(None, "stream", "span", None),
            P("stream", "span", None),
            P("stream", "span", None),
            P(None, "stream", "span", None),
            P("stream", "span", None),
            P("stream", "span", None),
        ),
        out_specs=(
            P(None, "stream", "span", None),
            P("stream", "span", None),
            P("stream", "span", None),
            P(None, "stream", "span", None),
            P("stream", None),
        ),
        check_vma=False,
    )
```

```python
import functools

import jax
import jax.numpy as jnp
import numpy as np
from jax import lax
from jax.experimental import pallas as pl
from jax.experimental.pallas import tpu as pltpu
from jax.sharding import PartitionSpec as P

SPECIES = 9
SCALARS = 11
adiabatic_gamma = 1.4
courant = 0.5
laminar_diffusivity = 0.05
momentum_thermal_quotient = 0.7
schmidt = 0.7
subgrid_thermal_quotient = 0.9
inject_rate = 5.0
inject_speed = 2.0
heat_capacity = 3.5
tiny_value = 1e-06
reaction_list = (
    ((4, 1), (5, 3)),
    ((5, 0), (4, 3)),
    ((0, 3), (2, 4)),
    ((5, 2), (3, 3)),
    ((0, 9), (4, 4)),
    ((5, 5, 9), (1,)),
    ((5, 4, 9), (3,)),
    ((4, 3, 9), (2,)),
    ((4, 1, 9), (6,)),
    ((6, 4), (0, 1)),
    ((6, 4), (3, 3)),
    ((6, 5), (1, 3)),
    ((6, 3), (2, 1)),
    ((6, 6), (7, 1)),
    ((7, 9), (3, 3)),
    ((7, 4), (2, 3)),
    ((7, 4), (6, 0)),
    ((7, 5), (3, 6)),
    ((7, 3), (6, 2)),
)
log_prefactor = np.array(
    [3.9, 3.2, 3.4, 3.0, 2.0, 6.0, 6.2, 6.5, 5.8, 3.8, 3.6, 3.5, 3.7, 3.1, 2.2, 3.3, 3.4, 3.0, 3.2],
    np.float32,
)
thermal_power_index = np.array(
    [
        0.0,
        0.5,
        0.5,
        1.0,
        -1.0,
        -0.5,
        -1.0,
        -2.0,
        -1.0,
        0.0,
        0.0,
        0.0,
        0.0,
        0.0,
        0.0,
        0.0,
        0.0,
        1.0,
        0.0,
    ],
    np.float32,
)
arrhenius_barrier = np.array(
    [
        1.6,
        0.7,
        0.4,
        1.5,
        2.0,
        0.0,
        0.0,
        0.0,
        0.0,
        0.1,
        0.05,
        0.0,
        0.0,
        0.2,
        1.8,
        0.4,
        0.8,
        0.3,
        0.1,
    ],
    np.float32,
)
molar_weight = np.array([0.125, 2.0, 1.125, 1.0625, 0.0625, 1.0, 2.0625, 2.125, 1.75], np.float32)
formation = np.array([0.0, 0.0, -2.42, 0.39, 2.18, 2.49, 0.12, -1.36, 0.0], np.float32)
pair_list = ((0, 0), (1, 1), (2, 2), (0, 1), (0, 2), (1, 2))


VMEM = pltpu.VMEM


def pair_up(count, start, wrap):
    pairs = []
    for low in range(start, count - 1, 2):
        pairs += [(low, low + 1), (low + 1, low)]
    if wrap and start == 1:
        pairs += [(count - 1, 0), (0, count - 1)]
    return pairs


def flip(count, bit):
    return [(index, index ^ bit) for index in range(count)]


def even_index(axis):
    return lax.rem(lax.axis_index(axis), 2) == 0


def call(body, outs, args, scratch=(), flops=0, name=None, from_hbm=False, to_hbm=False):
    nbytes = sum(int(np.prod(a.shape)) * 4 for a in args) + sum(
        int(np.prod(s)) * 4 for s in outs
    )
    return pl.pallas_call(
        body,
        out_shape=[
            jax.ShapeDtypeStruct(s, jnp.float32) if to_hbm else VMEM(s, jnp.float32) for s in outs
        ],
        in_specs=[pl.BlockSpec(memory_space=pltpu.HBM if from_hbm else VMEM)] * len(args),
        out_specs=[pl.BlockSpec(memory_space=VMEM)] * len(outs),
        scratch_shapes=list(scratch),
        compiler_params=pltpu.CompilerParams(vmem_limit_bytes=8 << 20),
        cost_estimate=pl.CostEstimate(flops=flops, bytes_accessed=nbytes, transcendentals=0),
        name=name,
    )(*[a if from_hbm else pltpu.with_memory_space_constraint(a, VMEM) for a in args])


def pack_stream(
    hbm_v, hbm_r, hbm_t, hbm_y, send_a, send_b, far_a, vel, dens, temp, spec, done
):
    copies = [
        pltpu.make_async_copy(src, dst, done.at[k])
        for k, (src, dst) in enumerate(
            ((hbm_v, vel), (hbm_t, temp), (hbm_r, dens), (hbm_y, spec))
        )
    ]
    for copy in copies:
        copy.start()
    even = even_index("stream")
    nx = vel.shape[1]
    copies[0].wait()
    for comp in range(3):
        for layer in range(2):
            low = vel[comp, layer]
            high = vel[comp, nx - 2 + layer]
            send_a[2 * comp + layer] = jnp.where(even, high, low)
            send_b[2 * comp + layer] = jnp.where(even, low, high)
    copies[1].wait()
    fastest = None
    for x in range(nx):
        speed = (
            jnp.abs(vel[0, x])
            + jnp.abs(vel[1, x])
            + jnp.abs(vel[2, x])
            + jnp.sqrt(adiabatic_gamma * temp[x])
        )
        fastest = speed if fastest is None else jnp.maximum(fastest, speed)
    send_a[6] = fastest
    copies[2].wait()
    copies[3].wait()
    for field in range(SCALARS):
        ref = dens if field == 0 else temp if field == 1 else spec.at[field - 2]
        low, high = ref[0], ref[nx - 1]
        far_a[field] = jnp.where(even, high, low)
        send_b[6 + field] = jnp.where(even, low, high)


def pack_span(vel, dens, temp, spec, got_a, got_b, send_c, send_d):
    even_s = even_index("stream")
    even_p = even_index("span")
    nx, nz = vel.shape[1], vel.shape[2]
    for comp in range(3):
        for x in range(nx + 4):
            if x < 2:
                tile = jnp.where(even_s, got_b[2 * comp + x], got_a[2 * comp + x])
            elif x < nx + 2:
                tile = vel[comp, x - 2]
            else:
                at = 2 * comp + x - nx - 2
                tile = jnp.where(even_s, got_a[at], got_b[at])
            first, last = tile[0:2], tile[nz - 2 : nz]
            row = 2 * (comp * (nx + 4) + x)
            send_c[row : row + 2] = jnp.where(even_p, last, first)
            send_d[row : row + 2] = jnp.where(even_p, first, last)
    base = 6 * (nx + 4)
    for field in range(SCALARS):
        ref = dens if field == 0 else temp if field == 1 else spec.at[field - 2]
        first, last = ref[:, 0, :], ref[:, nz - 1, :]
        row = base + field * nx
        send_c[row : row + nx] = jnp.where(even_p, last, first)
        send_d[row : row + nx] = jnp.where(even_p, first, last)


def along_y(tile, lane):
    width = tile.shape[-1]
    after = jnp.where(lane == width - 1, 0.0, pltpu.roll(tile, width - 1, 1))
    before = jnp.where(lane == 0, 0.0, pltpu.roll(tile, 1, 1))
    return after, before


def strain_of(grads):
    parts = [
        grads[i][i] if i == j else 0.5 * (grads[i][j] + grads[j][i]) for i, j in pair_list
    ]
    diagonal = parts[0] * parts[0] + parts[1] * parts[1] + parts[2] * parts[2]
    off = parts[3] * parts[3] + parts[4] * parts[4] + parts[5] * parts[5]
    return parts, jnp.sqrt(2.0 * (diagonal + 2.0 * off))


def germano(vel, got_a, got_b, got_c, got_d, top, red, mag, wide, shear, smooth):
    even_s = even_index("stream")
    even_p = even_index("span")
    nx, nz, ny = vel.shape[1], vel.shape[2], vel.shape[3]
    rows = 2 * nz
    zero = jnp.zeros((nz - 4, ny), jnp.float32)
    for comp in range(3):
        for x in range(nx + 4):
            if x < 2:
                tile = jnp.where(even_s, got_b[2 * comp + x], got_a[2 * comp + x])
            elif x < nx + 2:
                tile = vel[comp, x - 2]
            else:
                at = 2 * comp + x - nx - 2
                tile = jnp.where(even_s, got_a[at], got_b[at])
            row = 2 * (comp * (nx + 4) + x)
            one, two = got_c[row : row + 2], got_d[row : row + 2]
            wide[comp, x, 0:nz] = tile
            wide[comp, x, nz : nz + 2] = jnp.where(even_p, one, two)
            wide[comp, x, nz + 2 : rows - 2] = zero
            wide[comp, x, rows - 2 : rows] = jnp.where(even_p, two, one)
    lane = lax.broadcasted_iota(jnp.int32, (rows, ny), 1)

    def z_after(tile):
        return pltpu.roll(tile, rows - 1, 0)

    def z_before(tile):
        return pltpu.roll(tile, 1, 0)

    def gradients(ref, x, i):
        center = ref[i, x]
        after, before = along_y(center, lane)
        return [
            0.5 * (ref[i, x + 1] - ref[i, x - 1]),
            0.5 * (after - before),
            0.5 * (z_after(center) - z_before(center)),
        ]

    def z_filter(tile):
        return 0.25 * (z_after(tile) + z_before(tile)) + 0.5 * tile

    def x_filter(take):
        return 0.25 * (take(-1) + take(1)) + 0.5 * take(0)

    position = lax.axis_index("stream") * nx
    total = lax.axis_size("stream") * nx

    for x in range(nx + 2):
        keep = None
        if x == 0:
            keep = jnp.where(position > 0, 1.0, 0.0)
        elif x == nx + 1:
            keep = jnp.where(position + nx < total, 1.0, 0.0)
        parts, size = strain_of([gradients(wide, x + 1, i) for i in range(3)])
        if 1 <= x <= nx:
            mag[x - 1] = size[0:nz]
        if keep is not None:
            size = size * keep
        for k in range(6):
            shear[k, x] = size * parts[k]
        for i in range(3):
            value = z_filter(x_filter(lambda d: wide[i, x + 1 + d]))
            smooth[i, x] = value if keep is None else value * keep
    for x in range(nx):
        hat_parts, hat_size = strain_of([gradients(smooth, x + 1, i) for i in range(3)])
        lm = jnp.zeros((rows, ny), jnp.float32)
        mm = jnp.zeros((rows, ny), jnp.float32)
        for k, (i, j) in enumerate(pair_list):
            weight = 1.0 if i == j else 2.0
            product = z_filter(x_filter(lambda d: wide[i, x + 2 + d] * wide[j, x + 2 + d]))
            resolved = product - smooth[i, x + 1] * smooth[j, x + 1]
            model = z_filter(x_filter(lambda d: shear[k, x + 1 + d])) - 4.0 * hat_size * hat_parts[k]
            lm = lm + weight * resolved * model
            mm = mm + weight * model * model
        red[x : x + 1] = jnp.sum(lm[0:nz], axis=0, keepdims=True)
        red[nx + x : nx + x + 1] = jnp.sum(mm[0:nz], axis=0, keepdims=True)
    red[2 * nx : 2 * nx + nz] = top[...]


def chemistry(dens, inverse, temp, species):
    over = 1.0 / temp
    root = jnp.sqrt(temp)
    powers = {0.0: None, 0.5: root, 1.0: temp, -1.0: over, -0.5: root * over, -2.0: over * over}
    e05 = jnp.exp(-0.05 * over)
    e15 = jnp.exp(-1.5 * over)
    decay = {0: None, 5: e05, 150: e15}
    decay[10] = e05 * e05
    decay[20] = decay[10] * decay[10]
    decay[30] = decay[20] * decay[10]
    decay[40] = decay[20] * decay[20]
    decay[70] = decay[40] * decay[30]
    decay[80] = decay[40] * decay[40]
    decay[160] = e15 * decay[10]
    decay[180] = e15 * decay[30]
    decay[200] = decay[180] * decay[20]
    conc = [dens * (species[k] * float(1.0 / molar_weight[k])) for k in range(SPECIES)]
    total = conc[0]
    for k in range(1, SPECIES):
        total = total + conc[k]
    conc.append(total)
    products = {}

    def product(ids):
        if len(ids) == 1:
            return conc[ids[0]]
        if ids not in products:
            products[ids] = product(ids[:-1]) * conc[ids[-1]]
        return products[ids]

    produced = [None] * SPECIES
    for number, (reactants, results) in enumerate(reaction_list):
        ordered = tuple(sorted(reactants))
        pace = product(ordered) * float(np.exp(np.float64(log_prefactor[number])))
        power = powers[float(thermal_power_index[number])]
        if power is not None:
            pace = pace * power
        fall = decay[int(round(float(arrhenius_barrier[number]) * 100))]
        if fall is not None:
            pace = pace * fall
        change = {}
        for k in reactants:
            if k < SPECIES:
                change[k] = change.get(k, 0) - 1
        for k in results:
            change[k] = change.get(k, 0) + 1
        for k, times in change.items():
            if times == 0:
                continue
            term = pace if abs(times) == 1 else pace * float(abs(times))
            if produced[k] is None:
                produced[k] = term if times > 0 else -term
            else:
                produced[k] = produced[k] + term if times > 0 else produced[k] - term
    heat = None
    for k in range(SPECIES):
        if formation[k] != 0.0 and produced[k] is not None:
            term = produced[k] * float(-formation[k] / heat_capacity)
            heat = term if heat is None else heat + term
    source = [
        None if produced[k] is None else produced[k] * inverse * float(molar_weight[k])
        for k in range(SPECIES)
    ]
    return source, heat * inverse


def tendencies(
    vel, dens, temp, spec, fuel, got_a, got_b, got_c, got_d, far_a, mag, base, slope
):
    even_s = even_index("stream")
    even_p = even_index("span")
    nx, nz, ny = dens.shape
    lane = lax.broadcasted_iota(jnp.int32, (nz, ny), 1)
    line = lax.broadcasted_iota(jnp.int32, (nz, ny), 0)

    def own(field, x):
        if field < 3:
            return vel[field, x]
        if field == 3:
            return dens[x]
        if field == 4:
            return temp[x]
        return spec[field - 5, x]

    def cell(field, x):
        if 0 <= x < nx:
            return own(field, x)
        if field < 3:
            at = 2 * field + (1 if x < 0 else 0)
            one, two = got_a[at], got_b[at]
        else:
            one, two = far_a[field - 3], got_b[3 + field]
        return jnp.where(even_s, two, one) if x < 0 else jnp.where(even_s, one, two)

    def edges(field, x):
        if field < 3:
            row = 2 * (field * (nx + 4) + x + 2)
            c0, c1 = got_c[row : row + 1], got_c[row + 1 : row + 2]
            d0, d1 = got_d[row : row + 1], got_d[row + 1 : row + 2]
            return jnp.where(even_p, c0, d0), jnp.where(even_p, d1, c1)
        row = 6 * (nx + 4) + (field - 3) * nx + x
        c0, d0 = got_c[row : row + 1], got_d[row : row + 1]
        return jnp.where(even_p, c0, d0), jnp.where(even_p, d0, c0)

    def neighbours(field, x):
        center = own(field, x)
        after, before = along_y(center, lane)
        high, low = edges(field, x)
        up = jnp.where(line == nz - 1, high, pltpu.roll(center, nz - 1, 0))
        down = jnp.where(line == 0, low, pltpu.roll(center, 1, 0))
        return center, cell(field, x + 1), cell(field, x - 1), after, before, up, down

    for x in range(nx):
        v = [neighbours(i, x) for i in range(3)]
        r = neighbours(3, x)
        t = neighbours(4, x)
        half = [0.5 * v[i][0] for i in range(3)]
        inverse = 1.0 / r[0]
        size = mag[x]
        inject = fuel[x].astype(jnp.float32) * inject_rate
        species = [own(5 + k, x) for k in range(SPECIES)]
        source, release = chemistry(r[0], inverse, t[0], species)

        def advect(n):
            return half[0] * (n[1] - n[2]) + half[1] * (n[3] - n[4]) + half[2] * (n[5] - n[6])

        def laplace(n):
            return ((n[1] + n[2]) + (n[3] + n[4])) + ((n[5] + n[6]) - 6.0 * n[0])

        push = [r[m] * t[m] for m in range(1, 7)]
        scale = 0.5 * inverse
        for i in range(3):
            lap = laplace(v[i])
            value = laminar_diffusivity * lap - advect(v[i]) - (push[2 * i] - push[2 * i + 1]) * scale
            if i == 1:
                value = value + inject * (inject_speed - v[1][0])
            base[i, x] = value
            slope[i, x] = size * lap
        flux = (
            (r[1] * v[0][1] - r[2] * v[0][2])
            + (r[3] * v[1][3] - r[4] * v[1][4])
            + (r[5] * v[2][5] - r[6] * v[2][6])
        )
        base[3, x] = -0.5 * flux
        thin = size * (1.0 / subgrid_thermal_quotient)
        lap = laplace(t)
        base[4, x] = (laminar_diffusivity / momentum_thermal_quotient) * lap - advect(t) + release
        slope[3, x] = thin * lap
        for k in range(SPECIES):
            n = neighbours(5 + k, x)
            lap = laplace(n)
            value = (laminar_diffusivity / schmidt) * lap - advect(n)
            if source[k] is not None:
                value = value + source[k]
            if k == 0:
                value = value + inject * (1.0 - n[0])
            base[5 + k, x] = value
            slope[4 + k, x] = thin * lap


def finish(
    total_z, vel, dens, temp, spec, wall, base, slope, r0, r1, r2, r3, out_v, out_r, out_t, out_y, out_c
):
    nx = dens.shape[0]
    lm = (r0[0:nx] + r1[0:nx]) + (r2[0:nx] + r3[0:nx])
    mm = (r0[nx : 2 * nx] + r1[nx : 2 * nx]) + (r2[nx : 2 * nx] + r3[nx : 2 * nx])
    coef = jnp.maximum(0.5 * (lm / total_z) / (mm / total_z + tiny_value), 0.0)
    out_c[...] = coef
    top = jnp.maximum(
        jnp.maximum(r0[2 * nx :], r1[2 * nx :]), jnp.maximum(r2[2 * nx :], r3[2 * nx :])
    )
    step = courant / jnp.max(jnp.max(top, axis=0, keepdims=True), axis=1, keepdims=True)
    gain = coef * step
    for x in range(nx):
        g = gain[x : x + 1]
        open_cell = 1.0 - wall[x].astype(jnp.float32)
        for i in range(3):
            out_v[i, x] = open_cell * (vel[i, x] + step * base[i, x] + g * slope[i, x])
        out_r[x] = dens[x] + step * base[3, x]
        out_t[x] = temp[x] + step * base[4, x] + g * slope[3, x]
        for k in range(SPECIES):
            out_y[k, x] = spec[k, x] + step * base[5 + k, x] + g * slope[4 + k, x]


def per_device(vel, dens, temp, spec, wall, fuel):
    nx, nz, ny = dens.shape
    n_stream = lax.axis_size("stream")
    n_span = lax.axis_size("span")
    send_a, send_b, send_far, vel, dens, temp, spec = call(
        pack_stream,
        [(7, nz, ny), (6 + SCALARS, nz, ny), (SCALARS, nz, ny)]
        + [vel.shape, dens.shape, temp.shape, spec.shape],
        (vel, dens, temp, spec),
        scratch=[pltpu.SemaphoreType.DMA((4,))],
        name="pack_stream",
        from_hbm=True,
    )
    far_a = lax.ppermute(send_far, "stream", pair_up(n_stream, 0, False))
    got_a = lax.ppermute(send_a, "stream", pair_up(n_stream, 0, False))
    got_b = lax.ppermute(send_b, "stream", pair_up(n_stream, 1, False))
    rows = 6 * (nx + 4) + SCALARS * nx
    send_c, send_d = call(
        pack_span, [(rows, ny)] * 2, (vel, dens, temp, spec, got_a, got_b), name="pack_span"
    )
    got_c = lax.ppermute(send_c, "span", pair_up(n_span, 0, True))
    got_d = lax.ppermute(send_d, "span", pair_up(n_span, 1, True))
    top = jnp.maximum(send_a[6], got_a[6])
    bit = 2
    while bit < n_stream:
        top = jnp.maximum(top, lax.ppermute(top, "stream", flip(n_stream, bit)))
        bit *= 2
    red, mag = call(
        germano,
        [(2 * nx + nz, ny), (nx, nz, ny)],
        (vel, got_a, got_b, got_c, got_d, top),
        scratch=[
            VMEM((3, nx + 4, 2 * nz, ny), jnp.float32),
            VMEM((6, nx + 2, 2 * nz, ny), jnp.float32),
            VMEM((3, nx + 2, 2 * nz, ny), jnp.float32),
        ],
        name="germano",
    )
    base, slope = call(
        tendencies,
        [(5 + SPECIES, nx, nz, ny), (4 + SPECIES, nx, nz, ny)],
        (vel, dens, temp, spec, fuel, got_a, got_b, got_c, got_d, far_a, mag),
        name="tendencies",
    )
    bit = 1
    while bit * 4 < n_span:
        others = [lax.ppermute(red, "span", flip(n_span, bit * m)) for m in (1, 2, 3)]
        low = (red[: 2 * nx] + others[0][: 2 * nx]) + (others[1][: 2 * nx] + others[2][: 2 * nx])
        high = jnp.maximum(
            jnp.maximum(red[2 * nx :], others[0][2 * nx :]),
            jnp.maximum(others[1][2 * nx :], others[2][2 * nx :]),
        )
        red = jnp.concatenate([low, high], axis=0)
        bit *= 4
    others = [lax.ppermute(red, "span", flip(n_span, bit * m)) for m in (3, 2, 1)]
    return tuple(
        call(
            functools.partial(finish, float(nz * n_span)),
            [vel.shape, dens.shape, dens.shape, spec.shape, (nx, ny)],
            (vel, dens, temp, spec, wall, base, slope, red, *others),
            name="finish",
            to_hbm=True,
        )
    )


def solution(mesh):
    return jax.shard_map(
        per_device,
        mesh=mesh,
        in_specs=(
            P(None, "stream", "span", None),
            P("stream", "span", None),
            P("stream", "span", None),
            P(None, "stream", "span", None),
            P("stream", "span", None),
            P("stream", "span", None),
        ),
        out_specs=(
            P(None, "stream", "span", None),
            P("stream", "span", None),
            P("stream", "span", None),
            P(None, "stream", "span", None),
            P("stream", None),
        ),
        check_vma=False,
    )
```

```python
import functools

import jax
import jax.numpy as jnp
import numpy as np
from jax import lax
from jax.experimental import pallas as pl
from jax.experimental.pallas import tpu as pltpu
from jax.sharding import PartitionSpec as P

SPECIES = 9
SCALARS = 11
adiabatic_gamma = 1.4
courant = 0.5
laminar_diffusivity = 0.05
momentum_thermal_quotient = 0.7
schmidt = 0.7
subgrid_thermal_quotient = 0.9
inject_rate = 5.0
inject_speed = 2.0
heat_capacity = 3.5
tiny_value = 1e-06
reaction_list = (
    ((4, 1), (5, 3)),
    ((5, 0), (4, 3)),
    ((0, 3), (2, 4)),
    ((5, 2), (3, 3)),
    ((0, 9), (4, 4)),
    ((5, 5, 9), (1,)),
    ((5, 4, 9), (3,)),
    ((4, 3, 9), (2,)),
    ((4, 1, 9), (6,)),
    ((6, 4), (0, 1)),
    ((6, 4), (3, 3)),
    ((6, 5), (1, 3)),
    ((6, 3), (2, 1)),
    ((6, 6), (7, 1)),
    ((7, 9), (3, 3)),
    ((7, 4), (2, 3)),
    ((7, 4), (6, 0)),
    ((7, 5), (3, 6)),
    ((7, 3), (6, 2)),
)
log_prefactor = np.array(
    [3.9, 3.2, 3.4, 3.0, 2.0, 6.0, 6.2, 6.5, 5.8, 3.8, 3.6, 3.5, 3.7, 3.1, 2.2, 3.3, 3.4, 3.0, 3.2],
    np.float32,
)
thermal_power_index = np.array(
    [
        0.0,
        0.5,
        0.5,
        1.0,
        -1.0,
        -0.5,
        -1.0,
        -2.0,
        -1.0,
        0.0,
        0.0,
        0.0,
        0.0,
        0.0,
        0.0,
        0.0,
        0.0,
        1.0,
        0.0,
    ],
    np.float32,
)
arrhenius_barrier = np.array(
    [
        1.6,
        0.7,
        0.4,
        1.5,
        2.0,
        0.0,
        0.0,
        0.0,
        0.0,
        0.1,
        0.05,
        0.0,
        0.0,
        0.2,
        1.8,
        0.4,
        0.8,
        0.3,
        0.1,
    ],
    np.float32,
)
molar_weight = np.array([0.125, 2.0, 1.125, 1.0625, 0.0625, 1.0, 2.0625, 2.125, 1.75], np.float32)
formation = np.array([0.0, 0.0, -2.42, 0.39, 2.18, 2.49, 0.12, -1.36, 0.0], np.float32)
pair_list = ((0, 0), (1, 1), (2, 2), (0, 1), (0, 2), (1, 2))


VMEM = pltpu.VMEM


def pair_up(count, start, wrap):
    pairs = []
    for low in range(start, count - 1, 2):
        pairs += [(low, low + 1), (low + 1, low)]
    if wrap and start == 1:
        pairs += [(count - 1, 0), (0, count - 1)]
    return pairs


def flip(count, bit):
    return [(index, index ^ bit) for index in range(count)]


def even_index(axis):
    return lax.rem(lax.axis_index(axis), 2) == 0


def call(body, outs, args, scratch=(), flops=0, name=None, from_hbm=False, to_hbm=False):
    nbytes = sum(int(np.prod(a.shape)) * 4 for a in args) + sum(
        int(np.prod(s)) * 4 for s in outs
    )
    return pl.pallas_call(
        body,
        out_shape=[
            jax.ShapeDtypeStruct(s, jnp.float32) if to_hbm else VMEM(s, jnp.float32) for s in outs
        ],
        in_specs=[pl.BlockSpec(memory_space=pltpu.HBM if from_hbm else VMEM)] * len(args),
        out_specs=[pl.BlockSpec(memory_space=VMEM)] * len(outs),
        scratch_shapes=list(scratch),
        compiler_params=pltpu.CompilerParams(vmem_limit_bytes=8 << 20),
        cost_estimate=pl.CostEstimate(flops=flops, bytes_accessed=nbytes, transcendentals=0),
        name=name,
    )(*[pltpu.with_memory_space_constraint(a, pltpu.HBM if from_hbm else VMEM) for a in args])


def pack_stream(
    hbm_v, hbm_r, hbm_t, hbm_y, send_a, send_b, far_a, vel, dens, temp, spec, done
):
    copies = [
        pltpu.make_async_copy(src, dst, done.at[k])
        for k, (src, dst) in enumerate(
            ((hbm_v, vel), (hbm_t, temp), (hbm_r, dens), (hbm_y, spec))
        )
    ]
    for copy in copies:
        copy.start()
    even = even_index("stream")
    nx = vel.shape[1]
    copies[0].wait()
    for comp in range(3):
        for layer in range(2):
            low = vel[comp, layer]
            high = vel[comp, nx - 2 + layer]
            send_a[2 * comp + layer] = jnp.where(even, high, low)
            send_b[2 * comp + layer] = jnp.where(even, low, high)
    copies[1].wait()
    fastest = None
    for x in range(nx):
        speed = (
            jnp.abs(vel[0, x])
            + jnp.abs(vel[1, x])
            + jnp.abs(vel[2, x])
            + jnp.sqrt(adiabatic_gamma * temp[x])
        )
        fastest = speed if fastest is None else jnp.maximum(fastest, speed)
    send_a[6] = fastest
    copies[2].wait()
    copies[3].wait()
    for field in range(SCALARS):
        ref = dens if field == 0 else temp if field == 1 else spec.at[field - 2]
        low, high = ref[0], ref[nx - 1]
        far_a[field] = jnp.where(even, high, low)
        send_b[6 + field] = jnp.where(even, low, high)


def pack_span(vel, dens, temp, spec, got_a, got_b, near, got_n, send_c, send_d, top):
    even_s = even_index("stream")
    even_p = even_index("span")
    nx, nz = vel.shape[1], vel.shape[2]
    for comp in range(3):
        for x in range(nx + 4):
            if x < 2:
                tile = jnp.where(even_s, got_b[2 * comp + x], got_a[2 * comp + x])
            elif x < nx + 2:
                tile = vel[comp, x - 2]
            else:
                at = 2 * comp + x - nx - 2
                tile = jnp.where(even_s, got_a[at], got_b[at])
            first, last = tile[0:2], tile[nz - 2 : nz]
            row = 2 * (comp * (nx + 4) + x)
            send_c[row : row + 2] = jnp.where(even_p, last, first)
            send_d[row : row + 2] = jnp.where(even_p, first, last)
    top[...] = jnp.maximum(near[...], got_n[...])
    base = 6 * (nx + 4)
    for field in range(SCALARS):
        ref = dens if field == 0 else temp if field == 1 else spec.at[field - 2]
        first, last = ref[:, 0, :], ref[:, nz - 1, :]
        row = base + field * nx
        send_c[row : row + nx] = jnp.where(even_p, last, first)
        send_d[row : row + nx] = jnp.where(even_p, first, last)


def along_y(tile, lane):
    width = tile.shape[-1]
    after = jnp.where(lane == width - 1, 0.0, pltpu.roll(tile, width - 1, 1))
    before = jnp.where(lane == 0, 0.0, pltpu.roll(tile, 1, 1))
    return after, before


def strain_of(grads):
    parts = [
        grads[i][i] if i == j else 0.5 * (grads[i][j] + grads[j][i]) for i, j in pair_list
    ]
    diagonal = parts[0] * parts[0] + parts[1] * parts[1] + parts[2] * parts[2]
    off = parts[3] * parts[3] + parts[4] * parts[4] + parts[5] * parts[5]
    return parts, jnp.sqrt(2.0 * (diagonal + 2.0 * off))


def germano(vel, got_a, got_b, got_c, got_d, near, got_n, red, mag, wide, shear, smooth):
    even_s = even_index("stream")
    even_p = even_index("span")
    nx, nz, ny = vel.shape[1], vel.shape[2], vel.shape[3]
    rows = 2 * nz
    zero = jnp.zeros((nz - 4, ny), jnp.float32)
    for comp in range(3):
        for x in range(nx + 4):
            if x < 2:
                tile = jnp.where(even_s, got_b[2 * comp + x], got_a[2 * comp + x])
            elif x < nx + 2:
                tile = vel[comp, x - 2]
            else:
                at = 2 * comp + x - nx - 2
                tile = jnp.where(even_s, got_a[at], got_b[at])
            row = 2 * (comp * (nx + 4) + x)
            one, two = got_c[row : row + 2], got_d[row : row + 2]
            wide[comp, x, 0:nz] = tile
            wide[comp, x, nz : nz + 2] = jnp.where(even_p, one, two)
            wide[comp, x, nz + 2 : rows - 2] = zero
            wide[comp, x, rows - 2 : rows] = jnp.where(even_p, two, one)
    lane = lax.broadcasted_iota(jnp.int32, (rows, ny), 1)

    def z_after(tile):
        return pltpu.roll(tile, rows - 1, 0)

    def z_before(tile):
        return pltpu.roll(tile, 1, 0)

    def gradients(ref, x, i):
        center = ref[i, x]
        after, before = along_y(center, lane)
        return [
            0.5 * (ref[i, x + 1] - ref[i, x - 1]),
            0.5 * (after - before),
            0.5 * (z_after(center) - z_before(center)),
        ]

    def z_filter(tile):
        return 0.25 * (z_after(tile) + z_before(tile)) + 0.5 * tile

    def x_filter(take):
        return 0.25 * (take(-1) + take(1)) + 0.5 * take(0)

    position = lax.axis_index("stream") * nx
    total = lax.axis_size("stream") * nx

    for x in range(nx + 2):
        keep = None
        if x == 0:
            keep = jnp.where(position > 0, 1.0, 0.0)
        elif x == nx + 1:
            keep = jnp.where(position + nx < total, 1.0, 0.0)
        parts, size = strain_of([gradients(wide, x + 1, i) for i in range(3)])
        if 1 <= x <= nx:
            mag[x - 1] = size[0:nz]
        if keep is not None:
            size = size * keep
        for k in range(6):
            shear[k, x] = size * parts[k]
        for i in range(3):
            value = z_filter(x_filter(lambda d: wide[i, x + 1 + d]))
            smooth[i, x] = value if keep is None else value * keep
    for x in range(nx):
        hat_parts, hat_size = strain_of([gradients(smooth, x + 1, i) for i in range(3)])
        lm = jnp.zeros((rows, ny), jnp.float32)
        mm = jnp.zeros((rows, ny), jnp.float32)
        for k, (i, j) in enumerate(pair_list):
            weight = 1.0 if i == j else 2.0
            product = z_filter(x_filter(lambda d: wide[i, x + 2 + d] * wide[j, x + 2 + d]))
            resolved = product - smooth[i, x + 1] * smooth[j, x + 1]
            model = z_filter(x_filter(lambda d: shear[k, x + 1 + d])) - 4.0 * hat_size * hat_parts[k]
            lm = lm + weight * resolved * model
            mm = mm + weight * model * model
        red[x : x + 1] = jnp.sum(lm[0:nz], axis=0, keepdims=True)
        red[nx + x : nx + x + 1] = jnp.sum(mm[0:nz], axis=0, keepdims=True)
    red[2 * nx : 2 * nx + nz] = jnp.maximum(near[...], got_n[...])


def chemistry(dens, inverse, temp, species):
    over = 1.0 / temp
    root = jnp.sqrt(temp)
    powers = {0.0: None, 0.5: root, 1.0: temp, -1.0: over, -0.5: root * over, -2.0: over * over}
    e05 = jnp.exp(-0.05 * over)
    e15 = jnp.exp(-1.5 * over)
    decay = {0: None, 5: e05, 150: e15}
    decay[10] = e05 * e05
    decay[20] = decay[10] * decay[10]
    decay[30] = decay[20] * decay[10]
    decay[40] = decay[20] * decay[20]
    decay[70] = decay[40] * decay[30]
    decay[80] = decay[40] * decay[40]
    decay[160] = e15 * decay[10]
    decay[180] = e15 * decay[30]
    decay[200] = decay[180] * decay[20]
    conc = [dens * (species[k] * float(1.0 / molar_weight[k])) for k in range(SPECIES)]
    total = conc[0]
    for k in range(1, SPECIES):
        total = total + conc[k]
    conc.append(total)
    products = {}

    def product(ids):
        if len(ids) == 1:
            return conc[ids[0]]
        if ids not in products:
            products[ids] = product(ids[:-1]) * conc[ids[-1]]
        return products[ids]

    produced = [None] * SPECIES
    for number, (reactants, results) in enumerate(reaction_list):
        ordered = tuple(sorted(reactants))
        pace = product(ordered) * float(np.exp(np.float64(log_prefactor[number])))
        power = powers[float(thermal_power_index[number])]
        if power is not None:
            pace = pace * power
        fall = decay[int(round(float(arrhenius_barrier[number]) * 100))]
        if fall is not None:
            pace = pace * fall
        change = {}
        for k in reactants:
            if k < SPECIES:
                change[k] = change.get(k, 0) - 1
        for k in results:
            change[k] = change.get(k, 0) + 1
        for k, times in change.items():
            if times == 0:
                continue
            term = pace if abs(times) == 1 else pace * float(abs(times))
            if produced[k] is None:
                produced[k] = term if times > 0 else -term
            else:
                produced[k] = produced[k] + term if times > 0 else produced[k] - term
    heat = None
    for k in range(SPECIES):
        if formation[k] != 0.0 and produced[k] is not None:
            term = produced[k] * float(-formation[k] / heat_capacity)
            heat = term if heat is None else heat + term
    source = [
        None if produced[k] is None else produced[k] * inverse * float(molar_weight[k])
        for k in range(SPECIES)
    ]
    return source, heat * inverse


def tendencies(
    vel, dens, temp, spec, fuel, got_a, got_b, got_c, got_d, far_a, mag, base, slope
):
    even_s = even_index("stream")
    even_p = even_index("span")
    nx, nz, ny = dens.shape
    lane = lax.broadcasted_iota(jnp.int32, (nz, ny), 1)
    line = lax.broadcasted_iota(jnp.int32, (nz, ny), 0)

    def own(field, x):
        if field < 3:
            return vel[field, x]
        if field == 3:
            return dens[x]
        if field == 4:
            return temp[x]
        return spec[field - 5, x]

    def cell(field, x):
        if 0 <= x < nx:
            return own(field, x)
        if field < 3:
            at = 2 * field + (1 if x < 0 else 0)
            one, two = got_a[at], got_b[at]
        else:
            one, two = far_a[field - 3], got_b[3 + field]
        return jnp.where(even_s, two, one) if x < 0 else jnp.where(even_s, one, two)

    def edges(field, x):
        if field < 3:
            row = 2 * (field * (nx + 4) + x + 2)
            c0, c1 = got_c[row : row + 1], got_c[row + 1 : row + 2]
            d0, d1 = got_d[row : row + 1], got_d[row + 1 : row + 2]
            return jnp.where(even_p, c0, d0), jnp.where(even_p, d1, c1)
        row = 6 * (nx + 4) + (field - 3) * nx + x
        c0, d0 = got_c[row : row + 1], got_d[row : row + 1]
        return jnp.where(even_p, c0, d0), jnp.where(even_p, d0, c0)

    def neighbours(field, x):
        center = own(field, x)
        after, before = along_y(center, lane)
        high, low = edges(field, x)
        up = jnp.where(line == nz - 1, high, pltpu.roll(center, nz - 1, 0))
        down = jnp.where(line == 0, low, pltpu.roll(center, 1, 0))
        return center, cell(field, x + 1), cell(field, x - 1), after, before, up, down

    for x in range(nx):
        v = [neighbours(i, x) for i in range(3)]
        r = neighbours(3, x)
        t = neighbours(4, x)
        half = [0.5 * v[i][0] for i in range(3)]
        inverse = 1.0 / r[0]
        size = mag[x]
        inject = fuel[x].astype(jnp.float32) * inject_rate
        species = [own(5 + k, x) for k in range(SPECIES)]
        source, release = chemistry(r[0], inverse, t[0], species)

        def advect(n):
            return half[0] * (n[1] - n[2]) + half[1] * (n[3] - n[4]) + half[2] * (n[5] - n[6])

        def laplace(n):
            return ((n[1] + n[2]) + (n[3] + n[4])) + ((n[5] + n[6]) - 6.0 * n[0])

        push = [r[m] * t[m] for m in range(1, 7)]
        scale = 0.5 * inverse
        for i in range(3):
            lap = laplace(v[i])
            value = laminar_diffusivity * lap - advect(v[i]) - (push[2 * i] - push[2 * i + 1]) * scale
            if i == 1:
                value = value + inject * (inject_speed - v[1][0])
            base[i, x] = value
            slope[i, x] = size * lap
        flux = (
            (r[1] * v[0][1] - r[2] * v[0][2])
            + (r[3] * v[1][3] - r[4] * v[1][4])
            + (r[5] * v[2][5] - r[6] * v[2][6])
        )
        base[3, x] = -0.5 * flux
        thin = size * (1.0 / subgrid_thermal_quotient)
        lap = laplace(t)
        base[4, x] = (laminar_diffusivity / momentum_thermal_quotient) * lap - advect(t) + release
        slope[3, x] = thin * lap
        for k in range(SPECIES):
            n = neighbours(5 + k, x)
            lap = laplace(n)
            value = (laminar_diffusivity / schmidt) * lap - advect(n)
            if source[k] is not None:
                value = value + source[k]
            if k == 0:
                value = value + inject * (1.0 - n[0])
            base[5 + k, x] = value
            slope[4 + k, x] = thin * lap


def finish(
    total_z, vel, dens, temp, spec, wall, base, slope, r0, r1, r2, r3, out_v, out_r, out_t, out_y, out_c
):
    nx = dens.shape[0]
    lm = (r0[0:nx] + r1[0:nx]) + (r2[0:nx] + r3[0:nx])
    mm = (r0[nx : 2 * nx] + r1[nx : 2 * nx]) + (r2[nx : 2 * nx] + r3[nx : 2 * nx])
    coef = jnp.maximum(0.5 * (lm / total_z) / (mm / total_z + tiny_value), 0.0)
    out_c[...] = coef
    top = jnp.maximum(
        jnp.maximum(r0[2 * nx :], r1[2 * nx :]), jnp.maximum(r2[2 * nx :], r3[2 * nx :])
    )
    step = courant / jnp.max(jnp.max(top, axis=0, keepdims=True), axis=1, keepdims=True)
    gain = coef * step
    for x in range(nx):
        g = gain[x : x + 1]
        open_cell = 1.0 - wall[x].astype(jnp.float32)
        for i in range(3):
            out_v[i, x] = open_cell * (vel[i, x] + step * base[i, x] + g * slope[i, x])
        out_r[x] = dens[x] + step * base[3, x]
        out_t[x] = temp[x] + step * base[4, x] + g * slope[3, x]
        for k in range(SPECIES):
            out_y[k, x] = spec[k, x] + step * base[5 + k, x] + g * slope[4 + k, x]


def per_device(vel, dens, temp, spec, wall, fuel):
    nx, nz, ny = dens.shape
    n_stream = lax.axis_size("stream")
    n_span = lax.axis_size("span")
    send_a, send_b, send_far, vel, dens, temp, spec = call(
        pack_stream,
        [(7, nz, ny), (6 + SCALARS, nz, ny), (SCALARS, nz, ny)]
        + [vel.shape, dens.shape, temp.shape, spec.shape],
        (vel, dens, temp, spec),
        scratch=[pltpu.SemaphoreType.DMA((4,))],
        name="pack_stream",
        from_hbm=True,
    )
    far_a = lax.ppermute(send_far, "stream", pair_up(n_stream, 0, False))
    got_a = lax.ppermute(send_a, "stream", pair_up(n_stream, 0, False))
    got_b = lax.ppermute(send_b, "stream", pair_up(n_stream, 1, False))
    near = jnp.maximum(send_a[6], got_a[6])
    got_n = lax.ppermute(near, "stream", flip(n_stream, 2))
    rows = 6 * (nx + 4) + SCALARS * nx
    send_c, send_d, near = call(
        pack_span,
        [(rows, ny), (rows, ny), (nz, ny)],
        (vel, dens, temp, spec, got_a, got_b, near, got_n),
        name="pack_span",
    )
    got_c = lax.ppermute(send_c, "span", pair_up(n_span, 0, True))
    got_d = lax.ppermute(send_d, "span", pair_up(n_span, 1, True))
    bit = 4
    while bit * 2 < n_stream:
        near = jnp.maximum(near, lax.ppermute(near, "stream", flip(n_stream, bit)))
        bit *= 2
    got_n = lax.ppermute(near, "stream", flip(n_stream, bit))
    red, mag = call(
        germano,
        [(2 * nx + nz, ny), (nx, nz, ny)],
        (vel, got_a, got_b, got_c, got_d, near, got_n),
        scratch=[
            VMEM((3, nx + 4, 2 * nz, ny), jnp.float32),
            VMEM((6, nx + 2, 2 * nz, ny), jnp.float32),
            VMEM((3, nx + 2, 2 * nz, ny), jnp.float32),
        ],
        name="germano",
    )
    base, slope = call(
        tendencies,
        [(5 + SPECIES, nx, nz, ny), (4 + SPECIES, nx, nz, ny)],
        (vel, dens, temp, spec, fuel, got_a, got_b, got_c, got_d, far_a, mag),
        name="tendencies",
    )
    bit = 1
    while bit * 4 < n_span:
        others = [lax.ppermute(red, "span", flip(n_span, bit * m)) for m in (1, 2, 3)]
        low = (red[: 2 * nx] + others[0][: 2 * nx]) + (others[1][: 2 * nx] + others[2][: 2 * nx])
        high = jnp.maximum(
            jnp.maximum(red[2 * nx :], others[0][2 * nx :]),
            jnp.maximum(others[1][2 * nx :], others[2][2 * nx :]),
        )
        red = jnp.concatenate([low, high], axis=0)
        bit *= 4
    others = [lax.ppermute(red, "span", flip(n_span, bit * m)) for m in (3, 2, 1)]
    return tuple(
        call(
            functools.partial(finish, float(nz * n_span)),
            [vel.shape, dens.shape, dens.shape, spec.shape, (nx, ny)],
            (vel, dens, temp, spec, wall, base, slope, red, *others),
            name="finish",
            to_hbm=True,
        )
    )


def solution(mesh):
    return jax.shard_map(
        per_device,
        mesh=mesh,
        in_specs=(
            P(None, "stream", "span", None),
            P("stream", "span", None),
            P("stream", "span", None),
            P(None, "stream", "span", None),
            P("stream", "span", None),
            P("stream", "span", None),
        ),
        out_specs=(
            P(None, "stream", "span", None),
            P("stream", "span", None),
            P("stream", "span", None),
            P(None, "stream", "span", None),
            P("stream", None),
        ),
        check_vma=False,
    )
```

```python
import functools

import jax
import jax.numpy as jnp
import numpy as np
from jax import lax
from jax.experimental import pallas as pl
from jax.experimental.pallas import tpu as pltpu
from jax.sharding import PartitionSpec as P

SPECIES = 9
SCALARS = 11
adiabatic_gamma = 1.4
courant = 0.5
laminar_diffusivity = 0.05
momentum_thermal_quotient = 0.7
schmidt = 0.7
subgrid_thermal_quotient = 0.9
inject_rate = 5.0
inject_speed = 2.0
heat_capacity = 3.5
tiny_value = 1e-06
reaction_list = (
    ((4, 1), (5, 3)),
    ((5, 0), (4, 3)),
    ((0, 3), (2, 4)),
    ((5, 2), (3, 3)),
    ((0, 9), (4, 4)),
    ((5, 5, 9), (1,)),
    ((5, 4, 9), (3,)),
    ((4, 3, 9), (2,)),
    ((4, 1, 9), (6,)),
    ((6, 4), (0, 1)),
    ((6, 4), (3, 3)),
    ((6, 5), (1, 3)),
    ((6, 3), (2, 1)),
    ((6, 6), (7, 1)),
    ((7, 9), (3, 3)),
    ((7, 4), (2, 3)),
    ((7, 4), (6, 0)),
    ((7, 5), (3, 6)),
    ((7, 3), (6, 2)),
)
log_prefactor = np.array(
    [3.9, 3.2, 3.4, 3.0, 2.0, 6.0, 6.2, 6.5, 5.8, 3.8, 3.6, 3.5, 3.7, 3.1, 2.2, 3.3, 3.4, 3.0, 3.2],
    np.float32,
)
thermal_power_index = np.array(
    [
        0.0,
        0.5,
        0.5,
        1.0,
        -1.0,
        -0.5,
        -1.0,
        -2.0,
        -1.0,
        0.0,
        0.0,
        0.0,
        0.0,
        0.0,
        0.0,
        0.0,
        0.0,
        1.0,
        0.0,
    ],
    np.float32,
)
arrhenius_barrier = np.array(
    [
        1.6,
        0.7,
        0.4,
        1.5,
        2.0,
        0.0,
        0.0,
        0.0,
        0.0,
        0.1,
        0.05,
        0.0,
        0.0,
        0.2,
        1.8,
        0.4,
        0.8,
        0.3,
        0.1,
    ],
    np.float32,
)
molar_weight = np.array([0.125, 2.0, 1.125, 1.0625, 0.0625, 1.0, 2.0625, 2.125, 1.75], np.float32)
formation = np.array([0.0, 0.0, -2.42, 0.39, 2.18, 2.49, 0.12, -1.36, 0.0], np.float32)
pair_list = ((0, 0), (1, 1), (2, 2), (0, 1), (0, 2), (1, 2))


VMEM = pltpu.VMEM


def pair_up(count, start, wrap):
    pairs = []
    for low in range(start, count - 1, 2):
        pairs += [(low, low + 1), (low + 1, low)]
    if wrap and start == 1:
        pairs += [(count - 1, 0), (0, count - 1)]
    return pairs


def flip(count, bit):
    return [(index, index ^ bit) for index in range(count)]


def even_index(axis):
    return lax.rem(lax.axis_index(axis), 2) == 0


def call(body, outs, args, scratch=(), flops=0, name=None, from_hbm=False, to_hbm=False):
    nbytes = sum(int(np.prod(a.shape)) * 4 for a in args) + sum(
        int(np.prod(s)) * 4 for s in outs
    )
    return pl.pallas_call(
        body,
        out_shape=[
            jax.ShapeDtypeStruct(s, jnp.float32) if to_hbm else VMEM(s, jnp.float32) for s in outs
        ],
        in_specs=[pl.BlockSpec(memory_space=pltpu.HBM if from_hbm else VMEM)] * len(args),
        out_specs=[pl.BlockSpec(memory_space=VMEM)] * len(outs),
        scratch_shapes=list(scratch),
        compiler_params=pltpu.CompilerParams(vmem_limit_bytes=8 << 20),
        cost_estimate=pl.CostEstimate(flops=flops, bytes_accessed=nbytes, transcendentals=0),
        name=name,
    )(*[pltpu.with_memory_space_constraint(a, pltpu.HBM if from_hbm else VMEM) for a in args])


def pack_stream(
    hbm_v, hbm_r, hbm_t, hbm_y, send_a, send_b, far_a, vel, dens, temp, spec, done
):
    copies = [
        pltpu.make_async_copy(src, dst, done.at[k])
        for k, (src, dst) in enumerate(
            ((hbm_v, vel), (hbm_t, temp), (hbm_r, dens), (hbm_y, spec))
        )
    ]
    for copy in copies:
        copy.start()
    even = even_index("stream")
    nx = vel.shape[1]
    copies[0].wait()
    for comp in range(3):
        for layer in range(2):
            low = vel[comp, layer]
            high = vel[comp, nx - 2 + layer]
            send_a[2 * comp + layer] = jnp.where(even, high, low)
            send_b[2 * comp + layer] = jnp.where(even, low, high)
    copies[1].wait()
    fastest = None
    for x in range(nx):
        speed = (
            jnp.abs(vel[0, x])
            + jnp.abs(vel[1, x])
            + jnp.abs(vel[2, x])
            + jnp.sqrt(adiabatic_gamma * temp[x])
        )
        fastest = speed if fastest is None else jnp.maximum(fastest, speed)
    send_a[6] = fastest
    copies[2].wait()
    copies[3].wait()
    for field in range(SCALARS):
        ref = dens if field == 0 else temp if field == 1 else spec.at[field - 2]
        low, high = ref[0], ref[nx - 1]
        far_a[field] = jnp.where(even, high, low)
        send_b[6 + field] = jnp.where(even, low, high)


def pack_span(vel, dens, temp, spec, got_a, got_b, near, got_n, send_c, send_d, top):
    even_s = even_index("stream")
    even_p = even_index("span")
    nx, nz = vel.shape[1], vel.shape[2]
    for comp in range(3):
        for x in range(nx + 4):
            if x < 2:
                tile = jnp.where(even_s, got_b[2 * comp + x], got_a[2 * comp + x])
            elif x < nx + 2:
                tile = vel[comp, x - 2]
            else:
                at = 2 * comp + x - nx - 2
                tile = jnp.where(even_s, got_a[at], got_b[at])
            first, last = tile[0:2], tile[nz - 2 : nz]
            row = 2 * (comp * (nx + 4) + x)
            send_c[row : row + 2] = jnp.where(even_p, last, first)
            send_d[row : row + 2] = jnp.where(even_p, first, last)
    top[...] = jnp.maximum(near[...], got_n[...])
    base = 6 * (nx + 4)
    for field in range(SCALARS):
        ref = dens if field == 0 else temp if field == 1 else spec.at[field - 2]
        first, last = ref[:, 0, :], ref[:, nz - 1, :]
        row = base + field * nx
        send_c[row : row + nx] = jnp.where(even_p, last, first)
        send_d[row : row + nx] = jnp.where(even_p, first, last)


def along_y(tile, lane):
    width = tile.shape[-1]
    after = jnp.where(lane == width - 1, 0.0, pltpu.roll(tile, width - 1, 1))
    before = jnp.where(lane == 0, 0.0, pltpu.roll(tile, 1, 1))
    return after, before


def strain_of(grads):
    parts = [
        grads[i][i] if i == j else 0.5 * (grads[i][j] + grads[j][i]) for i, j in pair_list
    ]
    diagonal = parts[0] * parts[0] + parts[1] * parts[1] + parts[2] * parts[2]
    off = parts[3] * parts[3] + parts[4] * parts[4] + parts[5] * parts[5]
    return parts, jnp.sqrt(2.0 * (diagonal + 2.0 * off))


def germano(vel, got_a, got_b, got_c, got_d, near, got_n, red, mag, wide, shear, smooth):
    even_s = even_index("stream")
    even_p = even_index("span")
    nx, nz, ny = vel.shape[1], vel.shape[2], vel.shape[3]
    rows = 2 * nz
    zero = jnp.zeros((nz - 4, ny), jnp.float32)
    for comp in range(3):
        for x in range(nx + 4):
            if x < 2:
                tile = jnp.where(even_s, got_b[2 * comp + x], got_a[2 * comp + x])
            elif x < nx + 2:
                tile = vel[comp, x - 2]
            else:
                at = 2 * comp + x - nx - 2
                tile = jnp.where(even_s, got_a[at], got_b[at])
            row = 2 * (comp * (nx + 4) + x)
            one, two = got_c[row : row + 2], got_d[row : row + 2]
            wide[comp, x, 0:nz] = tile
            wide[comp, x, nz : nz + 2] = jnp.where(even_p, one, two)
            wide[comp, x, nz + 2 : rows - 2] = zero
            wide[comp, x, rows - 2 : rows] = jnp.where(even_p, two, one)
    lane = lax.broadcasted_iota(jnp.int32, (rows, ny), 1)

    def z_after(tile):
        return pltpu.roll(tile, rows - 1, 0)

    def z_before(tile):
        return pltpu.roll(tile, 1, 0)

    def gradients(ref, x, i):
        center = ref[i, x]
        after, before = along_y(center, lane)
        return [
            0.5 * (ref[i, x + 1] - ref[i, x - 1]),
            0.5 * (after - before),
            0.5 * (z_after(center) - z_before(center)),
        ]

    def z_filter(tile):
        return 0.25 * (z_after(tile) + z_before(tile)) + 0.5 * tile

    def x_filter(take):
        return 0.25 * (take(-1) + take(1)) + 0.5 * take(0)

    position = lax.axis_index("stream") * nx
    total = lax.axis_size("stream") * nx

    for x in range(nx + 2):
        keep = None
        if x == 0:
            keep = jnp.where(position > 0, 1.0, 0.0)
        elif x == nx + 1:
            keep = jnp.where(position + nx < total, 1.0, 0.0)
        parts, size = strain_of([gradients(wide, x + 1, i) for i in range(3)])
        if 1 <= x <= nx:
            mag[x - 1] = size[0:nz]
        if keep is not None:
            size = size * keep
        for k in range(6):
            shear[k, x] = size * parts[k]
        for i in range(3):
            value = z_filter(x_filter(lambda d: wide[i, x + 1 + d]))
            smooth[i, x] = value if keep is None else value * keep
    for x in range(nx):
        hat_parts, hat_size = strain_of([gradients(smooth, x + 1, i) for i in range(3)])
        lm = jnp.zeros((rows, ny), jnp.float32)
        mm = jnp.zeros((rows, ny), jnp.float32)
        for k, (i, j) in enumerate(pair_list):
            weight = 1.0 if i == j else 2.0
            product = z_filter(x_filter(lambda d: wide[i, x + 2 + d] * wide[j, x + 2 + d]))
            resolved = product - smooth[i, x + 1] * smooth[j, x + 1]
            model = z_filter(x_filter(lambda d: shear[k, x + 1 + d])) - 4.0 * hat_size * hat_parts[k]
            lm = lm + weight * resolved * model
            mm = mm + weight * model * model
        red[x : x + 1] = jnp.sum(lm[0:nz], axis=0, keepdims=True)
        red[nx + x : nx + x + 1] = jnp.sum(mm[0:nz], axis=0, keepdims=True)
    red[2 * nx : 2 * nx + nz] = jnp.maximum(near[...], got_n[...])


def chemistry(dens, inverse, temp, species):
    over = 1.0 / temp
    root = jnp.sqrt(temp)
    powers = {0.0: None, 0.5: root, 1.0: temp, -1.0: over, -0.5: root * over, -2.0: over * over}
    e05 = jnp.exp(-0.05 * over)
    e15 = jnp.exp(-1.5 * over)
    decay = {0: None, 5: e05, 150: e15}
    decay[10] = e05 * e05
    decay[20] = decay[10] * decay[10]
    decay[30] = decay[20] * decay[10]
    decay[40] = decay[20] * decay[20]
    decay[70] = decay[40] * decay[30]
    decay[80] = decay[40] * decay[40]
    decay[160] = e15 * decay[10]
    decay[180] = e15 * decay[30]
    decay[200] = decay[180] * decay[20]
    conc = [dens * (species[k] * float(1.0 / molar_weight[k])) for k in range(SPECIES)]
    total = conc[0]
    for k in range(1, SPECIES):
        total = total + conc[k]
    conc.append(total)
    products = {}

    def product(ids):
        if len(ids) == 1:
            return conc[ids[0]]
        if ids not in products:
            products[ids] = product(ids[:-1]) * conc[ids[-1]]
        return products[ids]

    produced = [None] * SPECIES
    for number, (reactants, results) in enumerate(reaction_list):
        ordered = tuple(sorted(reactants))
        pace = product(ordered) * float(np.exp(np.float64(log_prefactor[number])))
        power = powers[float(thermal_power_index[number])]
        if power is not None:
            pace = pace * power
        fall = decay[int(round(float(arrhenius_barrier[number]) * 100))]
        if fall is not None:
            pace = pace * fall
        change = {}
        for k in reactants:
            if k < SPECIES:
                change[k] = change.get(k, 0) - 1
        for k in results:
            change[k] = change.get(k, 0) + 1
        for k, times in change.items():
            if times == 0:
                continue
            term = pace if abs(times) == 1 else pace * float(abs(times))
            if produced[k] is None:
                produced[k] = term if times > 0 else -term
            else:
                produced[k] = produced[k] + term if times > 0 else produced[k] - term
    heat = None
    for k in range(SPECIES):
        if formation[k] != 0.0 and produced[k] is not None:
            term = produced[k] * float(-formation[k] / heat_capacity)
            heat = term if heat is None else heat + term
    source = [
        None if produced[k] is None else produced[k] * inverse * float(molar_weight[k])
        for k in range(SPECIES)
    ]
    return source, heat * inverse


def tendencies(
    vel, dens, temp, spec, fuel, got_a, got_b, got_c, got_d, far_a, mag, base, slope
):
    even_s = even_index("stream")
    even_p = even_index("span")
    nx, nz, ny = dens.shape
    lane = lax.broadcasted_iota(jnp.int32, (nz, ny), 1)
    line = lax.broadcasted_iota(jnp.int32, (nz, ny), 0)

    def own(field, x):
        if field < 3:
            return vel[field, x]
        if field == 3:
            return dens[x]
        if field == 4:
            return temp[x]
        return spec[field - 5, x]

    def cell(field, x):
        if 0 <= x < nx:
            return own(field, x)
        if field < 3:
            at = 2 * field + (1 if x < 0 else 0)
            one, two = got_a[at], got_b[at]
        else:
            one, two = far_a[field - 3], got_b[3 + field]
        return jnp.where(even_s, two, one) if x < 0 else jnp.where(even_s, one, two)

    def edges(field, x):
        if field < 3:
            row = 2 * (field * (nx + 4) + x + 2)
            c0, c1 = got_c[row : row + 1], got_c[row + 1 : row + 2]
            d0, d1 = got_d[row : row + 1], got_d[row + 1 : row + 2]
            return jnp.where(even_p, c0, d0), jnp.where(even_p, d1, c1)
        row = 6 * (nx + 4) + (field - 3) * nx + x
        c0, d0 = got_c[row : row + 1], got_d[row : row + 1]
        return jnp.where(even_p, c0, d0), jnp.where(even_p, d0, c0)

    def neighbours(field, x):
        center = own(field, x)
        after, before = along_y(center, lane)
        high, low = edges(field, x)
        up = jnp.where(line == nz - 1, high, pltpu.roll(center, nz - 1, 0))
        down = jnp.where(line == 0, low, pltpu.roll(center, 1, 0))
        return center, cell(field, x + 1), cell(field, x - 1), after, before, up, down

    for x in range(nx):
        v = [neighbours(i, x) for i in range(3)]
        r = neighbours(3, x)
        t = neighbours(4, x)
        half = [0.5 * v[i][0] for i in range(3)]
        inverse = 1.0 / r[0]
        size = mag[x]
        inject = fuel[x].astype(jnp.float32) * inject_rate
        species = [own(5 + k, x) for k in range(SPECIES)]
        source, release = chemistry(r[0], inverse, t[0], species)

        def advect(n):
            return half[0] * (n[1] - n[2]) + half[1] * (n[3] - n[4]) + half[2] * (n[5] - n[6])

        def laplace(n):
            return ((n[1] + n[2]) + (n[3] + n[4])) + ((n[5] + n[6]) - 6.0 * n[0])

        push = [r[m] * t[m] for m in range(1, 7)]
        scale = 0.5 * inverse
        for i in range(3):
            lap = laplace(v[i])
            value = laminar_diffusivity * lap - advect(v[i]) - (push[2 * i] - push[2 * i + 1]) * scale
            if i == 1:
                value = value + inject * (inject_speed - v[1][0])
            base[i, x] = value
            slope[i, x] = size * lap
        flux = (
            (r[1] * v[0][1] - r[2] * v[0][2])
            + (r[3] * v[1][3] - r[4] * v[1][4])
            + (r[5] * v[2][5] - r[6] * v[2][6])
        )
        base[3, x] = -0.5 * flux
        thin = size * (1.0 / subgrid_thermal_quotient)
        lap = laplace(t)
        base[4, x] = (laminar_diffusivity / momentum_thermal_quotient) * lap - advect(t) + release
        slope[3, x] = thin * lap
        for k in range(SPECIES):
            n = neighbours(5 + k, x)
            lap = laplace(n)
            value = (laminar_diffusivity / schmidt) * lap - advect(n)
            if source[k] is not None:
                value = value + source[k]
            if k == 0:
                value = value + inject * (1.0 - n[0])
            base[5 + k, x] = value
            slope[4 + k, x] = thin * lap


def finish(
    total_z, vel, dens, temp, spec, wall, base, slope, r0, r1, r2, r3, out_v, out_r, out_t, out_y, out_c
):
    nx = dens.shape[0]
    lm = (r0[0:nx] + r1[0:nx]) + (r2[0:nx] + r3[0:nx])
    mm = (r0[nx : 2 * nx] + r1[nx : 2 * nx]) + (r2[nx : 2 * nx] + r3[nx : 2 * nx])
    coef = jnp.maximum(0.5 * (lm / total_z) / (mm / total_z + tiny_value), 0.0)
    out_c[...] = coef
    top = jnp.maximum(
        jnp.maximum(r0[2 * nx :], r1[2 * nx :]), jnp.maximum(r2[2 * nx :], r3[2 * nx :])
    )
    step = courant / jnp.max(jnp.max(top, axis=0, keepdims=True), axis=1, keepdims=True)
    gain = coef * step
    for x in range(nx):
        g = gain[x : x + 1]
        open_cell = 1.0 - wall[x].astype(jnp.float32)
        for i in range(3):
            out_v[i, x] = open_cell * (vel[i, x] + step * base[i, x] + g * slope[i, x])
        out_r[x] = dens[x] + step * base[3, x]
        out_t[x] = temp[x] + step * base[4, x] + g * slope[3, x]
        for k in range(SPECIES):
            out_y[k, x] = spec[k, x] + step * base[5 + k, x] + g * slope[4 + k, x]


def per_device(vel, dens, temp, spec, wall, fuel):
    nx, nz, ny = dens.shape
    n_stream = lax.axis_size("stream")
    n_span = lax.axis_size("span")
    send_a, send_b, send_far, vel, dens, temp, spec = call(
        pack_stream,
        [(7, nz, ny), (6 + SCALARS, nz, ny), (SCALARS, nz, ny)]
        + [vel.shape, dens.shape, temp.shape, spec.shape],
        (vel, dens, temp, spec),
        scratch=[pltpu.SemaphoreType.DMA((4,))],
        name="pack_stream",
        from_hbm=True,
    )
    far_a = lax.ppermute(send_far, "stream", pair_up(n_stream, 0, False))
    got_a = lax.ppermute(send_a, "stream", pair_up(n_stream, 0, False))
    got_b = lax.ppermute(send_b, "stream", pair_up(n_stream, 1, False))
    near = jnp.maximum(send_a[6], got_a[6])
    got_n = lax.ppermute(near, "stream", flip(n_stream, 2))
    rows = 6 * (nx + 4) + SCALARS * nx
    send_c, send_d, near = call(
        pack_span,
        [(rows, ny), (rows, ny), (nz, ny)],
        (vel, dens, temp, spec, got_a, got_b, near, got_n),
        name="pack_span",
    )
    got_c = lax.ppermute(send_c, "span", pair_up(n_span, 0, True))
    got_d = lax.ppermute(send_d, "span", pair_up(n_span, 1, True))
    bit = 4
    while bit * 2 < n_stream:
        near = jnp.maximum(near, lax.ppermute(near, "stream", flip(n_stream, bit)))
        bit *= 2
    got_n = lax.ppermute(near, "stream", flip(n_stream, bit))
    red, mag = call(
        germano,
        [(2 * nx + nz, ny), (nx, nz, ny)],
        (vel, got_a, got_b, got_c, got_d, near, got_n),
        scratch=[
            VMEM((3, nx + 4, 2 * nz, ny), jnp.float32),
            VMEM((6, nx + 2, 2 * nz, ny), jnp.float32),
            VMEM((3, nx + 2, 2 * nz, ny), jnp.float32),
        ],
        name="germano",
        flops=1000000000,
    )
    base, slope = call(
        tendencies,
        [(5 + SPECIES, nx, nz, ny), (4 + SPECIES, nx, nz, ny)],
        (vel, dens, temp, spec, fuel, got_a, got_b, got_c, got_d, far_a, mag),
        name="tendencies",
    )
    bit = 1
    while bit * 4 < n_span:
        others = [lax.ppermute(red, "span", flip(n_span, bit * m)) for m in (1, 2, 3)]
        low = (red[: 2 * nx] + others[0][: 2 * nx]) + (others[1][: 2 * nx] + others[2][: 2 * nx])
        high = jnp.maximum(
            jnp.maximum(red[2 * nx :], others[0][2 * nx :]),
            jnp.maximum(others[1][2 * nx :], others[2][2 * nx :]),
        )
        red = jnp.concatenate([low, high], axis=0)
        bit *= 4
    others = [lax.ppermute(red, "span", flip(n_span, bit * m)) for m in (1, 3, 2)]
    return tuple(
        call(
            functools.partial(finish, float(nz * n_span)),
            [vel.shape, dens.shape, dens.shape, spec.shape, (nx, ny)],
            (vel, dens, temp, spec, wall, base, slope, red, *others),
            name="finish",
            to_hbm=True,
        )
    )


def solution(mesh):
    return jax.shard_map(
        per_device,
        mesh=mesh,
        in_specs=(
            P(None, "stream", "span", None),
            P("stream", "span", None),
            P("stream", "span", None),
            P(None, "stream", "span", None),
            P("stream", "span", None),
            P("stream", "span", None),
        ),
        out_specs=(
            P(None, "stream", "span", None),
            P("stream", "span", None),
            P("stream", "span", None),
            P(None, "stream", "span", None),
            P("stream", None),
        ),
        check_vma=False,
    )
```

```python
import functools

import jax
import jax.numpy as jnp
import numpy as np
from jax import lax
from jax.experimental import pallas as pl
from jax.experimental.pallas import tpu as pltpu
from jax.sharding import PartitionSpec as P

SPECIES = 9
SCALARS = 11
adiabatic_gamma = 1.4
courant = 0.5
laminar_diffusivity = 0.05
momentum_thermal_quotient = 0.7
schmidt = 0.7
subgrid_thermal_quotient = 0.9
inject_rate = 5.0
inject_speed = 2.0
heat_capacity = 3.5
tiny_value = 1e-06
reaction_list = (
    ((4, 1), (5, 3)),
    ((5, 0), (4, 3)),
    ((0, 3), (2, 4)),
    ((5, 2), (3, 3)),
    ((0, 9), (4, 4)),
    ((5, 5, 9), (1,)),
    ((5, 4, 9), (3,)),
    ((4, 3, 9), (2,)),
    ((4, 1, 9), (6,)),
    ((6, 4), (0, 1)),
    ((6, 4), (3, 3)),
    ((6, 5), (1, 3)),
    ((6, 3), (2, 1)),
    ((6, 6), (7, 1)),
    ((7, 9), (3, 3)),
    ((7, 4), (2, 3)),
    ((7, 4), (6, 0)),
    ((7, 5), (3, 6)),
    ((7, 3), (6, 2)),
)
log_prefactor = np.array(
    [3.9, 3.2, 3.4, 3.0, 2.0, 6.0, 6.2, 6.5, 5.8, 3.8, 3.6, 3.5, 3.7, 3.1, 2.2, 3.3, 3.4, 3.0, 3.2],
    np.float32,
)
thermal_power_index = np.array(
    [
        0.0,
        0.5,
        0.5,
        1.0,
        -1.0,
        -0.5,
        -1.0,
        -2.0,
        -1.0,
        0.0,
        0.0,
        0.0,
        0.0,
        0.0,
        0.0,
        0.0,
        0.0,
        1.0,
        0.0,
    ],
    np.float32,
)
arrhenius_barrier = np.array(
    [
        1.6,
        0.7,
        0.4,
        1.5,
        2.0,
        0.0,
        0.0,
        0.0,
        0.0,
        0.1,
        0.05,
        0.0,
        0.0,
        0.2,
        1.8,
        0.4,
        0.8,
        0.3,
        0.1,
    ],
    np.float32,
)
molar_weight = np.array([0.125, 2.0, 1.125, 1.0625, 0.0625, 1.0, 2.0625, 2.125, 1.75], np.float32)
formation = np.array([0.0, 0.0, -2.42, 0.39, 2.18, 2.49, 0.12, -1.36, 0.0], np.float32)
pair_list = ((0, 0), (1, 1), (2, 2), (0, 1), (0, 2), (1, 2))


VMEM = pltpu.VMEM


def pair_up(count, start, wrap):
    pairs = []
    for low in range(start, count - 1, 2):
        pairs += [(low, low + 1), (low + 1, low)]
    if wrap and start == 1:
        pairs += [(count - 1, 0), (0, count - 1)]
    return pairs


def flip(count, bit):
    return [(index, index ^ bit) for index in range(count)]


def even_index(axis):
    return lax.rem(lax.axis_index(axis), 2) == 0


def call(body, outs, args, scratch=(), flops=0, name=None, from_hbm=False, to_hbm=False):
    nbytes = sum(int(np.prod(a.shape)) * 4 for a in args) + sum(
        int(np.prod(s)) * 4 for s in outs
    )
    return pl.pallas_call(
        body,
        out_shape=[
            jax.ShapeDtypeStruct(s, jnp.float32) if to_hbm else VMEM(s, jnp.float32) for s in outs
        ],
        in_specs=[pl.BlockSpec(memory_space=pltpu.HBM if from_hbm else VMEM)] * len(args),
        out_specs=[pl.BlockSpec(memory_space=VMEM)] * len(outs),
        scratch_shapes=list(scratch),
        compiler_params=pltpu.CompilerParams(vmem_limit_bytes=8 << 20),
        cost_estimate=pl.CostEstimate(flops=flops, bytes_accessed=nbytes, transcendentals=0),
        name=name,
    )(*[pltpu.with_memory_space_constraint(a, pltpu.HBM if from_hbm else VMEM) for a in args])


def pack_stream(hbm_v, hbm_r, hbm_t, hbm_y, send_a, send_b, vel, temp, done):
    even = even_index("stream")
    nx = vel.shape[1]
    edge = jnp.where(even, 0, nx - 1)
    copies = [
        pltpu.make_async_copy(src, dst, done.at[k])
        for k, (src, dst) in enumerate(
            (
                (hbm_v, vel),
                (hbm_t, temp),
                (hbm_y.at[:, edge], send_b.at[pl.ds(8, SPECIES)]),
                (hbm_r.at[pl.ds(edge, 1)], send_b.at[pl.ds(6, 1)]),
            )
        )
    ]
    for copy in copies:
        copy.start()
    copies[0].wait()
    for comp in range(3):
        for layer in range(2):
            low = vel[comp, layer]
            high = vel[comp, nx - 2 + layer]
            send_a[2 * comp + layer] = jnp.where(even, high, low)
            send_b[2 * comp + layer] = jnp.where(even, low, high)
    copies[1].wait()
    send_b[7] = jnp.where(even, temp[0], temp[nx - 1])
    fastest = None
    for x in range(nx):
        speed = (
            jnp.abs(vel[0, x])
            + jnp.abs(vel[1, x])
            + jnp.abs(vel[2, x])
            + jnp.sqrt(adiabatic_gamma * temp[x])
        )
        fastest = speed if fastest is None else jnp.maximum(fastest, speed)
    send_a[6] = fastest
    copies[2].wait()
    copies[3].wait()


def pack_span(vel, dens, temp, spec, got_a, got_b, near, got_n, send_c, send_d, top):
    even_s = even_index("stream")
    even_p = even_index("span")
    nx, nz = vel.shape[1], vel.shape[2]
    for comp in range(3):
        for x in range(nx + 4):
            if x < 2:
                tile = jnp.where(even_s, got_b[2 * comp + x], got_a[2 * comp + x])
            elif x < nx + 2:
                tile = vel[comp, x - 2]
            else:
                at = 2 * comp + x - nx - 2
                tile = jnp.where(even_s, got_a[at], got_b[at])
            first, last = tile[0:2], tile[nz - 2 : nz]
            row = 2 * (comp * (nx + 4) + x)
            send_c[row : row + 2] = jnp.where(even_p, last, first)
            send_d[row : row + 2] = jnp.where(even_p, first, last)
    top[...] = jnp.maximum(near[...], got_n[...])
    base = 6 * (nx + 4)
    for field in range(SCALARS):
        ref = dens if field == 0 else temp if field == 1 else spec.at[field - 2]
        row = base + field * nx
        send_c[row : row + nx] = jnp.where(even_p, ref[:, nz - 1, :], ref[:, 0, :])


def pack_far(dens, temp, spec, far_a, far_d):
    even_s = even_index("stream")
    even_p = even_index("span")
    nx, nz = dens.shape[0], dens.shape[1]
    for field in range(SCALARS):
        ref = dens if field == 0 else temp if field == 1 else spec.at[field - 2]
        far_a[field] = jnp.where(even_s, ref[nx - 1], ref[0])
        row = field * nx
        far_d[row : row + nx] = jnp.where(even_p, ref[:, 0, :], ref[:, nz - 1, :])
    for row in range(SCALARS * nx, far_d.shape[0], nx):
        far_d[row : row + nx] = far_d[0:nx]


def along_y(tile, lane):
    width = tile.shape[-1]
    after = jnp.where(lane == width - 1, 0.0, pltpu.roll(tile, width - 1, 1))
    before = jnp.where(lane == 0, 0.0, pltpu.roll(tile, 1, 1))
    return after, before


def differences(ref, x, i, shift, lane):
    center = ref[i, x]
    after, before = along_y(center, lane)
    return [ref[i, x + 1] - ref[i, x - 1], after - before, shift(center, -1) - shift(center, 1)]


def strain_of(diffs):
    parts = [diffs[i][i] if i == j else diffs[i][j] + diffs[j][i] for i, j in pair_list]
    diagonal = parts[0] * parts[0] + parts[1] * parts[1] + parts[2] * parts[2]
    off = parts[3] * parts[3] + parts[4] * parts[4] + parts[5] * parts[5]
    return parts, jnp.sqrt(0.5 * diagonal + 0.25 * off)


def germano(vel, got_a, got_b, got_c, got_d, far_d, red, mag, wide, shear, smooth, square):
    even_s = even_index("stream")
    even_p = even_index("span")
    nx, nz, ny = vel.shape[1], vel.shape[2], vel.shape[3]
    rows = 2 * nz
    zero = jnp.zeros((nz - 4, ny), jnp.float32)
    for comp in range(3):
        for x in range(nx + 4):
            if x < 2:
                tile = jnp.where(even_s, got_b[2 * comp + x], got_a[2 * comp + x])
            elif x < nx + 2:
                tile = vel[comp, x - 2]
            else:
                at = 2 * comp + x - nx - 2
                tile = jnp.where(even_s, got_a[at], got_b[at])
            row = 2 * (comp * (nx + 4) + x)
            one, two = got_c[row : row + 2], got_d[row : row + 2]
            wide[comp, x, 0:nz] = tile
            wide[comp, x, nz : nz + 2] = jnp.where(even_p, one, two)
            wide[comp, x, nz + 2 : rows - 2] = zero
            wide[comp, x, rows - 2 : rows] = jnp.where(even_p, two, one)
    lane = lax.broadcasted_iota(jnp.int32, (rows, ny), 1)

    def shift(tile, by):
        return pltpu.roll(tile, by % rows, 0)

    def z_sum(tile):
        pair = tile + shift(tile, -1)
        return pair + shift(pair, 1)

    position = lax.axis_index("stream") * nx
    total = lax.axis_size("stream") * nx

    last = None
    for x in range(nx + 4):
        here = [wide[i, x] for i in range(3)]
        products = [here[i] * here[j] for i, j in pair_list]
        if last is not None:
            for k in range(6):
                square[k, x - 1] = products[k] + last[k]
        last = products

    for x in range(nx + 2):
        keep = 1.0
        if x == 0:
            keep = jnp.where(position > 0, 1.0, 0.0)
        elif x == nx + 1:
            keep = jnp.where(position + nx < total, 1.0, 0.0)
        parts, size = strain_of([differences(wide, x + 1, i, shift, lane) for i in range(3)])
        if 1 <= x <= nx:
            mag[x - 1] = size[0:nz]
        straight = size * (keep * 0.03125)
        crossed = size * (keep * 0.015625)
        for k, (i, j) in enumerate(pair_list):
            shear[k, x] = (straight if i == j else crossed) * parts[k]
        for i in range(3):
            value = (wide[i, x] + wide[i, x + 2]) + 2.0 * wide[i, x + 1]
            smooth[i, x] = z_sum(value) * (keep * 0.0625)
    for x in range(nx):
        hat_parts, hat_size = strain_of(
            [differences(smooth, x + 1, i, shift, lane) for i in range(3)]
        )
        straight = 2.0 * hat_size
        lm = [None, None]
        mm = [None, None]
        for k, (i, j) in enumerate(pair_list):
            kind = 0 if i == j else 1
            product = z_sum(square[k, x + 1] + square[k, x + 2])
            resolved = 0.0625 * product - smooth[i, x + 1] * smooth[j, x + 1]
            filtered = z_sum((shear[k, x] + shear[k, x + 2]) + 2.0 * shear[k, x + 1])
            model = filtered - (straight if i == j else hat_size) * hat_parts[k]
            lm[kind] = resolved * model if lm[kind] is None else lm[kind] + resolved * model
            mm[kind] = model * model if mm[kind] is None else mm[kind] + model * model
        lm = (lm[0] + 2.0 * lm[1])[0:nz]
        mm = (mm[0] + 2.0 * mm[1])[0:nz]
        lm = jnp.sum(lm, axis=0, keepdims=True)
        mm = jnp.sum(mm, axis=0, keepdims=True)
        half = ny // 2
        red[x : x + 1] = lm[:, :half]
        red[nx + x : nx + x + 1] = lm[:, half:]
        red[2 * nx + x : 2 * nx + x + 1] = mm[:, :half]
        red[3 * nx + x : 3 * nx + x + 1] = mm[:, half:]


def join(red, near, got_n, out):
    sums, half = red.shape
    out[:sums] = red[...]
    top = jnp.maximum(near[...], got_n[...])
    out[sums:] = jnp.maximum(top[:, :half], top[:, half:])


def chemistry(dens, inverse, temp, species):
    over = 1.0 / temp
    root = jnp.sqrt(temp)
    powers = {0.0: None, 0.5: root, 1.0: temp, -1.0: over, -0.5: root * over, -2.0: over * over}
    e05 = jnp.exp(-0.05 * over)
    e15 = jnp.exp(-1.5 * over)
    decay = {0: None, 5: e05, 150: e15}
    decay[10] = e05 * e05
    decay[20] = decay[10] * decay[10]
    decay[30] = decay[20] * decay[10]
    decay[40] = decay[20] * decay[20]
    decay[70] = decay[40] * decay[30]
    decay[80] = decay[40] * decay[40]
    decay[160] = e15 * decay[10]
    decay[180] = e15 * decay[30]
    decay[200] = decay[180] * decay[20]
    conc = [dens * (species[k] * float(1.0 / molar_weight[k])) for k in range(SPECIES)]
    total = conc[0]
    for k in range(1, SPECIES):
        total = total + conc[k]
    conc.append(total)
    products = {}

    def product(ids):
        if len(ids) == 1:
            return conc[ids[0]]
        if ids not in products:
            products[ids] = product(ids[:-1]) * conc[ids[-1]]
        return products[ids]

    produced = [None] * SPECIES
    for number, (reactants, results) in enumerate(reaction_list):
        ordered = tuple(sorted(reactants))
        pace = product(ordered) * float(np.exp(np.float64(log_prefactor[number])))
        power = powers[float(thermal_power_index[number])]
        if power is not None:
            pace = pace * power
        fall = decay[int(round(float(arrhenius_barrier[number]) * 100))]
        if fall is not None:
            pace = pace * fall
        change = {}
        for k in reactants:
            if k < SPECIES:
                change[k] = change.get(k, 0) - 1
        for k in results:
            change[k] = change.get(k, 0) + 1
        for k, times in change.items():
            if times == 0:
                continue
            term = pace if abs(times) == 1 else pace * float(abs(times))
            if produced[k] is None:
                produced[k] = term if times > 0 else -term
            else:
                produced[k] = produced[k] + term if times > 0 else produced[k] - term
    heat = None
    for k in range(SPECIES):
        if formation[k] != 0.0 and produced[k] is not None:
            term = produced[k] * float(-formation[k] / heat_capacity)
            heat = term if heat is None else heat + term
    source = [
        None if produced[k] is None else produced[k] * inverse * float(molar_weight[k])
        for k in range(SPECIES)
    ]
    return source, heat * inverse


def tendencies(
    vel, dens, temp, spec, fuel, got_a, got_b, got_c, got_d, far_a, far_d, mag, base, slope
):
    even_s = even_index("stream")
    even_p = even_index("span")
    nx, nz, ny = dens.shape
    lane = lax.broadcasted_iota(jnp.int32, (nz, ny), 1)
    line = lax.broadcasted_iota(jnp.int32, (nz, ny), 0)

    def own(field, x):
        if field < 3:
            return vel[field, x]
        if field == 3:
            return dens[x]
        if field == 4:
            return temp[x]
        return spec[field - 5, x]

    def cell(field, x):
        if 0 <= x < nx:
            return own(field, x)
        if field < 3:
            at = 2 * field + (1 if x < 0 else 0)
            one, two = got_a[at], got_b[at]
        else:
            one, two = far_a[field - 3], got_b[3 + field]
        return jnp.where(even_s, two, one) if x < 0 else jnp.where(even_s, one, two)

    def edges(field, x):
        if field < 3:
            row = 2 * (field * (nx + 4) + x + 2)
            c0, c1 = got_c[row : row + 1], got_c[row + 1 : row + 2]
            d0, d1 = got_d[row : row + 1], got_d[row + 1 : row + 2]
            return jnp.where(even_p, c0, d0), jnp.where(even_p, d1, c1)
        line_at = (field - 3) * nx + x
        row = 6 * (nx + 4) + line_at
        c0, d0 = got_c[row : row + 1], far_d[line_at : line_at + 1]
        return jnp.where(even_p, c0, d0), jnp.where(even_p, d0, c0)

    def neighbours(field, x):
        center = own(field, x)
        after, before = along_y(center, lane)
        high, low = edges(field, x)
        up = jnp.where(line == nz - 1, high, pltpu.roll(center, nz - 1, 0))
        down = jnp.where(line == 0, low, pltpu.roll(center, 1, 0))
        return center, cell(field, x + 1), cell(field, x - 1), after, before, up, down

    for x in range(nx):
        v = [neighbours(i, x) for i in range(3)]
        r = neighbours(3, x)
        t = neighbours(4, x)
        half = [0.5 * v[i][0] for i in range(3)]
        inverse = 1.0 / r[0]
        size = mag[x]
        inject = fuel[x].astype(jnp.float32) * inject_rate
        species = [own(5 + k, x) for k in range(SPECIES)]
        source, release = chemistry(r[0], inverse, t[0], species)

        def advect(n):
            return half[0] * (n[1] - n[2]) + half[1] * (n[3] - n[4]) + half[2] * (n[5] - n[6])

        def laplace(n):
            return ((n[1] + n[2]) + (n[3] + n[4])) + ((n[5] + n[6]) - 6.0 * n[0])

        push = [r[m] * t[m] for m in range(1, 7)]
        scale = 0.5 * inverse
        for i in range(3):
            lap = laplace(v[i])
            value = laminar_diffusivity * lap - advect(v[i]) - (push[2 * i] - push[2 * i + 1]) * scale
            if i == 1:
                value = value + inject * (inject_speed - v[1][0])
            base[i, x] = value
            slope[i, x] = size * lap
        flux = (
            (r[1] * v[0][1] - r[2] * v[0][2])
            + (r[3] * v[1][3] - r[4] * v[1][4])
            + (r[5] * v[2][5] - r[6] * v[2][6])
        )
        base[3, x] = -0.5 * flux
        thin = size * (1.0 / subgrid_thermal_quotient)
        lap = laplace(t)
        base[4, x] = (laminar_diffusivity / momentum_thermal_quotient) * lap - advect(t) + release
        slope[3, x] = thin * lap
        for k in range(SPECIES):
            n = neighbours(5 + k, x)
            lap = laplace(n)
            value = (laminar_diffusivity / schmidt) * lap - advect(n)
            if source[k] is not None:
                value = value + source[k]
            if k == 0:
                value = value + inject * (1.0 - n[0])
            base[5 + k, x] = value
            slope[4 + k, x] = thin * lap


def finish(
    total_z, vel, dens, temp, spec, wall, base, slope, r0, r1, r2, r3, out_v, out_r, out_t, out_y, out_c
):
    nx = dens.shape[0]
    sums = (r0[: 4 * nx] + r1[: 4 * nx]) + (r2[: 4 * nx] + r3[: 4 * nx])
    lm = jnp.concatenate([sums[:nx], sums[nx : 2 * nx]], axis=1)
    mm = jnp.concatenate([sums[2 * nx : 3 * nx], sums[3 * nx :]], axis=1)
    coef = jnp.maximum(0.5 * (lm / total_z) / (mm / total_z + tiny_value), 0.0)
    out_c[...] = coef
    top = jnp.maximum(
        jnp.maximum(r0[4 * nx :], r1[4 * nx :]), jnp.maximum(r2[4 * nx :], r3[4 * nx :])
    )
    step = courant / jnp.max(jnp.max(top, axis=0, keepdims=True), axis=1, keepdims=True)
    gain = coef * step
    for x in range(nx):
        g = gain[x : x + 1]
        open_cell = 1.0 - wall[x].astype(jnp.float32)
        for i in range(3):
            out_v[i, x] = open_cell * (vel[i, x] + step * base[i, x] + g * slope[i, x])
        out_r[x] = dens[x] + step * base[3, x]
        out_t[x] = temp[x] + step * base[4, x] + g * slope[3, x]
        for k in range(SPECIES):
            out_y[k, x] = spec[k, x] + step * base[5 + k, x] + g * slope[4 + k, x]


def per_device(vel, dens, temp, spec, wall, fuel):
    nx, nz, ny = dens.shape
    n_stream = lax.axis_size("stream")
    n_span = lax.axis_size("span")
    send_a, send_b, vel, temp = call(
        pack_stream,
        [(7, nz, ny), (6 + SCALARS, nz, ny), vel.shape, temp.shape],
        (vel, dens, temp, spec),
        scratch=[pltpu.SemaphoreType.DMA((4,))],
        name="pack_stream",
        from_hbm=True,
    )
    got_a = lax.ppermute(send_a, "stream", pair_up(n_stream, 0, False))
    got_b = lax.ppermute(send_b, "stream", pair_up(n_stream, 1, False))
    send_far, send_fd = call(
        pack_far,
        [(SCALARS, nz, ny), (6 * (nx + 4) + SCALARS * nx + nx, ny)],
        (dens, temp, spec),
        name="pack_far",
    )
    far_d = lax.ppermute(send_fd, "span", pair_up(n_span, 1, True))
    near = jnp.maximum(send_a[6], got_a[6])
    got_n = lax.ppermute(near, "stream", flip(n_stream, 2))
    rows = 6 * (nx + 4) + SCALARS * nx
    send_c, send_d, near = call(
        pack_span,
        [(rows, ny), (6 * (nx + 4), ny), (nz, ny)],
        (vel, dens, temp, spec, got_a, got_b, near, got_n),
        name="pack_span",
    )
    far_a = lax.ppermute(send_far, "stream", pair_up(n_stream, 0, False))
    got_c = lax.ppermute(send_c, "span", pair_up(n_span, 0, True))
    got_d = lax.ppermute(send_d, "span", pair_up(n_span, 1, True))
    bit = 4
    while bit * 2 < n_stream:
        near = jnp.maximum(near, lax.ppermute(near, "stream", flip(n_stream, bit)))
        bit *= 2
    got_n = lax.ppermute(near, "stream", flip(n_stream, bit))
    red, mag = call(
        germano,
        [(4 * nx, ny // 2), (nx, nz, ny)],
        (vel, got_a, got_b, got_c, got_d, far_d),
        scratch=[
            VMEM((3, nx + 4, 2 * nz, ny), jnp.float32),
            VMEM((6, nx + 2, 2 * nz, ny), jnp.float32),
            VMEM((3, nx + 2, 2 * nz, ny), jnp.float32),
            VMEM((6, nx + 3, 2 * nz, ny), jnp.float32),
        ],
        name="germano",
        flops=1000000000,
    )
    base, slope = call(
        tendencies,
        [(5 + SPECIES, nx, nz, ny), (4 + SPECIES, nx, nz, ny)],
        (vel, dens, temp, spec, fuel, got_a, got_b, got_c, got_d, far_a, far_d, mag),
        name="tendencies",
    )
    (red,) = call(join, [(4 * nx + nz, ny // 2)], (red, near, got_n), name="join")
    bit = 1
    while bit * 4 < n_span:
        others = [lax.ppermute(red, "span", flip(n_span, bit * m)) for m in (1, 2, 3)]
        low = (red[: 4 * nx] + others[0][: 4 * nx]) + (others[1][: 4 * nx] + others[2][: 4 * nx])
        high = jnp.maximum(
            jnp.maximum(red[4 * nx :], others[0][4 * nx :]),
            jnp.maximum(others[1][4 * nx :], others[2][4 * nx :]),
        )
        red = jnp.concatenate([low, high], axis=0)
        bit *= 4
    others = [lax.ppermute(red, "span", flip(n_span, bit * m)) for m in (1, 3, 2)]
    return tuple(
        call(
            functools.partial(finish, float(nz * n_span)),
            [vel.shape, dens.shape, dens.shape, spec.shape, (nx, ny)],
            (vel, dens, temp, spec, wall, base, slope, red, *others),
            name="finish",
            to_hbm=True,
        )
    )


def solution(mesh):
    return jax.shard_map(
        per_device,
        mesh=mesh,
        in_specs=(
            P(None, "stream", "span", None),
            P("stream", "span", None),
            P("stream", "span", None),
            P(None, "stream", "span", None),
            P("stream", "span", None),
            P("stream", "span", None),
        ),
        out_specs=(
            P(None, "stream", "span", None),
            P("stream", "span", None),
            P("stream", "span", None),
            P(None, "stream", "span", None),
            P("stream", None),
        ),
        check_vma=False,
    )
```

```python
import functools

import jax
import jax.numpy as jnp
import numpy as np
from jax import lax
from jax.experimental import pallas as pl
from jax.experimental.pallas import tpu as pltpu
from jax.sharding import PartitionSpec as P

SPECIES = 9
SCALARS = 11
adiabatic_gamma = 1.4
courant = 0.5
laminar_diffusivity = 0.05
momentum_thermal_quotient = 0.7
schmidt = 0.7
subgrid_thermal_quotient = 0.9
inject_rate = 5.0
inject_speed = 2.0
heat_capacity = 3.5
tiny_value = 1e-06
reaction_list = (
    ((4, 1), (5, 3)),
    ((5, 0), (4, 3)),
    ((0, 3), (2, 4)),
    ((5, 2), (3, 3)),
    ((0, 9), (4, 4)),
    ((5, 5, 9), (1,)),
    ((5, 4, 9), (3,)),
    ((4, 3, 9), (2,)),
    ((4, 1, 9), (6,)),
    ((6, 4), (0, 1)),
    ((6, 4), (3, 3)),
    ((6, 5), (1, 3)),
    ((6, 3), (2, 1)),
    ((6, 6), (7, 1)),
    ((7, 9), (3, 3)),
    ((7, 4), (2, 3)),
    ((7, 4), (6, 0)),
    ((7, 5), (3, 6)),
    ((7, 3), (6, 2)),
)
log_prefactor = np.array(
    [3.9, 3.2, 3.4, 3.0, 2.0, 6.0, 6.2, 6.5, 5.8, 3.8, 3.6, 3.5, 3.7, 3.1, 2.2, 3.3, 3.4, 3.0, 3.2],
    np.float32,
)
thermal_power_index = np.array(
    [
        0.0,
        0.5,
        0.5,
        1.0,
        -1.0,
        -0.5,
        -1.0,
        -2.0,
        -1.0,
        0.0,
        0.0,
        0.0,
        0.0,
        0.0,
        0.0,
        0.0,
        0.0,
        1.0,
        0.0,
    ],
    np.float32,
)
arrhenius_barrier = np.array(
    [
        1.6,
        0.7,
        0.4,
        1.5,
        2.0,
        0.0,
        0.0,
        0.0,
        0.0,
        0.1,
        0.05,
        0.0,
        0.0,
        0.2,
        1.8,
        0.4,
        0.8,
        0.3,
        0.1,
    ],
    np.float32,
)
molar_weight = np.array([0.125, 2.0, 1.125, 1.0625, 0.0625, 1.0, 2.0625, 2.125, 1.75], np.float32)
formation = np.array([0.0, 0.0, -2.42, 0.39, 2.18, 2.49, 0.12, -1.36, 0.0], np.float32)
pair_list = ((0, 0), (1, 1), (2, 2), (0, 1), (0, 2), (1, 2))


VMEM = pltpu.VMEM


def pair_up(count, start, wrap):
    pairs = []
    for low in range(start, count - 1, 2):
        pairs += [(low, low + 1), (low + 1, low)]
    if wrap and start == 1:
        pairs += [(count - 1, 0), (0, count - 1)]
    return pairs


def flip(count, bit):
    return [(index, index ^ bit) for index in range(count)]


def even_index(axis):
    return lax.rem(lax.axis_index(axis), 2) == 0


def call(body, outs, args, scratch=(), flops=0, name=None, from_hbm=False, to_hbm=False):
    nbytes = sum(int(np.prod(a.shape)) * 4 for a in args) + sum(
        int(np.prod(s)) * 4 for s in outs
    )
    return pl.pallas_call(
        body,
        out_shape=[
            jax.ShapeDtypeStruct(s, jnp.float32) if to_hbm else VMEM(s, jnp.float32) for s in outs
        ],
        in_specs=[pl.BlockSpec(memory_space=pltpu.HBM if from_hbm else VMEM)] * len(args),
        out_specs=[pl.BlockSpec(memory_space=VMEM)] * len(outs),
        scratch_shapes=list(scratch),
        compiler_params=pltpu.CompilerParams(vmem_limit_bytes=8 << 20),
        cost_estimate=pl.CostEstimate(flops=flops, bytes_accessed=nbytes, transcendentals=0),
        name=name,
    )(*[pltpu.with_memory_space_constraint(a, pltpu.HBM if from_hbm else VMEM) for a in args])


def pack_stream(hbm_v, hbm_r, hbm_t, hbm_y, send_a, send_b, vel, temp, done):
    even = even_index("stream")
    nx = vel.shape[1]
    edge = jnp.where(even, 0, nx - 1)
    copies = [
        pltpu.make_async_copy(src, dst, done.at[k])
        for k, (src, dst) in enumerate(
            (
                (hbm_v, vel),
                (hbm_t, temp),
                (hbm_y.at[:, edge], send_b.at[pl.ds(8, SPECIES)]),
                (hbm_r.at[pl.ds(edge, 1)], send_b.at[pl.ds(6, 1)]),
            )
        )
    ]
    for copy in copies:
        copy.start()
    copies[0].wait()
    for comp in range(3):
        for layer in range(2):
            low = vel[comp, layer]
            high = vel[comp, nx - 2 + layer]
            send_a[2 * comp + layer] = jnp.where(even, high, low)
            send_b[2 * comp + layer] = jnp.where(even, low, high)
    copies[1].wait()
    send_b[7] = jnp.where(even, temp[0], temp[nx - 1])
    fastest = None
    for x in range(nx):
        speed = (
            jnp.abs(vel[0, x])
            + jnp.abs(vel[1, x])
            + jnp.abs(vel[2, x])
            + jnp.sqrt(adiabatic_gamma * temp[x])
        )
        fastest = speed if fastest is None else jnp.maximum(fastest, speed)
    send_a[6] = fastest
    copies[2].wait()
    copies[3].wait()


def pack_span(vel, dens, temp, spec, got_a, got_b, near, got_n, send_c, send_d, top):
    even_s = even_index("stream")
    even_p = even_index("span")
    nx, nz = vel.shape[1], vel.shape[2]
    for comp in range(3):
        for x in range(nx + 4):
            if x < 2:
                tile = jnp.where(even_s, got_b[2 * comp + x], got_a[2 * comp + x])
            elif x < nx + 2:
                tile = vel[comp, x - 2]
            else:
                at = 2 * comp + x - nx - 2
                tile = jnp.where(even_s, got_a[at], got_b[at])
            first, last = tile[0:2], tile[nz - 2 : nz]
            row = 2 * (comp * (nx + 4) + x)
            send_c[row : row + 2] = jnp.where(even_p, last, first)
            send_d[row : row + 2] = jnp.where(even_p, first, last)
    top[...] = jnp.maximum(near[...], got_n[...])
    base = 6 * (nx + 4)
    for field in range(SCALARS):
        ref = dens if field == 0 else temp if field == 1 else spec.at[field - 2]
        row = base + field * nx
        send_c[row : row + nx] = jnp.where(even_p, ref[:, nz - 1, :], ref[:, 0, :])


def pack_far(dens, temp, spec, far_a, far_d):
    even_s = even_index("stream")
    even_p = even_index("span")
    nx, nz = dens.shape[0], dens.shape[1]
    for field in range(SCALARS):
        ref = dens if field == 0 else temp if field == 1 else spec.at[field - 2]
        far_a[field] = jnp.where(even_s, ref[nx - 1], ref[0])
        row = field * nx
        far_d[row : row + nx] = jnp.where(even_p, ref[:, 0, :], ref[:, nz - 1, :])
    for row in range(SCALARS * nx, far_d.shape[0], nx):
        far_d[row : row + nx] = far_d[0:nx]


def along_y(tile, lane):
    width = tile.shape[-1]
    after = jnp.where(lane == width - 1, 0.0, pltpu.roll(tile, width - 1, 1))
    before = jnp.where(lane == 0, 0.0, pltpu.roll(tile, 1, 1))
    return after, before


def differences(ref, x, i, shift, lane):
    center = ref[i, x]
    after, before = along_y(center, lane)
    return [ref[i, x + 1] - ref[i, x - 1], after - before, shift(center, -1) - shift(center, 1)]


def strain_of(diffs):
    parts = [diffs[i][i] if i == j else diffs[i][j] + diffs[j][i] for i, j in pair_list]
    diagonal = parts[0] * parts[0] + parts[1] * parts[1] + parts[2] * parts[2]
    off = parts[3] * parts[3] + parts[4] * parts[4] + parts[5] * parts[5]
    return parts, jnp.sqrt(0.5 * diagonal + 0.25 * off)


def germano(vel, got_a, got_b, got_c, got_d, far_d, red, mag, wide, shear, smooth, square):
    even_s = even_index("stream")
    even_p = even_index("span")
    nx, nz, ny = vel.shape[1], vel.shape[2], vel.shape[3]
    rows = 2 * nz
    zero = jnp.zeros((nz - 4, ny), jnp.float32)
    for comp in range(3):
        for x in range(nx + 4):
            if x < 2:
                tile = jnp.where(even_s, got_b[2 * comp + x], got_a[2 * comp + x])
            elif x < nx + 2:
                tile = vel[comp, x - 2]
            else:
                at = 2 * comp + x - nx - 2
                tile = jnp.where(even_s, got_a[at], got_b[at])
            row = 2 * (comp * (nx + 4) + x)
            one, two = got_c[row : row + 2], got_d[row : row + 2]
            wide[comp, x, 0:nz] = tile
            wide[comp, x, nz : nz + 2] = jnp.where(even_p, one, two)
            wide[comp, x, nz + 2 : rows - 2] = zero
            wide[comp, x, rows - 2 : rows] = jnp.where(even_p, two, one)
    lane = lax.broadcasted_iota(jnp.int32, (rows, ny), 1)

    def shift(tile, by):
        return pltpu.roll(tile, by % rows, 0)

    def z_sum(tile):
        pair = tile + shift(tile, -1)
        return pair + shift(pair, 1)

    position = lax.axis_index("stream") * nx
    total = lax.axis_size("stream") * nx

    last = None
    for x in range(nx + 4):
        here = [wide[i, x] for i in range(3)]
        products = [here[i] * here[j] for i, j in pair_list]
        if last is not None:
            for k in range(6):
                square[k, x - 1] = products[k] + last[k]
        last = products

    for x in range(nx + 2):
        keep = 1.0
        if x == 0:
            keep = jnp.where(position > 0, 1.0, 0.0)
        elif x == nx + 1:
            keep = jnp.where(position + nx < total, 1.0, 0.0)
        parts, size = strain_of([differences(wide, x + 1, i, shift, lane) for i in range(3)])
        if 1 <= x <= nx:
            mag[x - 1] = size[0:nz]
        straight = size * (keep * 0.03125)
        crossed = size * (keep * 0.015625)
        for k, (i, j) in enumerate(pair_list):
            shear[k, x] = (straight if i == j else crossed) * parts[k]
        for i in range(3):
            value = (wide[i, x] + wide[i, x + 2]) + 2.0 * wide[i, x + 1]
            smooth[i, x] = z_sum(value) * (keep * 0.0625)
    for x in range(nx):
        hat_parts, hat_size = strain_of(
            [differences(smooth, x + 1, i, shift, lane) for i in range(3)]
        )
        straight = 2.0 * hat_size
        lm = [None, None]
        mm = [None, None]
        for k, (i, j) in enumerate(pair_list):
            kind = 0 if i == j else 1
            product = z_sum(square[k, x + 1] + square[k, x + 2])
            resolved = 0.0625 * product - smooth[i, x + 1] * smooth[j, x + 1]
            filtered = z_sum((shear[k, x] + shear[k, x + 2]) + 2.0 * shear[k, x + 1])
            model = filtered - (straight if i == j else hat_size) * hat_parts[k]
            lm[kind] = resolved * model if lm[kind] is None else lm[kind] + resolved * model
            mm[kind] = model * model if mm[kind] is None else mm[kind] + model * model
        lm = (lm[0] + 2.0 * lm[1])[0:nz]
        mm = (mm[0] + 2.0 * mm[1])[0:nz]
        lm = jnp.sum(lm, axis=0, keepdims=True)
        mm = jnp.sum(mm, axis=0, keepdims=True)
        half = ny // 2
        red[x : x + 1] = lm[:, :half]
        red[nx + x : nx + x + 1] = lm[:, half:]
        red[2 * nx + x : 2 * nx + x + 1] = mm[:, :half]
        red[3 * nx + x : 3 * nx + x + 1] = mm[:, half:]


def join(red, near, got_n, out):
    sums, half = red.shape
    out[:sums] = red[...]
    top = jnp.maximum(near[...], got_n[...])
    out[sums:] = jnp.maximum(top[:, :half], top[:, half:])


def chemistry(dens, inverse, temp, species):
    over = 1.0 / temp
    root = jnp.sqrt(temp)
    powers = {0.0: None, 0.5: root, 1.0: temp, -1.0: over, -0.5: root * over, -2.0: over * over}
    e05 = jnp.exp(-0.05 * over)
    e15 = jnp.exp(-1.5 * over)
    decay = {0: None, 5: e05, 150: e15}
    decay[10] = e05 * e05
    decay[20] = decay[10] * decay[10]
    decay[30] = decay[20] * decay[10]
    decay[40] = decay[20] * decay[20]
    decay[70] = decay[40] * decay[30]
    decay[80] = decay[40] * decay[40]
    decay[160] = e15 * decay[10]
    decay[180] = e15 * decay[30]
    decay[200] = decay[180] * decay[20]
    conc = [dens * (species[k] * float(1.0 / molar_weight[k])) for k in range(SPECIES)]
    total = conc[0]
    for k in range(1, SPECIES):
        total = total + conc[k]
    conc.append(total)
    products = {}

    def product(ids):
        if len(ids) == 1:
            return conc[ids[0]]
        if ids not in products:
            products[ids] = product(ids[:-1]) * conc[ids[-1]]
        return products[ids]

    produced = [None] * SPECIES
    for number, (reactants, results) in enumerate(reaction_list):
        ordered = tuple(sorted(reactants))
        pace = product(ordered) * float(np.exp(np.float64(log_prefactor[number])))
        power = powers[float(thermal_power_index[number])]
        if power is not None:
            pace = pace * power
        fall = decay[int(round(float(arrhenius_barrier[number]) * 100))]
        if fall is not None:
            pace = pace * fall
        change = {}
        for k in reactants:
            if k < SPECIES:
                change[k] = change.get(k, 0) - 1
        for k in results:
            change[k] = change.get(k, 0) + 1
        for k, times in change.items():
            if times == 0:
                continue
            term = pace if abs(times) == 1 else pace * float(abs(times))
            if produced[k] is None:
                produced[k] = term if times > 0 else -term
            else:
                produced[k] = produced[k] + term if times > 0 else produced[k] - term
    heat = None
    for k in range(SPECIES):
        if formation[k] != 0.0 and produced[k] is not None:
            term = produced[k] * float(-formation[k] / heat_capacity)
            heat = term if heat is None else heat + term
    source = [
        None if produced[k] is None else produced[k] * inverse * float(molar_weight[k])
        for k in range(SPECIES)
    ]
    return source, heat * inverse


def tendencies(
    vel, dens, temp, spec, fuel, got_a, got_b, got_c, got_d, far_a, far_d, mag, base, slope
):
    even_s = even_index("stream")
    even_p = even_index("span")
    nx, nz, ny = dens.shape
    lane = lax.broadcasted_iota(jnp.int32, (nz, ny), 1)
    line = lax.broadcasted_iota(jnp.int32, (nz, ny), 0)

    def own(field, x):
        if field < 3:
            return vel[field, x]
        if field == 3:
            return dens[x]
        if field == 4:
            return temp[x]
        return spec[field - 5, x]

    def cell(field, x):
        if 0 <= x < nx:
            return own(field, x)
        if field < 3:
            at = 2 * field + (1 if x < 0 else 0)
            one, two = got_a[at], got_b[at]
        else:
            one, two = far_a[field - 3], got_b[3 + field]
        return jnp.where(even_s, two, one) if x < 0 else jnp.where(even_s, one, two)

    def edges(field, x):
        if field < 3:
            row = 2 * (field * (nx + 4) + x + 2)
            c0, c1 = got_c[row : row + 1], got_c[row + 1 : row + 2]
            d0, d1 = got_d[row : row + 1], got_d[row + 1 : row + 2]
            return jnp.where(even_p, c0, d0), jnp.where(even_p, d1, c1)
        line_at = (field - 3) * nx + x
        row = 6 * (nx + 4) + line_at
        c0, d0 = got_c[row : row + 1], far_d[line_at : line_at + 1]
        return jnp.where(even_p, c0, d0), jnp.where(even_p, d0, c0)

    def neighbours(field, x):
        center = own(field, x)
        after, before = along_y(center, lane)
        high, low = edges(field, x)
        up = jnp.where(line == nz - 1, high, pltpu.roll(center, nz - 1, 0))
        down = jnp.where(line == 0, low, pltpu.roll(center, 1, 0))
        return center, cell(field, x + 1), cell(field, x - 1), after, before, up, down

    for x in range(nx):
        v = [neighbours(i, x) for i in range(3)]
        r = neighbours(3, x)
        t = neighbours(4, x)
        half = [0.5 * v[i][0] for i in range(3)]
        inverse = 1.0 / r[0]
        size = mag[x]
        inject = fuel[x].astype(jnp.float32) * inject_rate
        species = [own(5 + k, x) for k in range(SPECIES)]
        source, release = chemistry(r[0], inverse, t[0], species)

        def advect(n):
            return half[0] * (n[1] - n[2]) + half[1] * (n[3] - n[4]) + half[2] * (n[5] - n[6])

        def laplace(n):
            return ((n[1] + n[2]) + (n[3] + n[4])) + ((n[5] + n[6]) - 6.0 * n[0])

        push = [r[m] * t[m] for m in range(1, 7)]
        scale = 0.5 * inverse
        for i in range(3):
            lap = laplace(v[i])
            value = laminar_diffusivity * lap - advect(v[i]) - (push[2 * i] - push[2 * i + 1]) * scale
            if i == 1:
                value = value + inject * (inject_speed - v[1][0])
            base[i, x] = value
            slope[i, x] = size * lap
        flux = (
            (r[1] * v[0][1] - r[2] * v[0][2])
            + (r[3] * v[1][3] - r[4] * v[1][4])
            + (r[5] * v[2][5] - r[6] * v[2][6])
        )
        base[3, x] = -0.5 * flux
        thin = size * (1.0 / subgrid_thermal_quotient)
        lap = laplace(t)
        base[4, x] = (laminar_diffusivity / momentum_thermal_quotient) * lap - advect(t) + release
        slope[3, x] = thin * lap
        for k in range(SPECIES):
            n = neighbours(5 + k, x)
            lap = laplace(n)
            value = (laminar_diffusivity / schmidt) * lap - advect(n)
            if source[k] is not None:
                value = value + source[k]
            if k == 0:
                value = value + inject * (1.0 - n[0])
            base[5 + k, x] = value
            slope[4 + k, x] = thin * lap


def finish(
    total_z, vel, dens, temp, spec, wall, base, slope, r0, r1, r2, r3, out_v, out_r, out_t, out_y, out_c
):
    nx = dens.shape[0]
    sums = (r0[: 4 * nx] + r1[: 4 * nx]) + (r2[: 4 * nx] + r3[: 4 * nx])
    lm = jnp.concatenate([sums[:nx], sums[nx : 2 * nx]], axis=1)
    mm = jnp.concatenate([sums[2 * nx : 3 * nx], sums[3 * nx :]], axis=1)
    coef = jnp.maximum(0.5 * (lm / total_z) / (mm / total_z + tiny_value), 0.0)
    out_c[...] = coef
    top = jnp.maximum(
        jnp.maximum(r0[4 * nx :], r1[4 * nx :]), jnp.maximum(r2[4 * nx :], r3[4 * nx :])
    )
    step = courant / jnp.max(jnp.max(top, axis=0, keepdims=True), axis=1, keepdims=True)
    gain = coef * step
    for x in range(nx):
        g = gain[x : x + 1]
        open_cell = 1.0 - wall[x].astype(jnp.float32)
        for i in range(3):
            out_v[i, x] = open_cell * (vel[i, x] + step * base[i, x] + g * slope[i, x])
        out_r[x] = dens[x] + step * base[3, x]
        out_t[x] = temp[x] + step * base[4, x] + g * slope[3, x]
        for k in range(SPECIES):
            out_y[k, x] = spec[k, x] + step * base[5 + k, x] + g * slope[4 + k, x]


def per_device(vel, dens, temp, spec, wall, fuel):
    nx, nz, ny = dens.shape
    n_stream = lax.axis_size("stream")
    n_span = lax.axis_size("span")
    send_a, send_b, vel, temp = call(
        pack_stream,
        [(7, nz, ny), (6 + SCALARS, nz, ny), vel.shape, temp.shape],
        (vel, dens, temp, spec),
        scratch=[pltpu.SemaphoreType.DMA((4,))],
        name="pack_stream",
        from_hbm=True,
    )
    got_a = lax.ppermute(send_a, "stream", pair_up(n_stream, 0, False))
    got_b = lax.ppermute(send_b, "stream", pair_up(n_stream, 1, False))
    send_far, send_fd = call(
        pack_far,
        [(SCALARS, nz, ny), (6 * (nx + 4) + SCALARS * nx + nx, ny)],
        (dens, temp, spec),
        name="pack_far",
    )
    far_d = lax.ppermute(send_fd, "span", pair_up(n_span, 1, True))
    near = jnp.maximum(send_a[6], got_a[6])
    got_n = lax.ppermute(near, "stream", flip(n_stream, 2))
    rows = 6 * (nx + 4) + SCALARS * nx
    send_c, send_d, near = call(
        pack_span,
        [(rows, ny), (6 * (nx + 4), ny), (nz, ny)],
        (vel, dens, temp, spec, got_a, got_b, near, got_n),
        name="pack_span",
    )
    got_c = lax.ppermute(send_c, "span", pair_up(n_span, 0, True))
    got_d = lax.ppermute(send_d, "span", pair_up(n_span, 1, True))
    send_far, got_c = lax.optimization_barrier((send_far, got_c))
    far_a = lax.ppermute(send_far, "stream", pair_up(n_stream, 0, False))
    bit = 4
    while bit * 2 < n_stream:
        near = jnp.maximum(near, lax.ppermute(near, "stream", flip(n_stream, bit)))
        bit *= 2
    got_n = lax.ppermute(near, "stream", flip(n_stream, bit))
    red, mag = call(
        germano,
        [(4 * nx, ny // 2), (nx, nz, ny)],
        (vel, got_a, got_b, got_c, got_d, far_d),
        scratch=[
            VMEM((3, nx + 4, 2 * nz, ny), jnp.float32),
            VMEM((6, nx + 2, 2 * nz, ny), jnp.float32),
            VMEM((3, nx + 2, 2 * nz, ny), jnp.float32),
            VMEM((6, nx + 3, 2 * nz, ny), jnp.float32),
        ],
        name="germano",
        flops=1000000000,
    )
    base, slope = call(
        tendencies,
        [(5 + SPECIES, nx, nz, ny), (4 + SPECIES, nx, nz, ny)],
        (vel, dens, temp, spec, fuel, got_a, got_b, got_c, got_d, far_a, far_d, mag),
        name="tendencies",
    )
    (red,) = call(join, [(4 * nx + nz, ny // 2)], (red, near, got_n), name="join")
    bit = 1
    while bit * 4 < n_span:
        others = [lax.ppermute(red, "span", flip(n_span, bit * m)) for m in (1, 2, 3)]
        low = (red[: 4 * nx] + others[0][: 4 * nx]) + (others[1][: 4 * nx] + others[2][: 4 * nx])
        high = jnp.maximum(
            jnp.maximum(red[4 * nx :], others[0][4 * nx :]),
            jnp.maximum(others[1][4 * nx :], others[2][4 * nx :]),
        )
        red = jnp.concatenate([low, high], axis=0)
        bit *= 4
    others = [lax.ppermute(red, "span", flip(n_span, bit * m)) for m in (1, 3, 2)]
    return tuple(
        call(
            functools.partial(finish, float(nz * n_span)),
            [vel.shape, dens.shape, dens.shape, spec.shape, (nx, ny)],
            (vel, dens, temp, spec, wall, base, slope, red, *others),
            name="finish",
            to_hbm=True,
        )
    )


def solution(mesh):
    return jax.shard_map(
        per_device,
        mesh=mesh,
        in_specs=(
            P(None, "stream", "span", None),
            P("stream", "span", None),
            P("stream", "span", None),
            P(None, "stream", "span", None),
            P("stream", "span", None),
            P("stream", "span", None),
        ),
        out_specs=(
            P(None, "stream", "span", None),
            P("stream", "span", None),
            P("stream", "span", None),
            P(None, "stream", "span", None),
            P("stream", None),
        ),
        check_vma=False,
    )
```

```python
import functools

import jax
import jax.numpy as jnp
import numpy as np
from jax import lax
from jax.experimental import pallas as pl
from jax.experimental.pallas import tpu as pltpu
from jax.sharding import PartitionSpec as P

SPECIES = 9
SCALARS = 11
adiabatic_gamma = 1.4
courant = 0.5
laminar_diffusivity = 0.05
momentum_thermal_quotient = 0.7
schmidt = 0.7
subgrid_thermal_quotient = 0.9
inject_rate = 5.0
inject_speed = 2.0
heat_capacity = 3.5
tiny_value = 1e-06
reaction_list = (
    ((4, 1), (5, 3)),
    ((5, 0), (4, 3)),
    ((0, 3), (2, 4)),
    ((5, 2), (3, 3)),
    ((0, 9), (4, 4)),
    ((5, 5, 9), (1,)),
    ((5, 4, 9), (3,)),
    ((4, 3, 9), (2,)),
    ((4, 1, 9), (6,)),
    ((6, 4), (0, 1)),
    ((6, 4), (3, 3)),
    ((6, 5), (1, 3)),
    ((6, 3), (2, 1)),
    ((6, 6), (7, 1)),
    ((7, 9), (3, 3)),
    ((7, 4), (2, 3)),
    ((7, 4), (6, 0)),
    ((7, 5), (3, 6)),
    ((7, 3), (6, 2)),
)
log_prefactor = np.array(
    [3.9, 3.2, 3.4, 3.0, 2.0, 6.0, 6.2, 6.5, 5.8, 3.8, 3.6, 3.5, 3.7, 3.1, 2.2, 3.3, 3.4, 3.0, 3.2],
    np.float32,
)
thermal_power_index = np.array(
    [
        0.0,
        0.5,
        0.5,
        1.0,
        -1.0,
        -0.5,
        -1.0,
        -2.0,
        -1.0,
        0.0,
        0.0,
        0.0,
        0.0,
        0.0,
        0.0,
        0.0,
        0.0,
        1.0,
        0.0,
    ],
    np.float32,
)
arrhenius_barrier = np.array(
    [
        1.6,
        0.7,
        0.4,
        1.5,
        2.0,
        0.0,
        0.0,
        0.0,
        0.0,
        0.1,
        0.05,
        0.0,
        0.0,
        0.2,
        1.8,
        0.4,
        0.8,
        0.3,
        0.1,
    ],
    np.float32,
)
molar_weight = np.array([0.125, 2.0, 1.125, 1.0625, 0.0625, 1.0, 2.0625, 2.125, 1.75], np.float32)
formation = np.array([0.0, 0.0, -2.42, 0.39, 2.18, 2.49, 0.12, -1.36, 0.0], np.float32)
pair_list = ((0, 0), (1, 1), (2, 2), (0, 1), (0, 2), (1, 2))


VMEM = pltpu.VMEM


def pair_up(count, start, wrap):
    pairs = []
    for low in range(start, count - 1, 2):
        pairs += [(low, low + 1), (low + 1, low)]
    if wrap and start == 1:
        pairs += [(count - 1, 0), (0, count - 1)]
    return pairs


def flip(count, bit):
    return [(index, index ^ bit) for index in range(count)]


def even_index(axis):
    return lax.rem(lax.axis_index(axis), 2) == 0


def call(body, outs, args, scratch=(), flops=0, name=None, from_hbm=False, to_hbm=False):
    nbytes = sum(int(np.prod(a.shape)) * 4 for a in args) + sum(
        int(np.prod(s)) * 4 for s in outs
    )
    return pl.pallas_call(
        body,
        out_shape=[
            jax.ShapeDtypeStruct(s, jnp.float32) if to_hbm else VMEM(s, jnp.float32) for s in outs
        ],
        in_specs=[pl.BlockSpec(memory_space=pltpu.HBM if from_hbm else VMEM)] * len(args),
        out_specs=[pl.BlockSpec(memory_space=VMEM)] * len(outs),
        scratch_shapes=list(scratch),
        compiler_params=pltpu.CompilerParams(vmem_limit_bytes=8 << 20),
        cost_estimate=pl.CostEstimate(flops=flops, bytes_accessed=nbytes, transcendentals=0),
        name=name,
    )(*[pltpu.with_memory_space_constraint(a, pltpu.HBM if from_hbm else VMEM) for a in args])


def pack_stream(hbm_v, hbm_r, hbm_t, hbm_y, send_a, send_b, vel, temp, done):
    even = even_index("stream")
    nx = vel.shape[1]
    edge = jnp.where(even, 0, nx - 1)
    copies = [
        pltpu.make_async_copy(src, dst, done.at[k])
        for k, (src, dst) in enumerate(
            (
                (hbm_v, vel),
                (hbm_t, temp),
                (hbm_y.at[:, edge], send_b.at[pl.ds(8, SPECIES)]),
                (hbm_r.at[pl.ds(edge, 1)], send_b.at[pl.ds(6, 1)]),
            )
        )
    ]
    for copy in copies:
        copy.start()
    copies[0].wait()
    for comp in range(3):
        for layer in range(2):
            low = vel[comp, layer]
            high = vel[comp, nx - 2 + layer]
            send_a[2 * comp + layer] = jnp.where(even, high, low)
            send_b[2 * comp + layer] = jnp.where(even, low, high)
    copies[1].wait()
    send_b[7] = jnp.where(even, temp[0], temp[nx - 1])
    fastest = None
    for x in range(nx):
        speed = (
            jnp.abs(vel[0, x])
            + jnp.abs(vel[1, x])
            + jnp.abs(vel[2, x])
            + jnp.sqrt(adiabatic_gamma * temp[x])
        )
        fastest = speed if fastest is None else jnp.maximum(fastest, speed)
    send_a[6] = fastest
    copies[2].wait()
    copies[3].wait()


def pack_span(vel, dens, temp, spec, got_a, got_b, near, got_n, send_c, send_d, top):
    even_s = even_index("stream")
    even_p = even_index("span")
    nx, nz = vel.shape[1], vel.shape[2]
    for comp in range(3):
        for x in range(nx + 4):
            if x < 2:
                tile = jnp.where(even_s, got_b[2 * comp + x], got_a[2 * comp + x])
            elif x < nx + 2:
                tile = vel[comp, x - 2]
            else:
                at = 2 * comp + x - nx - 2
                tile = jnp.where(even_s, got_a[at], got_b[at])
            first, last = tile[0:2], tile[nz - 2 : nz]
            row = 2 * (comp * (nx + 4) + x)
            send_c[row : row + 2] = jnp.where(even_p, last, first)
            send_d[row : row + 2] = jnp.where(even_p, first, last)
    top[...] = jnp.maximum(near[...], got_n[...])
    base = 6 * (nx + 4)
    for field in range(SCALARS):
        ref = dens if field == 0 else temp if field == 1 else spec.at[field - 2]
        row = base + field * nx
        send_c[row : row + nx] = jnp.where(even_p, ref[:, nz - 1, :], ref[:, 0, :])


def pack_far(dens, temp, spec, far_a, far_d):
    even_s = even_index("stream")
    even_p = even_index("span")
    nx, nz = dens.shape[0], dens.shape[1]
    for field in range(SCALARS):
        ref = dens if field == 0 else temp if field == 1 else spec.at[field - 2]
        far_a[field] = jnp.where(even_s, ref[nx - 1], ref[0])
        row = field * nx
        far_d[row : row + nx] = jnp.where(even_p, ref[:, 0, :], ref[:, nz - 1, :])
    for row in range(SCALARS * nx, far_d.shape[0], nx):
        far_d[row : row + nx] = far_d[0:nx]
    for extra in range(SCALARS, far_a.shape[0]):
        far_a[extra] = far_a[0]


def along_y(tile, lane):
    width = tile.shape[-1]
    after = jnp.where(lane == width - 1, 0.0, pltpu.roll(tile, width - 1, 1))
    before = jnp.where(lane == 0, 0.0, pltpu.roll(tile, 1, 1))
    return after, before


def differences(ref, x, i, shift, lane):
    center = ref[i, x]
    after, before = along_y(center, lane)
    return [ref[i, x + 1] - ref[i, x - 1], after - before, shift(center, -1) - shift(center, 1)]


def strain_of(diffs):
    parts = [diffs[i][i] if i == j else diffs[i][j] + diffs[j][i] for i, j in pair_list]
    diagonal = parts[0] * parts[0] + parts[1] * parts[1] + parts[2] * parts[2]
    off = parts[3] * parts[3] + parts[4] * parts[4] + parts[5] * parts[5]
    return parts, jnp.sqrt(0.5 * diagonal + 0.25 * off)


def germano(vel, got_a, got_b, got_c, got_d, far_a, far_d, red, mag, wide, shear, smooth, square):
    even_s = even_index("stream")
    even_p = even_index("span")
    nx, nz, ny = vel.shape[1], vel.shape[2], vel.shape[3]
    rows = 2 * nz
    zero = jnp.zeros((nz - 4, ny), jnp.float32)
    for comp in range(3):
        for x in range(nx + 4):
            if x < 2:
                tile = jnp.where(even_s, got_b[2 * comp + x], got_a[2 * comp + x])
            elif x < nx + 2:
                tile = vel[comp, x - 2]
            else:
                at = 2 * comp + x - nx - 2
                tile = jnp.where(even_s, got_a[at], got_b[at])
            row = 2 * (comp * (nx + 4) + x)
            one, two = got_c[row : row + 2], got_d[row : row + 2]
            wide[comp, x, 0:nz] = tile
            wide[comp, x, nz : nz + 2] = jnp.where(even_p, one, two)
            wide[comp, x, nz + 2 : rows - 2] = zero
            wide[comp, x, rows - 2 : rows] = jnp.where(even_p, two, one)
    lane = lax.broadcasted_iota(jnp.int32, (rows, ny), 1)

    def shift(tile, by):
        return pltpu.roll(tile, by % rows, 0)

    def z_sum(tile):
        pair = tile + shift(tile, -1)
        return pair + shift(pair, 1)

    position = lax.axis_index("stream") * nx
    total = lax.axis_size("stream") * nx

    last = None
    for x in range(nx + 4):
        here = [wide[i, x] for i in range(3)]
        products = [here[i] * here[j] for i, j in pair_list]
        if last is not None:
            for k in range(6):
                square[k, x - 1] = products[k] + last[k]
        last = products

    for x in range(nx + 2):
        keep = 1.0
        if x == 0:
            keep = jnp.where(position > 0, 1.0, 0.0)
        elif x == nx + 1:
            keep = jnp.where(position + nx < total, 1.0, 0.0)
        parts, size = strain_of([differences(wide, x + 1, i, shift, lane) for i in range(3)])
        if 1 <= x <= nx:
            mag[x - 1] = size[0:nz]
        straight = size * (keep * 0.03125)
        crossed = size * (keep * 0.015625)
        for k, (i, j) in enumerate(pair_list):
            shear[k, x] = (straight if i == j else crossed) * parts[k]
        for i in range(3):
            value = (wide[i, x] + wide[i, x + 2]) + 2.0 * wide[i, x + 1]
            smooth[i, x] = z_sum(value) * (keep * 0.0625)
    for x in range(nx):
        hat_parts, hat_size = strain_of(
            [differences(smooth, x + 1, i, shift, lane) for i in range(3)]
        )
        straight = 2.0 * hat_size
        lm = [None, None]
        mm = [None, None]
        for k, (i, j) in enumerate(pair_list):
            kind = 0 if i == j else 1
            product = z_sum(square[k, x + 1] + square[k, x + 2])
            resolved = 0.0625 * product - smooth[i, x + 1] * smooth[j, x + 1]
            filtered = z_sum((shear[k, x] + shear[k, x + 2]) + 2.0 * shear[k, x + 1])
            model = filtered - (straight if i == j else hat_size) * hat_parts[k]
            lm[kind] = resolved * model if lm[kind] is None else lm[kind] + resolved * model
            mm[kind] = model * model if mm[kind] is None else mm[kind] + model * model
        lm = (lm[0] + 2.0 * lm[1])[0:nz]
        mm = (mm[0] + 2.0 * mm[1])[0:nz]
        lm = jnp.sum(lm, axis=0, keepdims=True)
        mm = jnp.sum(mm, axis=0, keepdims=True)
        half = ny // 2
        red[x : x + 1] = lm[:, :half]
        red[nx + x : nx + x + 1] = lm[:, half:]
        red[2 * nx + x : 2 * nx + x + 1] = mm[:, :half]
        red[3 * nx + x : 3 * nx + x + 1] = mm[:, half:]


def join(red, near, got_n, out):
    sums, half = red.shape
    out[:sums] = red[...]
    top = jnp.maximum(near[...], got_n[...])
    out[sums:] = jnp.maximum(top[:, :half], top[:, half:])


def chemistry(dens, inverse, temp, species):
    over = 1.0 / temp
    root = jnp.sqrt(temp)
    powers = {0.0: None, 0.5: root, 1.0: temp, -1.0: over, -0.5: root * over, -2.0: over * over}
    e05 = jnp.exp(-0.05 * over)
    e15 = jnp.exp(-1.5 * over)
    decay = {0: None, 5: e05, 150: e15}
    decay[10] = e05 * e05
    decay[20] = decay[10] * decay[10]
    decay[30] = decay[20] * decay[10]
    decay[40] = decay[20] * decay[20]
    decay[70] = decay[40] * decay[30]
    decay[80] = decay[40] * decay[40]
    decay[160] = e15 * decay[10]
    decay[180] = e15 * decay[30]
    decay[200] = decay[180] * decay[20]
    conc = [dens * (species[k] * float(1.0 / molar_weight[k])) for k in range(SPECIES)]
    total = conc[0]
    for k in range(1, SPECIES):
        total = total + conc[k]
    conc.append(total)
    products = {}

    def product(ids):
        if len(ids) == 1:
            return conc[ids[0]]
        if ids not in products:
            products[ids] = product(ids[:-1]) * conc[ids[-1]]
        return products[ids]

    produced = [None] * SPECIES
    for number, (reactants, results) in enumerate(reaction_list):
        ordered = tuple(sorted(reactants))
        pace = product(ordered) * float(np.exp(np.float64(log_prefactor[number])))
        power = powers[float(thermal_power_index[number])]
        if power is not None:
            pace = pace * power
        fall = decay[int(round(float(arrhenius_barrier[number]) * 100))]
        if fall is not None:
            pace = pace * fall
        change = {}
        for k in reactants:
            if k < SPECIES:
                change[k] = change.get(k, 0) - 1
        for k in results:
            change[k] = change.get(k, 0) + 1
        for k, times in change.items():
            if times == 0:
                continue
            term = pace if abs(times) == 1 else pace * float(abs(times))
            if produced[k] is None:
                produced[k] = term if times > 0 else -term
            else:
                produced[k] = produced[k] + term if times > 0 else produced[k] - term
    heat = None
    for k in range(SPECIES):
        if formation[k] != 0.0 and produced[k] is not None:
            term = produced[k] * float(-formation[k] / heat_capacity)
            heat = term if heat is None else heat + term
    source = [
        None if produced[k] is None else produced[k] * inverse * float(molar_weight[k])
        for k in range(SPECIES)
    ]
    return source, heat * inverse


def tendencies(
    vel, dens, temp, spec, fuel, got_a, got_b, got_c, got_d, far_a, far_d, mag, base, slope
):
    even_s = even_index("stream")
    even_p = even_index("span")
    nx, nz, ny = dens.shape
    lane = lax.broadcasted_iota(jnp.int32, (nz, ny), 1)
    line = lax.broadcasted_iota(jnp.int32, (nz, ny), 0)

    def own(field, x):
        if field < 3:
            return vel[field, x]
        if field == 3:
            return dens[x]
        if field == 4:
            return temp[x]
        return spec[field - 5, x]

    def cell(field, x):
        if 0 <= x < nx:
            return own(field, x)
        if field < 3:
            at = 2 * field + (1 if x < 0 else 0)
            one, two = got_a[at], got_b[at]
        else:
            one, two = far_a[field - 3], got_b[3 + field]
        return jnp.where(even_s, two, one) if x < 0 else jnp.where(even_s, one, two)

    def edges(field, x):
        if field < 3:
            row = 2 * (field * (nx + 4) + x + 2)
            c0, c1 = got_c[row : row + 1], got_c[row + 1 : row + 2]
            d0, d1 = got_d[row : row + 1], got_d[row + 1 : row + 2]
            return jnp.where(even_p, c0, d0), jnp.where(even_p, d1, c1)
        line_at = (field - 3) * nx + x
        row = 6 * (nx + 4) + line_at
        c0, d0 = got_c[row : row + 1], far_d[line_at : line_at + 1]
        return jnp.where(even_p, c0, d0), jnp.where(even_p, d0, c0)

    def neighbours(field, x):
        center = own(field, x)
        after, before = along_y(center, lane)
        high, low = edges(field, x)
        up = jnp.where(line == nz - 1, high, pltpu.roll(center, nz - 1, 0))
        down = jnp.where(line == 0, low, pltpu.roll(center, 1, 0))
        return center, cell(field, x + 1), cell(field, x - 1), after, before, up, down

    for x in range(nx):
        v = [neighbours(i, x) for i in range(3)]
        r = neighbours(3, x)
        t = neighbours(4, x)
        half = [0.5 * v[i][0] for i in range(3)]
        inverse = 1.0 / r[0]
        size = mag[x]
        inject = fuel[x].astype(jnp.float32) * inject_rate
        species = [own(5 + k, x) for k in range(SPECIES)]
        source, release = chemistry(r[0], inverse, t[0], species)

        def advect(n):
            return half[0] * (n[1] - n[2]) + half[1] * (n[3] - n[4]) + half[2] * (n[5] - n[6])

        def laplace(n):
            return ((n[1] + n[2]) + (n[3] + n[4])) + ((n[5] + n[6]) - 6.0 * n[0])

        push = [r[m] * t[m] for m in range(1, 7)]
        scale = 0.5 * inverse
        for i in range(3):
            lap = laplace(v[i])
            value = laminar_diffusivity * lap - advect(v[i]) - (push[2 * i] - push[2 * i + 1]) * scale
            if i == 1:
                value = value + inject * (inject_speed - v[1][0])
            base[i, x] = value
            slope[i, x] = size * lap
        flux = (
            (r[1] * v[0][1] - r[2] * v[0][2])
            + (r[3] * v[1][3] - r[4] * v[1][4])
            + (r[5] * v[2][5] - r[6] * v[2][6])
        )
        base[3, x] = -0.5 * flux
        thin = size * (1.0 / subgrid_thermal_quotient)
        lap = laplace(t)
        base[4, x] = (laminar_diffusivity / momentum_thermal_quotient) * lap - advect(t) + release
        slope[3, x] = thin * lap
        for k in range(SPECIES):
            n = neighbours(5 + k, x)
            lap = laplace(n)
            value = (laminar_diffusivity / schmidt) * lap - advect(n)
            if source[k] is not None:
                value = value + source[k]
            if k == 0:
                value = value + inject * (1.0 - n[0])
            base[5 + k, x] = value
            slope[4 + k, x] = thin * lap


def finish(
    total_z, vel, dens, temp, spec, wall, base, slope, r0, r1, r2, r3, out_v, out_r, out_t, out_y, out_c
):
    nx = dens.shape[0]
    sums = (r0[: 4 * nx] + r1[: 4 * nx]) + (r2[: 4 * nx] + r3[: 4 * nx])
    lm = jnp.concatenate([sums[:nx], sums[nx : 2 * nx]], axis=1)
    mm = jnp.concatenate([sums[2 * nx : 3 * nx], sums[3 * nx :]], axis=1)
    coef = jnp.maximum(0.5 * (lm / total_z) / (mm / total_z + tiny_value), 0.0)
    out_c[...] = coef
    top = jnp.maximum(
        jnp.maximum(r0[4 * nx :], r1[4 * nx :]), jnp.maximum(r2[4 * nx :], r3[4 * nx :])
    )
    step = courant / jnp.max(jnp.max(top, axis=0, keepdims=True), axis=1, keepdims=True)
    gain = coef * step
    for x in range(nx):
        g = gain[x : x + 1]
        open_cell = 1.0 - wall[x].astype(jnp.float32)
        for i in range(3):
            out_v[i, x] = open_cell * (vel[i, x] + step * base[i, x] + g * slope[i, x])
        out_r[x] = dens[x] + step * base[3, x]
        out_t[x] = temp[x] + step * base[4, x] + g * slope[3, x]
        for k in range(SPECIES):
            out_y[k, x] = spec[k, x] + step * base[5 + k, x] + g * slope[4 + k, x]


def per_device(vel, dens, temp, spec, wall, fuel):
    nx, nz, ny = dens.shape
    n_stream = lax.axis_size("stream")
    n_span = lax.axis_size("span")
    send_a, send_b, vel, temp = call(
        pack_stream,
        [(7, nz, ny), (6 + SCALARS, nz, ny), vel.shape, temp.shape],
        (vel, dens, temp, spec),
        scratch=[pltpu.SemaphoreType.DMA((4,))],
        name="pack_stream",
        from_hbm=True,
    )
    got_a = lax.ppermute(send_a, "stream", pair_up(n_stream, 0, False))
    got_b = lax.ppermute(send_b, "stream", pair_up(n_stream, 1, False))
    send_far, send_fd = call(
        pack_far,
        [(21, nz, ny), (6 * (nx + 4) + SCALARS * nx + 2 * nx, ny)],
        (dens, temp, spec),
        name="pack_far",
    )
    far_d = lax.ppermute(send_fd, "span", pair_up(n_span, 1, True))
    near = jnp.maximum(send_a[6], got_a[6])
    got_n = lax.ppermute(near, "stream", flip(n_stream, 2))
    rows = 6 * (nx + 4) + SCALARS * nx
    send_c, send_d, near = call(
        pack_span,
        [(rows, ny), (6 * (nx + 4), ny), (nz, ny)],
        (vel, dens, temp, spec, got_a, got_b, near, got_n),
        name="pack_span",
    )
    far_a = lax.ppermute(send_far, "stream", pair_up(n_stream, 0, False))
    got_c = lax.ppermute(send_c, "span", pair_up(n_span, 0, True))
    got_d = lax.ppermute(send_d, "span", pair_up(n_span, 1, True))
    bit = 4
    while bit * 2 < n_stream:
        near = jnp.maximum(near, lax.ppermute(near, "stream", flip(n_stream, bit)))
        bit *= 2
    got_n = lax.ppermute(near, "stream", flip(n_stream, bit))
    red, mag = call(
        germano,
        [(4 * nx, ny // 2), (nx, nz, ny)],
        (vel, got_a, got_b, got_c, got_d, far_a, far_d),
        scratch=[
            VMEM((3, nx + 4, 2 * nz, ny), jnp.float32),
            VMEM((6, nx + 2, 2 * nz, ny), jnp.float32),
            VMEM((3, nx + 2, 2 * nz, ny), jnp.float32),
            VMEM((6, nx + 3, 2 * nz, ny), jnp.float32),
        ],
        name="germano",
        flops=1000000000,
    )
    base, slope = call(
        tendencies,
        [(5 + SPECIES, nx, nz, ny), (4 + SPECIES, nx, nz, ny)],
        (vel, dens, temp, spec, fuel, got_a, got_b, got_c, got_d, far_a, far_d, mag),
        name="tendencies",
    )
    (red,) = call(join, [(4 * nx + nz, ny // 2)], (red, near, got_n), name="join")
    bit = 1
    while bit * 4 < n_span:
        others = [lax.ppermute(red, "span", flip(n_span, bit * m)) for m in (1, 2, 3)]
        low = (red[: 4 * nx] + others[0][: 4 * nx]) + (others[1][: 4 * nx] + others[2][: 4 * nx])
        high = jnp.maximum(
            jnp.maximum(red[4 * nx :], others[0][4 * nx :]),
            jnp.maximum(others[1][4 * nx :], others[2][4 * nx :]),
        )
        red = jnp.concatenate([low, high], axis=0)
        bit *= 4
    others = [lax.ppermute(red, "span", flip(n_span, bit * m)) for m in (1, 3, 2)]
    return tuple(
        call(
            functools.partial(finish, float(nz * n_span)),
            [vel.shape, dens.shape, dens.shape, spec.shape, (nx, ny)],
            (vel, dens, temp, spec, wall, base, slope, red, *others),
            name="finish",
            to_hbm=True,
        )
    )


def solution(mesh):
    return jax.shard_map(
        per_device,
        mesh=mesh,
        in_specs=(
            P(None, "stream", "span", None),
            P("stream", "span", None),
            P("stream", "span", None),
            P(None, "stream", "span", None),
            P("stream", "span", None),
            P("stream", "span", None),
        ),
        out_specs=(
            P(None, "stream", "span", None),
            P("stream", "span", None),
            P("stream", "span", None),
            P(None, "stream", "span", None),
            P("stream", None),
        ),
        check_vma=False,
    )
```

```python
import functools

import jax
import jax.numpy as jnp
import numpy as np
from jax import lax
from jax.experimental import pallas as pl
from jax.experimental.pallas import tpu as pltpu
from jax.sharding import PartitionSpec as P

SPECIES = 9
SCALARS = 11
adiabatic_gamma = 1.4
courant = 0.5
laminar_diffusivity = 0.05
momentum_thermal_quotient = 0.7
schmidt = 0.7
subgrid_thermal_quotient = 0.9
inject_rate = 5.0
inject_speed = 2.0
heat_capacity = 3.5
tiny_value = 1e-06
reaction_list = (
    ((4, 1), (5, 3)),
    ((5, 0), (4, 3)),
    ((0, 3), (2, 4)),
    ((5, 2), (3, 3)),
    ((0, 9), (4, 4)),
    ((5, 5, 9), (1,)),
    ((5, 4, 9), (3,)),
    ((4, 3, 9), (2,)),
    ((4, 1, 9), (6,)),
    ((6, 4), (0, 1)),
    ((6, 4), (3, 3)),
    ((6, 5), (1, 3)),
    ((6, 3), (2, 1)),
    ((6, 6), (7, 1)),
    ((7, 9), (3, 3)),
    ((7, 4), (2, 3)),
    ((7, 4), (6, 0)),
    ((7, 5), (3, 6)),
    ((7, 3), (6, 2)),
)
log_prefactor = np.array(
    [3.9, 3.2, 3.4, 3.0, 2.0, 6.0, 6.2, 6.5, 5.8, 3.8, 3.6, 3.5, 3.7, 3.1, 2.2, 3.3, 3.4, 3.0, 3.2],
    np.float32,
)
thermal_power_index = np.array(
    [
        0.0,
        0.5,
        0.5,
        1.0,
        -1.0,
        -0.5,
        -1.0,
        -2.0,
        -1.0,
        0.0,
        0.0,
        0.0,
        0.0,
        0.0,
        0.0,
        0.0,
        0.0,
        1.0,
        0.0,
    ],
    np.float32,
)
arrhenius_barrier = np.array(
    [
        1.6,
        0.7,
        0.4,
        1.5,
        2.0,
        0.0,
        0.0,
        0.0,
        0.0,
        0.1,
        0.05,
        0.0,
        0.0,
        0.2,
        1.8,
        0.4,
        0.8,
        0.3,
        0.1,
    ],
    np.float32,
)
molar_weight = np.array([0.125, 2.0, 1.125, 1.0625, 0.0625, 1.0, 2.0625, 2.125, 1.75], np.float32)
formation = np.array([0.0, 0.0, -2.42, 0.39, 2.18, 2.49, 0.12, -1.36, 0.0], np.float32)
pair_list = ((0, 0), (1, 1), (2, 2), (0, 1), (0, 2), (1, 2))


VMEM = pltpu.VMEM


def pair_up(count, start, wrap):
    pairs = []
    for low in range(start, count - 1, 2):
        pairs += [(low, low + 1), (low + 1, low)]
    if wrap and start == 1:
        pairs += [(count - 1, 0), (0, count - 1)]
    return pairs


def flip(count, bit):
    return [(index, index ^ bit) for index in range(count)]


def even_index(axis):
    return lax.rem(lax.axis_index(axis), 2) == 0


def call(body, outs, args, scratch=(), flops=0, name=None, from_hbm=False, to_hbm=False):
    nbytes = sum(int(np.prod(a.shape)) * 4 for a in args) + sum(
        int(np.prod(s)) * 4 for s in outs
    )
    return pl.pallas_call(
        body,
        out_shape=[
            jax.ShapeDtypeStruct(s, jnp.float32) if to_hbm else VMEM(s, jnp.float32) for s in outs
        ],
        in_specs=[pl.BlockSpec(memory_space=pltpu.HBM if from_hbm else VMEM)] * len(args),
        out_specs=[pl.BlockSpec(memory_space=VMEM)] * len(outs),
        scratch_shapes=list(scratch),
        compiler_params=pltpu.CompilerParams(vmem_limit_bytes=8 << 20),
        cost_estimate=pl.CostEstimate(flops=flops, bytes_accessed=nbytes, transcendentals=0),
        name=name,
    )(*[pltpu.with_memory_space_constraint(a, pltpu.HBM if from_hbm else VMEM) for a in args])


def pack_stream(hbm_v, hbm_r, hbm_t, hbm_y, send_a, send_b, vel, temp, done):
    even = even_index("stream")
    nx = vel.shape[1]
    edge = jnp.where(even, 0, nx - 1)
    copies = [
        pltpu.make_async_copy(src, dst, done.at[k])
        for k, (src, dst) in enumerate(
            (
                (hbm_v, vel),
                (hbm_t, temp),
                (hbm_y.at[:, edge], send_b.at[pl.ds(8, SPECIES)]),
                (hbm_r.at[pl.ds(edge, 1)], send_b.at[pl.ds(6, 1)]),
            )
        )
    ]
    for copy in copies:
        copy.start()
    copies[0].wait()
    for comp in range(3):
        for layer in range(2):
            low = vel[comp, layer]
            high = vel[comp, nx - 2 + layer]
            send_a[2 * comp + layer] = jnp.where(even, high, low)
            send_b[2 * comp + layer] = jnp.where(even, low, high)
    copies[1].wait()
    send_b[7] = jnp.where(even, temp[0], temp[nx - 1])
    fastest = None
    for x in range(nx):
        speed = (
            jnp.abs(vel[0, x])
            + jnp.abs(vel[1, x])
            + jnp.abs(vel[2, x])
            + jnp.sqrt(adiabatic_gamma * temp[x])
        )
        fastest = speed if fastest is None else jnp.maximum(fastest, speed)
    send_a[6] = fastest
    copies[2].wait()
    copies[3].wait()


def pack_span(vel, dens, temp, spec, got_a, got_b, near, got_n, send_c, send_d, top):
    even_s = even_index("stream")
    even_p = even_index("span")
    nx, nz = vel.shape[1], vel.shape[2]
    for comp in range(3):
        for x in range(nx + 4):
            if x < 2:
                tile = jnp.where(even_s, got_b[2 * comp + x], got_a[2 * comp + x])
            elif x < nx + 2:
                tile = vel[comp, x - 2]
            else:
                at = 2 * comp + x - nx - 2
                tile = jnp.where(even_s, got_a[at], got_b[at])
            first, last = tile[0:2], tile[nz - 2 : nz]
            row = 2 * (comp * (nx + 4) + x)
            send_c[row : row + 2] = jnp.where(even_p, last, first)
            send_d[row : row + 2] = jnp.where(even_p, first, last)
    top[...] = jnp.maximum(near[...], got_n[...])
    base = 6 * (nx + 4)
    for field in range(SCALARS):
        ref = dens if field == 0 else temp if field == 1 else spec.at[field - 2]
        row = base + field * nx
        send_c[row : row + nx] = jnp.where(even_p, ref[:, nz - 1, :], ref[:, 0, :])


def pack_far(dens, temp, spec, far_a, far_d):
    even_s = even_index("stream")
    even_p = even_index("span")
    nx, nz = dens.shape[0], dens.shape[1]
    for field in range(SCALARS):
        ref = dens if field == 0 else temp if field == 1 else spec.at[field - 2]
        far_a[field] = jnp.where(even_s, ref[nx - 1], ref[0])
        row = field * nx
        far_d[row : row + nx] = jnp.where(even_p, ref[:, 0, :], ref[:, nz - 1, :])
    for row in range(SCALARS * nx, far_d.shape[0], nx):
        far_d[row : row + nx] = far_d[0:nx]
    for extra in range(SCALARS, far_a.shape[0]):
        far_a[extra] = far_a[0]


def along_y(tile, lane):
    width = tile.shape[-1]
    after = jnp.where(lane == width - 1, 0.0, pltpu.roll(tile, width - 1, 1))
    before = jnp.where(lane == 0, 0.0, pltpu.roll(tile, 1, 1))
    return after, before


def differences(ref, x, i, shift, lane):
    center = ref[i, x]
    after, before = along_y(center, lane)
    return [ref[i, x + 1] - ref[i, x - 1], after - before, shift(center, -1) - shift(center, 1)]


def strain_of(diffs):
    parts = [diffs[i][i] if i == j else diffs[i][j] + diffs[j][i] for i, j in pair_list]
    diagonal = parts[0] * parts[0] + parts[1] * parts[1] + parts[2] * parts[2]
    off = parts[3] * parts[3] + parts[4] * parts[4] + parts[5] * parts[5]
    return parts, jnp.sqrt(0.5 * diagonal + 0.25 * off)


def germano(vel, got_a, got_b, got_c, got_d, far_a, far_d, red, mag, wide, shear, smooth, square):
    even_s = even_index("stream")
    even_p = even_index("span")
    nx, nz, ny = vel.shape[1], vel.shape[2], vel.shape[3]
    rows = 2 * nz
    zero = jnp.zeros((nz - 4, ny), jnp.float32)
    for comp in range(3):
        for x in range(nx + 4):
            if x < 2:
                tile = jnp.where(even_s, got_b[2 * comp + x], got_a[2 * comp + x])
            elif x < nx + 2:
                tile = vel[comp, x - 2]
            else:
                at = 2 * comp + x - nx - 2
                tile = jnp.where(even_s, got_a[at], got_b[at])
            row = 2 * (comp * (nx + 4) + x)
            one, two = got_c[row : row + 2], got_d[row : row + 2]
            wide[comp, x, 0:nz] = tile
            wide[comp, x, nz : nz + 2] = jnp.where(even_p, one, two)
            wide[comp, x, nz + 2 : rows - 2] = zero
            wide[comp, x, rows - 2 : rows] = jnp.where(even_p, two, one)
    lane = lax.broadcasted_iota(jnp.int32, (rows, ny), 1)

    def shift(tile, by):
        return pltpu.roll(tile, by % rows, 0)

    def z_sum(tile):
        pair = tile + shift(tile, -1)
        return pair + shift(pair, 1)

    position = lax.axis_index("stream") * nx
    total = lax.axis_size("stream") * nx

    last = None
    for x in range(nx + 4):
        here = [wide[i, x] for i in range(3)]
        products = [here[i] * here[j] for i, j in pair_list]
        if last is not None:
            for k in range(6):
                square[k, x - 1] = products[k] + last[k]
        last = products

    for x in range(nx + 2):
        keep = 1.0
        if x == 0:
            keep = jnp.where(position > 0, 1.0, 0.0)
        elif x == nx + 1:
            keep = jnp.where(position + nx < total, 1.0, 0.0)
        parts, size = strain_of([differences(wide, x + 1, i, shift, lane) for i in range(3)])
        if 1 <= x <= nx:
            mag[x - 1] = size[0:nz]
        straight = size * (keep * 0.03125)
        crossed = size * (keep * 0.015625)
        for k, (i, j) in enumerate(pair_list):
            shear[k, x] = (straight if i == j else crossed) * parts[k]
        for i in range(3):
            value = (wide[i, x] + wide[i, x + 2]) + 2.0 * wide[i, x + 1]
            smooth[i, x] = z_sum(value) * (keep * 0.0625)
    for x in range(nx):
        hat_parts, hat_size = strain_of(
            [differences(smooth, x + 1, i, shift, lane) for i in range(3)]
        )
        straight = 2.0 * hat_size
        lm = [None, None]
        mm = [None, None]
        for k, (i, j) in enumerate(pair_list):
            kind = 0 if i == j else 1
            product = z_sum(square[k, x + 1] + square[k, x + 2])
            resolved = 0.0625 * product - smooth[i, x + 1] * smooth[j, x + 1]
            filtered = z_sum((shear[k, x] + shear[k, x + 2]) + 2.0 * shear[k, x + 1])
            model = filtered - (straight if i == j else hat_size) * hat_parts[k]
            lm[kind] = resolved * model if lm[kind] is None else lm[kind] + resolved * model
            mm[kind] = model * model if mm[kind] is None else mm[kind] + model * model
        lm = (lm[0] + 2.0 * lm[1])[0:nz]
        mm = (mm[0] + 2.0 * mm[1])[0:nz]
        lm = jnp.sum(lm, axis=0, keepdims=True)
        mm = jnp.sum(mm, axis=0, keepdims=True)
        half = ny // 2
        red[x : x + 1] = lm[:, :half]
        red[nx + x : nx + x + 1] = lm[:, half:]
        red[2 * nx + x : 2 * nx + x + 1] = mm[:, :half]
        red[3 * nx + x : 3 * nx + x + 1] = mm[:, half:]


def join(red, near, got_n, out):
    sums, half = red.shape
    out[:sums] = red[...]
    top = jnp.maximum(near[...], got_n[...])
    out[sums:] = jnp.maximum(top[:, :half], top[:, half:])


def chemistry(dens, inverse, temp, species):
    over = 1.0 / temp
    root = jnp.sqrt(temp)
    powers = {0.0: None, 0.5: root, 1.0: temp, -1.0: over, -0.5: root * over, -2.0: over * over}
    e05 = jnp.exp(-0.05 * over)
    e15 = jnp.exp(-1.5 * over)
    decay = {0: None, 5: e05, 150: e15}
    decay[10] = e05 * e05
    decay[20] = decay[10] * decay[10]
    decay[30] = decay[20] * decay[10]
    decay[40] = decay[20] * decay[20]
    decay[70] = decay[40] * decay[30]
    decay[80] = decay[40] * decay[40]
    decay[160] = e15 * decay[10]
    decay[180] = e15 * decay[30]
    decay[200] = decay[180] * decay[20]
    conc = [dens * (species[k] * float(1.0 / molar_weight[k])) for k in range(SPECIES)]
    total = conc[0]
    for k in range(1, SPECIES):
        total = total + conc[k]
    conc.append(total)
    products = {}

    def product(ids):
        if len(ids) == 1:
            return conc[ids[0]]
        if ids not in products:
            products[ids] = product(ids[:-1]) * conc[ids[-1]]
        return products[ids]

    produced = [None] * SPECIES
    for number, (reactants, results) in enumerate(reaction_list):
        ordered = tuple(sorted(reactants))
        pace = product(ordered) * float(np.exp(np.float64(log_prefactor[number])))
        power = powers[float(thermal_power_index[number])]
        if power is not None:
            pace = pace * power
        fall = decay[int(round(float(arrhenius_barrier[number]) * 100))]
        if fall is not None:
            pace = pace * fall
        change = {}
        for k in reactants:
            if k < SPECIES:
                change[k] = change.get(k, 0) - 1
        for k in results:
            change[k] = change.get(k, 0) + 1
        for k, times in change.items():
            if times == 0:
                continue
            term = pace if abs(times) == 1 else pace * float(abs(times))
            if produced[k] is None:
                produced[k] = term if times > 0 else -term
            else:
                produced[k] = produced[k] + term if times > 0 else produced[k] - term
    heat = None
    for k in range(SPECIES):
        if formation[k] != 0.0 and produced[k] is not None:
            term = produced[k] * float(-formation[k] / heat_capacity)
            heat = term if heat is None else heat + term
    source = [
        None if produced[k] is None else produced[k] * inverse * float(molar_weight[k])
        for k in range(SPECIES)
    ]
    return source, heat * inverse


def tendencies(
    vel, dens, temp, spec, fuel, got_a, got_b, got_c, got_d, far_a, far_d, mag, base, slope
):
    even_s = even_index("stream")
    even_p = even_index("span")
    nx, nz, ny = dens.shape
    lane = lax.broadcasted_iota(jnp.int32, (nz, ny), 1)
    line = lax.broadcasted_iota(jnp.int32, (nz, ny), 0)

    def own(field, x):
        if field < 3:
            return vel[field, x]
        if field == 3:
            return dens[x]
        if field == 4:
            return temp[x]
        return spec[field - 5, x]

    def cell(field, x):
        if 0 <= x < nx:
            return own(field, x)
        if field < 3:
            at = 2 * field + (1 if x < 0 else 0)
            one, two = got_a[at], got_b[at]
        else:
            one, two = far_a[field - 3], got_b[3 + field]
        return jnp.where(even_s, two, one) if x < 0 else jnp.where(even_s, one, two)

    def edges(field, x):
        if field < 3:
            row = 2 * (field * (nx + 4) + x + 2)
            c0, c1 = got_c[row : row + 1], got_c[row + 1 : row + 2]
            d0, d1 = got_d[row : row + 1], got_d[row + 1 : row + 2]
            return jnp.where(even_p, c0, d0), jnp.where(even_p, d1, c1)
        line_at = (field - 3) * nx + x
        row = 6 * (nx + 4) + line_at
        c0, d0 = got_c[row : row + 1], far_d[line_at : line_at + 1]
        return jnp.where(even_p, c0, d0), jnp.where(even_p, d0, c0)

    def neighbours(field, x):
        center = own(field, x)
        after, before = along_y(center, lane)
        high, low = edges(field, x)
        up = jnp.where(line == nz - 1, high, pltpu.roll(center, nz - 1, 0))
        down = jnp.where(line == 0, low, pltpu.roll(center, 1, 0))
        return center, cell(field, x + 1), cell(field, x - 1), after, before, up, down

    for x in range(nx):
        v = [neighbours(i, x) for i in range(3)]
        r = neighbours(3, x)
        t = neighbours(4, x)
        half = [0.5 * v[i][0] for i in range(3)]
        inverse = 1.0 / r[0]
        size = mag[x]
        inject = fuel[x].astype(jnp.float32) * inject_rate
        species = [own(5 + k, x) for k in range(SPECIES)]
        source, release = chemistry(r[0], inverse, t[0], species)

        def advect(n):
            return half[0] * (n[1] - n[2]) + half[1] * (n[3] - n[4]) + half[2] * (n[5] - n[6])

        def laplace(n):
            return ((n[1] + n[2]) + (n[3] + n[4])) + ((n[5] + n[6]) - 6.0 * n[0])

        push = [r[m] * t[m] for m in range(1, 7)]
        scale = 0.5 * inverse
        for i in range(3):
            lap = laplace(v[i])
            value = laminar_diffusivity * lap - advect(v[i]) - (push[2 * i] - push[2 * i + 1]) * scale
            if i == 1:
                value = value + inject * (inject_speed - v[1][0])
            base[i, x] = value
            slope[i, x] = size * lap
        flux = (
            (r[1] * v[0][1] - r[2] * v[0][2])
            + (r[3] * v[1][3] - r[4] * v[1][4])
            + (r[5] * v[2][5] - r[6] * v[2][6])
        )
        base[3, x] = -0.5 * flux
        thin = size * (1.0 / subgrid_thermal_quotient)
        lap = laplace(t)
        base[4, x] = (laminar_diffusivity / momentum_thermal_quotient) * lap - advect(t) + release
        slope[3, x] = thin * lap
        for k in range(SPECIES):
            n = neighbours(5 + k, x)
            lap = laplace(n)
            value = (laminar_diffusivity / schmidt) * lap - advect(n)
            if source[k] is not None:
                value = value + source[k]
            if k == 0:
                value = value + inject * (1.0 - n[0])
            base[5 + k, x] = value
            slope[4 + k, x] = thin * lap


def finish(
    total_z, vel, dens, temp, spec, wall, base, slope, r0, r1, r2, r3, out_v, out_r, out_t, out_y, out_c
):
    nx = dens.shape[0]
    sums = (r0[: 4 * nx] + r1[: 4 * nx]) + (r2[: 4 * nx] + r3[: 4 * nx])
    lm = jnp.concatenate([sums[:nx], sums[nx : 2 * nx]], axis=1)
    mm = jnp.concatenate([sums[2 * nx : 3 * nx], sums[3 * nx :]], axis=1)
    coef = jnp.maximum(0.5 * (lm / total_z) / (mm / total_z + tiny_value), 0.0)
    out_c[...] = coef
    top = jnp.maximum(
        jnp.maximum(r0[4 * nx :], r1[4 * nx :]), jnp.maximum(r2[4 * nx :], r3[4 * nx :])
    )
    step = courant / jnp.max(jnp.max(top, axis=0, keepdims=True), axis=1, keepdims=True)
    gain = coef * step
    for x in range(nx):
        g = gain[x : x + 1]
        open_cell = 1.0 - wall[x].astype(jnp.float32)
        for i in range(3):
            out_v[i, x] = open_cell * (vel[i, x] + step * base[i, x] + g * slope[i, x])
        out_r[x] = dens[x] + step * base[3, x]
        out_t[x] = temp[x] + step * base[4, x] + g * slope[3, x]
        for k in range(SPECIES):
            out_y[k, x] = spec[k, x] + step * base[5 + k, x] + g * slope[4 + k, x]


def per_device(vel, dens, temp, spec, wall, fuel):
    nx, nz, ny = dens.shape
    n_stream = lax.axis_size("stream")
    n_span = lax.axis_size("span")
    send_a, send_b, vel, temp = call(
        pack_stream,
        [(7, nz, ny), (6 + SCALARS, nz, ny), vel.shape, temp.shape],
        (vel, dens, temp, spec),
        scratch=[pltpu.SemaphoreType.DMA((4,))],
        name="pack_stream",
        from_hbm=True,
    )
    got_a = lax.ppermute(send_a, "stream", pair_up(n_stream, 0, False))
    got_b = lax.ppermute(send_b, "stream", pair_up(n_stream, 1, False))
    send_far, send_fd = call(
        pack_far,
        [(21, nz, ny), (6 * (nx + 4) + SCALARS * nx + 2 * nx, ny)],
        (dens, temp, spec),
        name="pack_far",
    )
    far_d = lax.ppermute(send_fd, "span", pair_up(n_span, 1, True))
    near = jnp.maximum(send_a[6], got_a[6])
    got_n = lax.ppermute(near, "stream", flip(n_stream, 2))
    rows = 6 * (nx + 4) + SCALARS * nx
    send_c, send_d, near = call(
        pack_span,
        [(rows, ny), (6 * (nx + 4), ny), (nz, ny)],
        (vel, dens, temp, spec, got_a, got_b, near, got_n),
        name="pack_span",
    )
    far_a = lax.ppermute(send_far, "stream", pair_up(n_stream, 0, False))
    got_c = lax.ppermute(send_c, "span", pair_up(n_span, 0, True))
    got_d = lax.ppermute(send_d, "span", pair_up(n_span, 1, True))
    bit = 4
    while bit * 2 < n_stream:
        near = jnp.maximum(near, lax.ppermute(near, "stream", flip(n_stream, bit)))
        bit *= 2
    got_n = lax.ppermute(near, "stream", flip(n_stream, bit))
    red, mag = call(
        germano,
        [(4 * nx, ny // 2), (nx, nz, ny)],
        (vel, got_a, got_b, got_c, got_d, far_a, far_d),
        scratch=[
            VMEM((3, nx + 4, 2 * nz, ny), jnp.float32),
            VMEM((6, nx + 2, 2 * nz, ny), jnp.float32),
            VMEM((3, nx + 2, 2 * nz, ny), jnp.float32),
            VMEM((6, nx + 3, 2 * nz, ny), jnp.float32),
        ],
        name="germano",
        flops=1000000000,
    )
    base, slope = call(
        tendencies,
        [(5 + SPECIES, nx, nz, ny), (4 + SPECIES, nx, nz, ny)],
        (vel, dens, temp, spec, fuel, got_a, got_b, got_c, got_d, far_a, far_d, mag),
        name="tendencies",
    )
    (red,) = call(join, [(4 * nx + nz, ny // 2)], (red, near, got_n), name="join")
    bit = 1
    while bit * 4 < n_span:
        others = [lax.ppermute(red, "span", flip(n_span, bit * m)) for m in (1, 2, 3)]
        low = (red[: 4 * nx] + others[0][: 4 * nx]) + (others[1][: 4 * nx] + others[2][: 4 * nx])
        high = jnp.maximum(
            jnp.maximum(red[4 * nx :], others[0][4 * nx :]),
            jnp.maximum(others[1][4 * nx :], others[2][4 * nx :]),
        )
        red = jnp.concatenate([low, high], axis=0)
        bit *= 4
    others = [lax.ppermute(red, "span", flip(n_span, bit * m)) for m in (3, 1, 2)]
    return tuple(
        call(
            functools.partial(finish, float(nz * n_span)),
            [vel.shape, dens.shape, dens.shape, spec.shape, (nx, ny)],
            (vel, dens, temp, spec, wall, base, slope, red, *others),
            name="finish",
            to_hbm=True,
        )
    )


def solution(mesh):
    return jax.shard_map(
        per_device,
        mesh=mesh,
        in_specs=(
            P(None, "stream", "span", None),
            P("stream", "span", None),
            P("stream", "span", None),
            P(None, "stream", "span", None),
            P("stream", "span", None),
            P("stream", "span", None),
        ),
        out_specs=(
            P(None, "stream", "span", None),
            P("stream", "span", None),
            P("stream", "span", None),
            P(None, "stream", "span", None),
            P("stream", None),
        ),
        check_vma=False,
    )
```
